32 devices in a mesh: wide: 8 (over z, x), narrow: 4 (over y, core).
Axes of the slice: x: 2, y: 2, z: 4, core: 2. Of those that a mesh axis runs over, the one named last changes fastest.
Arguments:
- tokens: bfloat16 [18432, 768], P(('wide', 'narrow')), may hold values from -6 to 6
- segment_ids: int32 [32, 576], P(('wide', 'narrow')), may hold values from 0 to 7, as said below
- patch_valid: int32 [32, 576], P(('wide', 'narrow')), may hold values from 0 to 1, as said below
- routes: int32 [18432, 2], P(('wide', 'narrow')), may hold values from 0 to 7, all different within a row
- priority: int32 [32, 576], P(('wide', 'narrow')), may hold values from 0 to 575, each once within a row
- gain_attn: bfloat16 [768], P(('wide', 'narrow')), may hold values from 0.099609375 to 1.8984375
- shift_attn: bfloat16 [768], P(('wide', 'narrow')), may hold values from -3 to 3
- w_qkv: bfloat16 [768, 2304], P(('wide', 'narrow')), may hold values from -0.3125 to 0.3125
- query_bias: bfloat16 [768], P(('wide', 'narrow')), may hold values from -3 to 3
- value_bias: bfloat16 [768], P(('wide', 'narrow')), may hold values from -3 to 3
- w_proj: bfloat16 [768, 768], P(('wide', 'narrow')), may hold values from -1.75 to 1.75
- proj_bias: bfloat16 [768], P(('wide', 'narrow')), may hold values from -3 to 3
- gain_moe: bfloat16 [768], P(('wide', 'narrow')), may hold values from 0.099609375 to 1.8984375
- shift_moe: bfloat16 [768], P(('wide', 'narrow')), may hold values from -1.5 to 1.5
- w_router: bfloat16 [768, 8], P(('wide', 'narrow')), may hold values from -0.5 to 0.5
- w_in: bfloat16 [8, 768, 3072], P('wide', None, 'narrow'), may hold values from -0.21875 to 0.21875
- in_bias: bfloat16 [8, 3072], P('wide', 'narrow'), may hold values from -3 to 3
- w_out: bfloat16 [8, 3072, 768], P('wide', 'narrow'), may hold values from -88 to 88
- out_bias: bfloat16 [8, 768], P('wide'), may hold values from -488 to 488
- cotangent: bfloat16 [18432, 768], P(('wide', 'narrow')), may hold values from -6 to 6
Outputs:
- block_out: bfloat16 [18432, 768], P(('wide', 'narrow'))
- grad_tokens: bfloat16 [18432, 768], P(('wide', 'narrow'))
- grad_gain_attn: float32 [768], P(('wide', 'narrow'))
- grad_shift_attn: float32 [768], P(('wide', 'narrow'))
- grad_w_qkv: float32 [768, 2304], P(('wide', 'narrow'))
- grad_query_bias: float32 [768], P(('wide', 'narrow'))
- grad_value_bias: float32 [768], P(('wide', 'narrow'))
- grad_w_proj: float32 [768, 768], P(('wide', 'narrow'))
- grad_proj_bias: float32 [768], P(('wide', 'narrow'))
- grad_gain_moe: float32 [768], P(('wide', 'narrow'))
- grad_shift_moe: float32 [768], P(('wide', 'narrow'))
- grad_w_router: float32 [768, 8], P(('wide', 'narrow'))
- grad_w_in: float32 [8, 768, 3072], P('wide', None, 'narrow')
- grad_in_bias: float32 [8, 3072], P('wide', 'narrow')
- grad_w_out: float32 [8, 3072, 768], P('wide', 'narrow')
- grad_out_bias: float32 [8, 768], P('wide')
The draws below stay inside these ranges and needn't reach their ends.
Inputs may be any that keep to these rules, and one draw needn't show every extreme that they name: `segment_ids`: along each row of 576 patches the image numbers never fall; row 0 is one image. `patch_valid`: each row is 1 except for a tail of 0 to 71 padded patches. `routes`: the two experts of a patch differ. `priority`: each row holds every rank of 0 to 575 once.
All inputs are finite; a program needn't handle non-finite values.
Results may differ from the reference program's by a relative error of at most 0.02.
The reference program's roundings to bfloat16 on the way count: a program that leaves them out, or rounds other values in their place, can miss the bound.
Values may be sent and summed in bfloat16 or wider, within the bound.
A program may use at most 256 MiB of HBM per device.

```python
import jax
import jax.numpy as jnp
from jax import lax

D = 768
HEADS = 12
HEAD = 64
FF = 3072
EXPERTS = 8
TOK_DEV = 576
TOKENS = 18432
CAP = 152
DEVICES = 32


def draw_segment_ids(key, part):
    cut_points = jax.random.randint(jax.random.fold_in(key, 11), (DEVICES, 7), 1, TOK_DEV)
    row_ids = jnp.arange(DEVICES, dtype=jnp.int32)
    cut_points = jnp.where(row_ids[:, None] == 0, TOK_DEV, cut_points)
    places = jnp.arange(TOK_DEV, dtype=jnp.int32)
    return jnp.sum((places[None, :, None] >= cut_points[:, None, :]).astype(jnp.int32), axis=2).astype(jnp.int32)


def draw_patch_valid(key, part):
    tails = jax.random.randint(jax.random.fold_in(key, 23), (DEVICES, 1), 0, TOK_DEV // 8)
    places = jnp.arange(TOK_DEV, dtype=jnp.int32)
    return (places[None, :] < TOK_DEV - tails).astype(jnp.int32)


def expert_offsets(key):
    return jax.random.uniform(jax.random.fold_in(key, 41), (EXPERTS,), jnp.float32, -3.0, 3.0)


def expert_factors(key):
    return 4.0 * jnp.exp(-expert_offsets(key))


def moe_shift_values(key):
    return 0.5 * jax.random.truncated_normal(jax.random.fold_in(key, 31), -3.0, 3.0, (D,), jnp.float32)


def draw_shift_moe(key, part):
    return moe_shift_values(key).astype(jnp.bfloat16)


def draw_w_router(key, part):
    noise = jax.random.truncated_normal(jax.random.fold_in(key, 37), -6.0, 6.0, (D, EXPERTS), jnp.float32) * D ** (-0.5)
    shift_vals = moe_shift_values(key)
    return (noise + shift_vals[:, None] * expert_offsets(key)[None, :] * (4.0 / D)).astype(jnp.bfloat16)


def draw_w_out(key, part):
    noise = jax.random.truncated_normal(jax.random.fold_in(key, 43), -6.0, 6.0, (EXPERTS, FF, D), jnp.float32)
    return (noise * (EXPERTS / (2.0 * FF ** 0.5)) * expert_factors(key)[:, None, None]).astype(jnp.bfloat16)


def draw_out_bias(key, part):
    noise = jax.random.truncated_normal(jax.random.fold_in(key, 47), -3.0, 3.0, (EXPERTS, D), jnp.float32)
    return (noise * (0.25 * EXPERTS) * expert_factors(key)[:, None]).astype(jnp.bfloat16)


def shard_levels(key, shape, split, smallest, largest):
    def one(dim, blocks):
        steps = jax.random.uniform(jax.random.fold_in(jax.random.fold_in(key, 6), dim), (blocks,), jnp.float32, smallest / len(split), largest / len(split))
        return jnp.repeat(jnp.exp(steps), shape[dim] // blocks).reshape((-1,) + (1,) * (len(shape) - dim - 1))

    loudness = one(*split[0])
    for cut in split[1:]:
        loudness = loudness * one(*cut)
    return loudness


def different_ones(key, rows, count, top, lift):
    order = jax.random.permutation(jax.random.fold_in(key, 1), count)
    boost = order
    for power in range(3):
        boost = boost * boost // count
    boost = boost * lift // count
    chance = jax.random.randint(jax.random.fold_in(key, 2), (rows, count), 0, 4096) + boost
    fixed_rows = jax.random.permutation(jax.random.fold_in(key, 3), rows)[jnp.arange(count) % rows]
    chance = jnp.where(jnp.arange(rows)[:, None] == fixed_rows[None, :], 1 << 14, chance)
    merit = chance * count + jnp.arange(count)
    return lax.top_k(merit.astype(jnp.int32), top)[1].astype(jnp.int32)


def centred(own_key, shape, deviation, limit, cuts=(), kind=jnp.bfloat16):
    drawn = jax.random.normal(own_key, shape, jnp.float32) * deviation
    if len(cuts) > 0:
        drawn = shard_levels(own_key, shape, cuts, -0.22, 0.18) * drawn
    return jnp.clip(drawn, min=-limit, max=limit).astype(kind)


def setup_inputs(seed: int = 0) -> dict:
    arg_keys = jax.random.split(jax.random.key(seed), 21)
    return {
        "tokens": centred(arg_keys[0], (TOKENS, D), 1.0, 6.0, ((0, 32),)),
        "segment_ids": draw_segment_ids(jax.random.fold_in(arg_keys[20], 71), 0),
        "patch_valid": draw_patch_valid(jax.random.fold_in(arg_keys[20], 71), 0),
        "routes": different_ones(arg_keys[3], TOKENS, EXPERTS, 2, 2048),
        "priority": jax.vmap(lambda own: jax.random.permutation(own, TOK_DEV))(jax.random.split(arg_keys[4], DEVICES)).reshape((DEVICES, TOK_DEV)).astype(jnp.int32),
        "gain_attn": jnp.clip(1.0 + 0.18 * jax.random.normal(arg_keys[5], (D,), jnp.float32), 0.099609375, 1.8984375).astype(jnp.bfloat16),
        "shift_attn": centred(arg_keys[6], (D,), 0.5, 3.0, ((0, 32),)),
        "w_qkv": centred(arg_keys[7], (D, 3 * D), (D // 2) ** -0.5, 0.3125, ((0, 32),)),
        "query_bias": centred(arg_keys[8], (D,), 0.5, 3.0, ((0, 32),)),
        "value_bias": centred(arg_keys[9], (D,), 0.5, 3.0, ((0, 32),)),
        "w_proj": centred(arg_keys[10], (D, D), (D // 64) ** -0.5, 1.75, ((0, 32),)),
        "proj_bias": centred(arg_keys[11], (D,), 0.5, 3.0, ((0, 32),)),
        "gain_moe": jnp.clip(1.0 + 0.18 * jax.random.normal(arg_keys[12], (D,), jnp.float32), 0.099609375, 1.8984375).astype(jnp.bfloat16),
        "shift_moe": draw_shift_moe(jax.random.fold_in(arg_keys[20], 71), 0),
        "w_router": draw_w_router(jax.random.fold_in(arg_keys[20], 71), 0),
        "w_in": centred(arg_keys[15], (EXPERTS, D, FF), D ** -0.5, 0.21875, ((0, 8), (2, 4))),
        "in_bias": centred(arg_keys[16], (EXPERTS, FF), 0.5, 3.0, ((0, 8), (1, 4))),
        "w_out": draw_w_out(jax.random.fold_in(arg_keys[20], 71), 0),
        "out_bias": draw_out_bias(jax.random.fold_in(arg_keys[20], 71), 0),
        "cotangent": centred(arg_keys[19], (TOKENS, D), 1.0, 6.0, ((0, 32),)),
    }


@jax.custom_vjp
def low(v):
    return lax.optimization_barrier(v.astype(jnp.bfloat16)).astype(jnp.float32)

@jax.custom_vjp
def low_back(v):
    return v

def low_keep(v):
    return (low(v), None)

def low_pass(kept, grad):
    return (grad,)

def back_keep(v):
    return (v, None)

def back_low(kept, grad):
    return (low(grad),)
low.defvjp(low_keep, low_pass)
low_back.defvjp(back_keep, back_low)
EPSILON = 1e-06
MASKED = -1000000000.0
HIGHEST = lax.Precision.HIGHEST

def layer_norm(values, gain_vec, shift_vec):
    center = lax.optimization_barrier(jnp.mean(values, axis=-1, keepdims=True))
    offset = values - center
    spread = lax.optimization_barrier(jnp.mean(offset * offset, axis=-1, keepdims=True))
    return offset * lax.rsqrt(spread + EPSILON) * gain_vec + shift_vec

def pair_tables(route_row, priority_row, valid_row, experts, capacity):
    row_count = route_row.shape[0]
    labels = jnp.arange(experts, dtype=jnp.int32)
    rank_ids = jnp.arange(row_count, dtype=jnp.int32)
    ranking = (priority_row[None, :] == rank_ids[:, None]).astype(jnp.float32)
    slot_ids = jnp.arange(experts * capacity, dtype=jnp.int32)
    slot_expert = slot_ids // capacity
    slot_place = (slot_ids % capacity).astype(jnp.float32)
    filled = jnp.zeros((experts,), jnp.float32)
    columns = []
    for pair_index in range(2):
        target = route_row[:, pair_index]
        onehot = ((target[:, None] == labels[None, :]) & (valid_row[:, None] == 1)).astype(jnp.float32)
        ranked = jnp.dot(ranking, onehot, precision=HIGHEST)
        earlier = jnp.cumsum(ranked, axis=0) - ranked
        queue_pos = jnp.dot(ranking.T, earlier, precision=HIGHEST) + filled[None, :]
        position = lax.optimization_barrier(jnp.sum(queue_pos * onehot, axis=1))
        matches = (target[None, :] == slot_expert[:, None]) & (position[None, :] == slot_place[:, None]) & (valid_row[None, :] == 1)
        columns.append(matches.astype(jnp.float32))
        filled = filled + lax.optimization_barrier(jnp.sum(onehot, axis=0))
    return jnp.concatenate(columns, axis=1)

def block_group(param_tree, expert_tree, tokens_row, segment_row, valid_row, route_row, priority_row):
    gain_attn, shift_attn, w_qkv, query_bias, value_bias, w_proj, proj_bias, gain_moe, shift_moe, w_router = param_tree
    w_in, in_bias, w_out, out_bias = expert_tree
    places = jnp.arange(TOK_DEV, dtype=jnp.int32)
    allowed = (segment_row[:, None] == segment_row[None, :]) & ((valid_row[None, :] == 1) | (places[:, None] == places[None, :]))
    normed_attn = low(layer_norm(tokens_row, gain_attn, shift_attn))
    qkv_rows = jnp.dot(normed_attn, w_qkv, precision=HIGHEST)
    queries = low_back(low(qkv_rows[:, :D] + query_bias)).reshape(TOK_DEV, HEADS, HEAD)
    keys_all = low_back(low(qkv_rows[:, D:2 * D])).reshape(TOK_DEV, HEADS, HEAD)
    values_all = low_back(low(qkv_rows[:, 2 * D:] + value_bias)).reshape(TOK_DEV, HEADS, HEAD)
    scores = low_back(jnp.einsum('qhc,khc->hqk', queries, keys_all, precision=HIGHEST) * HEAD ** (-0.5))
    scores = jnp.where(allowed[None], scores, MASKED)
    attn_probs = jax.nn.softmax(scores, axis=-1)
    head_mix = jnp.einsum('hqk,khc->qhc', low(attn_probs), values_all, precision=HIGHEST).reshape(TOK_DEV, D)
    attended = low_back(low(head_mix))
    branch = low_back(jnp.dot(attended, w_proj, precision=HIGHEST) + proj_bias)
    middle = tokens_row + branch
    normed_moe = low(layer_norm(middle, gain_moe, shift_moe))
    logits = low_back(jnp.dot(normed_moe, w_router, precision=HIGHEST))
    router_probs = jax.nn.softmax(logits, axis=-1)
    labels = jnp.arange(EXPERTS, dtype=jnp.int32)
    gate_first = lax.optimization_barrier(jnp.sum(router_probs * (route_row[:, 0:1] == labels[None, :]).astype(jnp.float32), axis=-1))
    gate_second = lax.optimization_barrier(jnp.sum(router_probs * (route_row[:, 1:2] == labels[None, :]).astype(jnp.float32), axis=-1))
    pair_table = pair_tables(route_row, priority_row, valid_row, EXPERTS, CAP)
    dispatch = pair_table[:, :TOK_DEV] + pair_table[:, TOK_DEV:]
    expert_in = low_back(jnp.dot(dispatch, normed_moe, precision=HIGHEST)).reshape(EXPERTS, CAP, D)
    pre_act = low_back(jnp.einsum('ecd,edf->ecf', expert_in, w_in, precision=HIGHEST) + in_bias[:, None, :])
    hidden = low(jax.nn.gelu(pre_act, approximate=True))
    expert_out = low_back(low(jnp.einsum('ecf,efd->ecd', hidden, w_out, precision=HIGHEST) + out_bias[:, None, :]))
    picked = jnp.dot(pair_table.T, expert_out.reshape(EXPERTS * CAP, D), precision=HIGHEST)
    mixture = gate_first[:, None] * picked[:TOK_DEV] + gate_second[:, None] * picked[TOK_DEV:]
    return middle + mixture

def reference(tokens, segment_ids, patch_valid, routes, priority, gain_attn, shift_attn, w_qkv, query_bias, value_bias, w_proj, proj_bias, gain_moe, shift_moe, w_router, w_in, in_bias, w_out, out_bias, cotangent):
    param_set = jax.tree.map(lambda leaf_arr: leaf_arr.astype(jnp.float32), (gain_attn, shift_attn, w_qkv, query_bias, value_bias, w_proj, proj_bias, gain_moe, shift_moe, w_router))
    expert_set = jax.tree.map(lambda leaf_arr: leaf_arr.astype(jnp.float32), (w_in, in_bias, w_out, out_bias))
    inputs = tokens.astype(jnp.float32).reshape(DEVICES, TOK_DEV, D)
    route_rows = routes.reshape(DEVICES, TOK_DEV, 2)
    group_fn = jax.checkpoint(block_group)

    def forward(token_rows, param_tree, expert_tree):

        def scan_step(scan_carry, group_data):
            return (scan_carry, group_fn(param_tree, expert_tree, *group_data))
        _, group_outs = lax.scan(scan_step, jnp.zeros((), jnp.float32), (token_rows, segment_ids, patch_valid, route_rows, priority))
        return group_outs
    block_rows, pullback = jax.vjp(forward, inputs, param_set, expert_set)
    grad_rows, grad_params, grad_experts = pullback(cotangent.astype(jnp.float32).reshape(DEVICES, TOK_DEV, D))
    grad_gain_attn, grad_shift_attn, grad_w_qkv, grad_query_bias, grad_value_bias, grad_w_proj, grad_proj_bias, grad_gain_moe, grad_shift_moe, grad_w_router = grad_params
    grad_w_in, grad_in_bias, grad_w_out, grad_out_bias = grad_experts
    return (block_rows.reshape(TOKENS, D).astype(jnp.bfloat16), grad_rows.reshape(TOKENS, D).astype(jnp.bfloat16), grad_gain_attn, grad_shift_attn, grad_w_qkv, grad_query_bias, grad_value_bias, grad_w_proj, grad_proj_bias, grad_gain_moe, grad_shift_moe, grad_w_router, grad_w_in, grad_in_bias, grad_w_out, grad_out_bias)
```

```python
import functools

import jax
import jax.numpy as jnp
from jax import lax
from jax.experimental import pallas as pl
from jax.experimental.pallas import tpu as pltpu
from jax.sharding import PartitionSpec as P

HEAD = 64
PAIR = 2 * HEAD
EPSILON = 1e-06
MASKED = -1000000000.0
MESH = pl.DeviceIdType.MESH
LOW = jnp.bfloat16
F32 = jnp.float32
VMEM_LIMIT = 58 * 1024 * 1024


def dot(a, b):
    return jnp.dot(a, b, preferred_element_type=F32)


def dot_nt(a, b):
    return lax.dot_general(a, b, (((1,), (1,)), ((), ())), preferred_element_type=F32)


def dot_tn(a, b):
    return lax.dot_general(a, b, (((0,), (0,)), ((), ())), preferred_element_type=F32)


def grid_of(wide, narrow):
    along_x = 1 << ((wide.bit_length() - 1) // 2)
    return wide // along_x, along_x, narrow // 2, 2


def place_of(dims):
    depth, across, rows, cores = dims
    wide, narrow = lax.axis_index("wide"), lax.axis_index("narrow")
    return wide // across, wide % across, narrow // cores, narrow % cores


def device_at(dims, z, x, y, c):
    depth, across, rows, cores = dims
    return (z * across + x, y * cores + c)


def greet(peers):
    barrier = pltpu.get_barrier_semaphore()
    for peer in peers:
        pl.semaphore_signal(barrier, inc=1, device_id=peer, device_id_type=MESH)
    pl.semaphore_wait(barrier, len(peers))


def neighbours(dims):
    depth, across, rows, cores = dims
    z, x, y, c = place_of(dims)
    peers = [device_at(dims, (z + d) % depth, x, y, c) for d in range(1, depth)]
    peers += [device_at(dims, z, (x + d) % across, y, c) for d in range(1, across)]
    peers += [device_at(dims, z, x, (y + d) % rows, c) for d in range(1, rows)]
    peers += [device_at(dims, z, x, y, 1 - c)]
    return peers


def gather_kernel(dims, cut, shard, out, s1, r1, sx, rx, sy, ry, sa, ra, sb, rb, sc, rc, local):
    depth, across, rows, cores = dims
    z, x, y, c = place_of(dims)
    width = shard.shape[1]

    def block(dz, dx, dy, core):
        wide = ((z - dz) % depth) * across + (x - dx) % across
        return out.at[(wide * rows + (y - dy) % rows) * cores + core]

    def send(src, dst, ssem, rsem, to):
        copy = pltpu.make_async_remote_copy(
            src_ref=src, dst_ref=dst, send_sem=ssem, recv_sem=rsem, device_id=to, device_id_type=MESH
        )
        copy.start()
        return copy

    greet(neighbours(dims))
    own = block(0, 0, 0, c)
    keep = pltpu.make_async_copy(shard, own, local)
    keep.start()
    first, by_x, by_y, half_a, half_b, by_core = {}, {}, {}, {}, {}, {}
    for dz in range(1, depth):
        first[dz] = send(
            shard, own, s1.at[dz - 1], r1.at[dz - 1], device_at(dims, (z + dz) % depth, x, y, c)
        )

    def to_core(dz, dx, dy):
        at = (dz * across + dx) * rows + dy
        src = shard if (dz, dx, dy) == (0, 0, 0) else block(dz, dx, dy, c)
        by_core[at] = send(
            src, block(dz, dx, dy, c), sc.at[at], rc.at[at], device_at(dims, z, x, y, 1 - c)
        )

    def spread(dz):
        if dz:
            first[dz].wait_recv()
        src = block(dz, 0, 0, c) if dz else shard
        for dx in range(1, across):
            at = dz * (across - 1) + dx - 1
            by_x[dz, dx] = send(
                src, block(dz, 0, 0, c), sx.at[at], rx.at[at],
                device_at(dims, z, (x + dx) % across, y, c),
            )
        for dy in range(1, rows):
            at = dz * (rows - 1) + dy - 1
            by_y[dz, dy] = send(
                src, block(dz, 0, 0, c), sy.at[at], ry.at[at],
                device_at(dims, z, x, (y + dy) % rows, c),
            )
        to_core(dz, 0, 0)

    def corner(dz):
        for dx in range(1, across):
            by_x[dz, dx].wait_recv()
            part = block(dz, dx, 0, c).at[:, pl.ds(0, cut)]
            for dy in range(1, rows):
                at = (dz * (across - 1) + dx - 1) * (rows - 1) + dy - 1
                half_a[dz, dx, dy] = send(
                    part, part, sa.at[at], ra.at[at], device_at(dims, z, x, (y + dy) % rows, c)
                )
            to_core(dz, dx, 0)
        for dy in range(1, rows):
            by_y[dz, dy].wait_recv()
            part = block(dz, 0, dy, c).at[:, pl.ds(cut, width - cut)]
            for dx in range(1, across):
                at = (dz * (across - 1) + dx - 1) * (rows - 1) + dy - 1
                half_b[dz, dx, dy] = send(
                    part, part, sb.at[at], rb.at[at], device_at(dims, z, (x + dx) % across, y, c)
                )
            to_core(dz, 0, dy)

    def finish(dz):
        for dx in range(1, across):
            for dy in range(1, rows):
                half_a[dz, dx, dy].wait_recv()
                half_b[dz, dx, dy].wait_recv()
                to_core(dz, dx, dy)

    for step in range(depth + 2):
        if step < depth:
            spread(step)
        if 0 <= step - 1 < depth:
            corner(step - 1)
        if 0 <= step - 2 < depth:
            finish(step - 2)
    for copy in by_core.values():
        copy.wait_recv()
    for group in (first, by_x, by_y, half_a, half_b, by_core):
        for copy in group.values():
            copy.wait_send()
    keep.wait()


def gather_params(dims, shard):
    depth, across, rows, cores = dims
    count = depth * across * rows * cores
    height, width = shard.shape
    cut = (width // 256) * 128
    sizes = (
        depth - 1,
        depth * (across - 1),
        depth * (rows - 1),
        depth * (across - 1) * (rows - 1),
        depth * (across - 1) * (rows - 1),
        depth * across * rows,
    )
    sems = []
    for size in sizes:
        sems += [pltpu.SemaphoreType.DMA((size,))] * 2
    out = pl.pallas_call(
        functools.partial(gather_kernel, dims, cut),
        out_shape=jax.ShapeDtypeStruct((count, height, width), shard.dtype),
        in_specs=[pl.BlockSpec(memory_space=pl.ANY)],
        out_specs=pl.BlockSpec(memory_space=pl.ANY),
        scratch_shapes=sems + [pltpu.SemaphoreType.DMA],
        compiler_params=pltpu.CompilerParams(collective_id=0, has_side_effects=True),
        name="gather_params",
    )(shard)
    return out.reshape(count * height, width)


def scatter_kernel(
    dims, cut, grads, out, mine, r1, r2a, r2b, r3x, r3y, r4, out_a, out_b, out_z,
    s1, q1, s2a, q2a, s2b, q2b, s3x, q3x, s3y, q3y, s4, q4, local,
):
    depth, across, rows, cores = dims
    z, x, y, c = place_of(dims)
    width = grads.shape[-1]
    rest = width - cut

    def send(src, dst, ssem, rsem, to):
        copy = pltpu.make_async_remote_copy(
            src_ref=src, dst_ref=dst, send_sem=ssem, recv_sem=rsem, device_id=to, device_id_type=MESH
        )
        copy.start()
        return copy

    greet(neighbours(dims))
    order = [*range(1, depth), 0]
    first, keeps = {}, {}
    for dz in order:
        planes = pl.ds(((z + dz) % depth) * across, across)
        first[dz] = send(
            grads.at[planes, :, 1 - c], r1.at[dz], s1.at[dz], q1.at[dz],
            device_at(dims, z, x, y, 1 - c),
        )
        keeps[dz] = pltpu.make_async_copy(grads.at[planes, :, c], mine.at[dz], local.at[dz])
        keeps[dz].start()
    corner_a, corner_b, side_x, side_y, last = {}, {}, {}, {}, {}

    def total(*terms):
        acc = terms[0].astype(F32)
        for term in terms[1:]:
            acc = acc + term.astype(F32)
        return acc

    def begin(dz):
        keeps[dz].wait()
        first[dz].wait_recv()
        for a in range(across):
            for b in range(rows):
                mine[dz, a, b] = total(mine[dz, a, b], r1[dz, a, b]).astype(LOW)
        for dx in range(1, across):
            for dy in range(1, rows):
                at = (dz * (across - 1) + dx - 1) * (rows - 1) + dy - 1
                block = mine.at[dz, (x + dx) % across, (y + dy) % rows]
                corner_a[dz, dx, dy] = send(
                    block.at[:, pl.ds(0, cut)], r2a.at[at], s2a.at[at], q2a.at[at],
                    device_at(dims, z, x, (y + dy) % rows, c),
                )
                corner_b[dz, dx, dy] = send(
                    block.at[:, pl.ds(cut, rest)], r2b.at[at], s2b.at[at], q2b.at[at],
                    device_at(dims, z, (x + dx) % across, y, c),
                )

    def middle(dz):
        for dx in range(1, across):
            at = dz * (across - 1) + dx - 1
            block = mine.at[dz, (x + dx) % across, y]
            arrived = []
            for dy in range(1, rows):
                corner_a[dz, dx, dy].wait_recv()
                arrived.append(r2a[at * (rows - 1) + dy - 1])
            out_a[at, :, pl.ds(0, cut)] = total(block[:, pl.ds(0, cut)], *arrived).astype(LOW)
            out_a[at, :, pl.ds(cut, rest)] = block[:, pl.ds(cut, rest)]
            side_x[dz, dx] = send(
                out_a.at[at], r3x.at[at], s3x.at[at], q3x.at[at],
                device_at(dims, z, (x + dx) % across, y, c),
            )
        for dy in range(1, rows):
            at = dz * (rows - 1) + dy - 1
            block = mine.at[dz, x, (y + dy) % rows]
            arrived = []
            for dx in range(1, across):
                corner_b[dz, dx, dy].wait_recv()
                arrived.append(r2b[(dz * (across - 1) + dx - 1) * (rows - 1) + dy - 1])
            out_b[at, :, pl.ds(0, cut)] = block[:, pl.ds(0, cut)]
            out_b[at, :, pl.ds(cut, rest)] = total(block[:, pl.ds(cut, rest)], *arrived).astype(LOW)
            side_y[dz, dy] = send(
                out_b.at[at], r3y.at[at], s3y.at[at], q3y.at[at],
                device_at(dims, z, x, (y + dy) % rows, c),
            )

    def end(dz):
        arrived = []
        for dx in range(1, across):
            side_x[dz, dx].wait_recv()
            arrived.append(r3x[dz * (across - 1) + dx - 1])
        for dy in range(1, rows):
            side_y[dz, dy].wait_recv()
            arrived.append(r3y[dz * (rows - 1) + dy - 1])
        summed = total(mine[dz, x, y], *arrived)
        if dz:
            out_z[dz - 1] = summed.astype(LOW)
            last[dz] = send(
                out_z.at[dz - 1], r4.at[dz - 1], s4.at[dz - 1], q4.at[dz - 1],
                device_at(dims, (z + dz) % depth, x, y, c),
            )
        else:
            out[...] = summed

    for step in range(depth + 2):
        if step < depth:
            begin(order[step])
        if 0 <= step - 1 < depth:
            middle(order[step - 1])
        if 0 <= step - 2 < depth:
            end(order[step - 2])
    for dz in range(1, depth):
        last[dz].wait_recv()
        out[...] += r4[dz - 1].astype(F32)
    for group in (first, corner_a, corner_b, side_x, side_y, last):
        for copy in group.values():
            copy.wait_send()


def scatter_grads(dims, grads):
    depth, across, rows, cores = dims
    wide = depth * across
    height, width = grads.shape[0] // (wide * rows * cores), grads.shape[1]
    cut = (width // 256) * 128
    grads = grads.reshape(wide, rows, cores, height, width)
    n_x, n_y = depth * (across - 1), depth * (rows - 1)
    n_c = n_x * (rows - 1)
    sems = []
    for size in (depth, n_c, n_c, n_x, n_y, depth - 1):
        sems += [pltpu.SemaphoreType.DMA((size,))] * 2
    return pl.pallas_call(
        functools.partial(scatter_kernel, dims, cut),
        out_shape=jax.ShapeDtypeStruct((height, width), F32),
        in_specs=[pl.BlockSpec(memory_space=pl.ANY)],
        out_specs=pl.BlockSpec(memory_space=pltpu.VMEM),
        scratch_shapes=[
            pltpu.VMEM((depth, across, rows, height, width), LOW),
            pltpu.VMEM((depth, across, rows, height, width), LOW),
            pltpu.VMEM((n_c, height, cut), LOW),
            pltpu.VMEM((n_c, height, width - cut), LOW),
            pltpu.VMEM((n_x, height, width), LOW),
            pltpu.VMEM((n_y, height, width), LOW),
            pltpu.VMEM((depth - 1, height, width), LOW),
            pltpu.VMEM((n_x, height, width), LOW),
            pltpu.VMEM((n_y, height, width), LOW),
            pltpu.VMEM((depth - 1, height, width), LOW),
            *sems,
            pltpu.SemaphoreType.DMA((depth,)),
        ],
        compiler_params=pltpu.CompilerParams(
            collective_id=1, has_side_effects=True, vmem_limit_bytes=VMEM_LIMIT
        ),
        name="scatter_grads",
    )(grads)


def norm_parts(values):
    center = jnp.mean(values, axis=-1, keepdims=True)
    offset = values - center
    spread = jnp.mean(offset * offset, axis=-1, keepdims=True)
    scale = lax.rsqrt(spread + EPSILON)
    return offset * scale, scale


def fwd_kernel(
    experts, tokens, wq, wk, wv, wp, small, seg_col, seg_row, valid_row, routes,
    normed, q_out, k_out, v_out, attended, lse_rows, middle, moe_low, probs_out, gates_out, vecs,
    total, bias, lse,
):
    pair = pl.program_id(0)
    count, model = tokens.shape
    lanes = lax.broadcasted_iota(jnp.int32, (count, PAIR), 1)

    @pl.when(pair == 0)
    def _():
        turned = jnp.transpose(small[...].astype(F32))
        vecs[...] = turned[experts : experts + 8]
        xhat, _ = norm_parts(tokens[...].astype(F32))
        normed[...] = (xhat * vecs[0:1] + vecs[1:2]).astype(LOW)
        keys_at = lax.broadcasted_iota(jnp.int32, (count, count), 1)
        rows_at = lax.broadcasted_iota(jnp.int32, (count, count), 0)
        allowed = (seg_col[...] == seg_row[...]) & ((valid_row[...] == 1) | (keys_at == rows_at))
        bias[...] = jnp.where(allowed, 0.0, MASKED)
        total[...] = jnp.zeros_like(total)
        lse[...] = jnp.zeros_like(lse)

    here = pl.ds(pl.multiple_of(pair * PAIR, PAIR), PAIR)
    source = normed[...]
    queries = (dot(source, wq[...]) + vecs[2:3, here]).astype(LOW) * LOW(HEAD**-0.5)
    keys = dot(source, wk[...]).astype(LOW)
    values = (dot(source, wv[...]) + vecs[3:4, here]).astype(LOW)
    q_out[...] = queries
    k_out[...] = keys
    v_out[...] = values
    mixed = None
    for half in range(2):
        side = (lanes < HEAD) if half == 0 else (lanes >= HEAD)
        own_keys = jnp.where(side, keys, LOW(0))
        own_values = jnp.where(side, values, LOW(0))
        scores = dot_nt(queries, own_keys) + bias[...]
        peak = jnp.max(scores, axis=1, keepdims=True)
        raised = jnp.exp(scores - peak)
        row_total = jnp.sum(raised, axis=1, keepdims=True)
        attn = (raised * (1.0 / row_total)).astype(LOW)
        part = dot(attn, own_values)
        mixed = part if mixed is None else mixed + part
        lse[...] = jnp.where(lanes == 2 * pair + half, peak + jnp.log(row_total), lse[...])
    mixed = mixed.astype(LOW)
    attended[...] = mixed
    total[...] += dot(mixed, wp[...])

    @pl.when(pair == pl.num_programs(0) - 1)
    def _():
        lse_rows[...] = jnp.transpose(lse[...])
        mid = tokens[...].astype(F32) + (total[...] + vecs[4:5])
        middle[...] = mid
        xhat, _ = norm_parts(mid)
        low = (xhat * vecs[5:6] + vecs[6:7]).astype(LOW)
        moe_low[...] = low
        logits = jnp.where(lanes < experts, dot(low, small[...]), -jnp.inf)
        raised = jnp.exp(logits - jnp.max(logits, axis=1, keepdims=True))
        probs = raised / jnp.sum(raised, axis=1, keepdims=True)
        probs_out[...] = probs
        gate_a = jnp.sum(jnp.where(lanes == routes[:, 0:1], probs, 0.0), axis=1, keepdims=True)
        gate_b = jnp.sum(jnp.where(lanes == routes[:, 1:2], probs, 0.0), axis=1, keepdims=True)
        gates_out[...] = jnp.where(lanes == 0, gate_a, gate_b)


def attention_forward(experts, tokens, params, segment_ids, patch_valid, routes):
    count, model = tokens.shape
    pairs = model // PAIR
    full = lambda shape: pl.BlockSpec(shape, lambda p: (0,) * len(shape))
    column = lambda first: pl.BlockSpec((model, PAIR), lambda p: (0, first + p))
    moving = pl.BlockSpec((count, PAIR), lambda p: (0, p))
    low = lambda *shape: jax.ShapeDtypeStruct(shape, LOW)
    f32 = lambda *shape: jax.ShapeDtypeStruct(shape, F32)
    return pl.pallas_call(
        functools.partial(fwd_kernel, experts),
        grid=(pairs,),
        out_shape=(
            low(count, model), low(count, model), low(count, model), low(count, model),
            low(count, model), f32(PAIR, count), f32(count, model), low(count, model),
            f32(count, PAIR), f32(count, PAIR), f32(8, model),
        ),
        in_specs=[
            full((count, model)),
            column(0),
            column(pairs),
            column(2 * pairs),
            pl.BlockSpec((PAIR, model), lambda p: (p, 3)),
            pl.BlockSpec((model, PAIR), lambda p: (0, 4 * pairs)),
            full((count, 1)),
            full((1, count)),
            full((1, count)),
            full((count, 2)),
        ],
        out_specs=[
            full((count, model)), moving, moving, moving, moving, full((PAIR, count)),
            full((count, model)), full((count, model)), full((count, PAIR)), full((count, PAIR)),
            full((8, model)),
        ],
        scratch_shapes=[
            pltpu.VMEM((count, model), F32),
            pltpu.VMEM((count, count), F32),
            pltpu.VMEM((count, PAIR), F32),
        ],
        compiler_params=pltpu.CompilerParams(
            dimension_semantics=("arbitrary",), vmem_limit_bytes=VMEM_LIMIT
        ),
        cost_estimate=pl.CostEstimate(flops=6 * 10**9, bytes_accessed=15 * 10**6, transcendentals=4 * 10**6),
        name="attention_forward",
    )(tokens, params, params, params, params, params, segment_ids.reshape(count, 1), segment_ids, patch_valid, routes)


def norm_back(grad, gain, xhat, scale):
    scaled = grad * gain
    mean_a = jnp.mean(scaled, axis=-1, keepdims=True)
    mean_b = jnp.mean(scaled * xhat, axis=-1, keepdims=True)
    return scale * (scaled - mean_a - xhat * mean_b)


def bwd_kernel(
    experts, tokens, normed, queries, keys, values, attended, lse_rows, middle, moe_low, probs, vecs,
    wq, wk, wv, wp, small, seg_col, seg_row, valid_col, routes, slots, token_rows, gate_slots, cotangent,
    grads, tokens_grad,
    bias, normed_t, branch, middle_grad, total, sums, moe_total, router,
):
    pair = pl.program_id(0)
    count, model = tokens.shape
    lanes = lax.broadcasted_iota(jnp.int32, (count, PAIR), 1)

    @pl.when(pair == 0)
    def _():
        keys_at = lax.broadcasted_iota(jnp.int32, (count, count), 0)
        rows_at = lax.broadcasted_iota(jnp.int32, (count, count), 1)
        allowed = (seg_col[...] == seg_row[...]) & ((valid_col[...] == 1) | (keys_at == rows_at))
        bias[...] = jnp.where(allowed, 0.0, MASKED)
        normed_t[...] = jnp.transpose(normed[...])
        total[...] = jnp.zeros_like(total)
        sums[...] = jnp.zeros_like(sums)
        total_slots = token_rows.shape[0]
        slot_at = lax.broadcasted_iota(jnp.int32, (count, total_slots), 1)
        hit_a = slot_at == slots[:, 0:1]
        hit_b = slot_at == slots[:, 1:2]
        picked = jnp.where(hit_a | hit_b, 1.0, 0.0).astype(LOW)
        moe_total[...] = dot(picked, token_rows[...])
        grad_a = jnp.sum(jnp.where(hit_a, gate_slots[...], 0.0), axis=1, keepdims=True)
        grad_b = jnp.sum(jnp.where(hit_b, gate_slots[...], 0.0), axis=1, keepdims=True)
        prob_grad = jnp.where(lanes == routes[:, 0:1], grad_a, 0.0) + jnp.where(
            lanes == routes[:, 1:2], grad_b, 0.0
        )
        own = probs[...]
        logit_grad = (own * (prob_grad - jnp.sum(prob_grad * own, axis=1, keepdims=True))).astype(LOW)
        router[...] = dot_tn(moe_low[...], logit_grad)
        moe_grad = moe_total[...] + dot_nt(logit_grad, small[...])
        xhat, scale = norm_parts(middle[...])
        sums[5:6] = jnp.sum(moe_grad * xhat, axis=0, keepdims=True)
        sums[6:7] = jnp.sum(moe_grad, axis=0, keepdims=True)
        mid = cotangent[...].astype(F32) + norm_back(moe_grad, vecs[5:6], xhat, scale)
        middle_grad[...] = mid
        low = mid.astype(LOW)
        branch[...] = low
        sums[4:5] = jnp.sum(low.astype(F32), axis=0, keepdims=True)

    here = pl.ds(pl.multiple_of(pair * PAIR, PAIR), PAIR)
    upward = branch[...]
    grad_mixed = dot_nt(upward, wp[...]).astype(LOW)
    grads[here, 3 * model : 4 * model] = dot_tn(attended[...], upward).astype(grads.dtype)
    q_pair, k_pair, v_pair = queries[...], keys[...], values[...]
    k_turned = jnp.transpose(k_pair)
    sides = lax.broadcasted_iota(jnp.int32, (PAIR, count), 0)
    q_grad_t, k_grad, v_grad = None, None, None
    for half in range(2):
        side = (lanes < HEAD) if half == 0 else (lanes >= HEAD)
        side_t = (sides < HEAD) if half == 0 else (sides >= HEAD)
        own_keys = jnp.where(side, k_pair, LOW(0))
        own_values = jnp.where(side, v_pair, LOW(0))
        own_queries = jnp.where(side, q_pair, LOW(0))
        own_grads = jnp.where(side, grad_mixed, LOW(0))
        own_turned = jnp.where(side_t, k_turned, LOW(0))
        scores = dot_nt(own_keys, q_pair) + bias[...]
        attn = jnp.exp(scores - lse_rows[pl.ds(2 * pair + half, 1), :])
        attn_grad = dot_nt(own_values, grad_mixed)
        mean = jnp.sum(attn * attn_grad, axis=0, keepdims=True)
        score_grad = (attn * (attn_grad - mean)).astype(LOW)
        v_part = dot(attn.astype(LOW), own_grads)
        k_part = dot(score_grad, own_queries)
        q_part = dot(own_turned, score_grad)
        if half == 0:
            q_grad_t, k_grad, v_grad = q_part, k_part, v_part
        else:
            q_grad_t, k_grad, v_grad = q_grad_t + q_part, k_grad + k_part, v_grad + v_part
    q_grad = (jnp.transpose(q_grad_t) * HEAD**-0.5).astype(LOW)
    k_grad = k_grad.astype(LOW)
    v_grad = v_grad.astype(LOW)
    sums[2:3, here] = jnp.sum(q_grad.astype(F32), axis=0, keepdims=True)
    sums[3:4, here] = jnp.sum(v_grad.astype(F32), axis=0, keepdims=True)
    source = normed_t[...]
    for which, part in enumerate((q_grad, k_grad, v_grad)):
        at = pl.ds(pl.multiple_of(which * model + pair * PAIR, PAIR), PAIR)
        grads[:, at] = dot(source, part).astype(grads.dtype)
    total[...] += dot_nt(q_grad, wq[...]) + dot_nt(k_grad, wk[...]) + dot_nt(v_grad, wv[...])

    @pl.when(pair == pl.num_programs(0) - 1)
    def _():
        grad = total[...]
        xhat, scale = norm_parts(tokens[...].astype(F32))
        sums[0:1] = jnp.sum(grad * xhat, axis=0, keepdims=True)
        sums[1:2] = jnp.sum(grad, axis=0, keepdims=True)
        tokens_grad[...] = (middle_grad[...] + norm_back(grad, vecs[0:1], xhat, scale)).astype(LOW)
        stacked = jnp.concatenate([sums[...], jnp.zeros((PAIR - 8, model), F32)], axis=0)
        turned = pltpu.roll(jnp.transpose(stacked), experts, 1)
        wide_lanes = lax.broadcasted_iota(jnp.int32, (model, PAIR), 1)
        grads[:, 4 * model :] = jnp.where(wide_lanes < experts, router[...], turned).astype(grads.dtype)


def attention_backward(
    experts, tokens, saved, params, segment_ids, patch_valid, routes, slots, token_rows, gate_slots, cotangent
):
    normed, queries, keys, values, attended, lse_rows, middle, moe_low, probs, vecs = saved
    count, model = tokens.shape
    pairs = model // PAIR
    total_slots = token_rows.shape[0]
    full = lambda shape: pl.BlockSpec(shape, lambda p: (0,) * len(shape))
    column = lambda first: pl.BlockSpec((model, PAIR), lambda p: (0, first + p))
    moving = pl.BlockSpec((count, PAIR), lambda p: (0, p))
    return pl.pallas_call(
        functools.partial(bwd_kernel, experts),
        grid=(pairs,),
        out_shape=(
            jax.ShapeDtypeStruct((model, 4 * model + PAIR), LOW),
            jax.ShapeDtypeStruct((count, model), LOW),
        ),
        in_specs=[
            full((count, model)),
            full((count, model)),
            moving, moving, moving, moving,
            full((PAIR, count)),
            full((count, model)),
            full((count, model)),
            full((count, PAIR)),
            full((8, model)),
            column(0),
            column(pairs),
            column(2 * pairs),
            pl.BlockSpec((PAIR, model), lambda p: (p, 3)),
            pl.BlockSpec((model, PAIR), lambda p: (0, 4 * pairs)),
            full((count, 1)),
            full((1, count)),
            full((count, 1)),
            full((count, 2)),
            full((count, 2)),
            full((total_slots, model)),
            full((1, total_slots)),
            full((count, model)),
        ],
        out_specs=[full((model, 4 * model + PAIR)), full((count, model))],
        scratch_shapes=[
            pltpu.VMEM((count, count), F32),
            pltpu.VMEM((model, count), LOW),
            pltpu.VMEM((count, model), LOW),
            pltpu.VMEM((count, model), F32),
            pltpu.VMEM((count, model), F32),
            pltpu.VMEM((8, model), F32),
            pltpu.VMEM((count, model), F32),
            pltpu.VMEM((model, PAIR), F32),
        ],
        compiler_params=pltpu.CompilerParams(
            dimension_semantics=("arbitrary",), vmem_limit_bytes=VMEM_LIMIT
        ),
        cost_estimate=pl.CostEstimate(flops=14 * 10**9, bytes_accessed=25 * 10**6, transcendentals=4 * 10**6),
        name="attention_backward",
    )(
        tokens, normed, queries, keys, values, attended, lse_rows, middle, moe_low, probs, vecs,
        params, params, params, params, params,
        segment_ids.reshape(count, 1), segment_ids, patch_valid.reshape(count, 1), routes, slots,
        token_rows, gate_slots, cotangent,
    )


def gelu_and_slope(v):
    root = 0.7978845608028654
    cubic = 0.044715
    square = v * v
    bend = jnp.tanh(root * v * (1.0 + cubic * square))
    slope = 0.5 * (1.0 + bend) + 0.5 * v * (1.0 - bend * bend) * root * (1.0 + 3.0 * cubic * square)
    return 0.5 * v * (1.0 + bend), slope


def expert_kernel(
    rows, ups, gates, w_in, b_in, w_out, b_out,
    y_out, dx_out, gate_grad, hidden_out, pre_out, bias_grad, out_bias_grad, weighted_out,
    y_acc, dx_acc, gate_acc,
):
    part = pl.program_id(0)
    x = rows[...]
    g = ups[...]

    @pl.when(part == 0)
    def _():
        y_acc[...] = jnp.zeros_like(y_acc)
        dx_acc[...] = jnp.zeros_like(dx_acc)
        gate_acc[...] = jnp.zeros_like(gate_acc)
        weighted = (gates[...] * g.astype(F32)).astype(LOW)
        weighted_out[...] = weighted
        out_bias_grad[...] = jnp.sum(weighted.astype(F32), axis=0, keepdims=True)

    pre = dot(x, w_in[0]) + b_in[...].astype(F32)
    back = dot_nt(g, w_out[0])
    value, slope = gelu_and_slope(pre)
    hidden = value.astype(LOW)
    gate_acc[...] += jnp.sum(hidden.astype(F32) * back, axis=1, keepdims=True)
    pre_grad = (slope * (gates[...] * back)).astype(LOW)
    hidden_out[...] = hidden
    pre_out[...] = pre_grad
    bias_grad[...] = jnp.sum(pre_grad.astype(F32), axis=0, keepdims=True)
    y_acc[...] += dot(hidden, w_out[0])
    dx_acc[...] += dot_nt(pre_grad, w_in[0])

    @pl.when(part == pl.num_programs(0) - 1)
    def _():
        bias = b_out[...].astype(F32)
        y_out[...] = (y_acc[...] + bias).astype(LOW)
        dx_out[...] = dx_acc[...].astype(LOW)
        gate_grad[...] = gate_acc[...] + jnp.sum(g.astype(F32) * bias, axis=1, keepdims=True)


def expert_stage(rows, ups, gates, w_in, b_in, w_out, b_out):
    count, model = rows.shape
    parts, _, wide = w_in.shape
    full = lambda shape: pl.BlockSpec(shape, lambda p: (0,) * len(shape))
    low = lambda *shape: jax.ShapeDtypeStruct(shape, LOW)
    f32 = lambda *shape: jax.ShapeDtypeStruct(shape, F32)
    return pl.pallas_call(
        expert_kernel,
        grid=(parts,),
        out_shape=(
            low(count, model), low(count, model), f32(count, 1), low(count, parts * wide),
            low(count, parts * wide), f32(1, parts * wide), f32(1, model), low(count, model),
        ),
        in_specs=[
            full((count, model)), full((count, model)), full((count, 1)),
            pl.BlockSpec((1, model, wide), lambda p: (p, 0, 0)),
            pl.BlockSpec((1, wide), lambda p: (0, p)),
            pl.BlockSpec((1, wide, model), lambda p: (p, 0, 0)),
            full((1, model)),
        ],
        out_specs=[
            full((count, model)), full((count, model)), full((count, 1)),
            pl.BlockSpec((count, wide), lambda p: (0, p)),
            pl.BlockSpec((count, wide), lambda p: (0, p)),
            pl.BlockSpec((1, wide), lambda p: (0, p)),
            full((1, model)),
            full((count, model)),
        ],
        scratch_shapes=[
            pltpu.VMEM((count, model), F32), pltpu.VMEM((count, model), F32), pltpu.VMEM((count, 1), F32),
        ],
        compiler_params=pltpu.CompilerParams(
            dimension_semantics=("arbitrary",), vmem_limit_bytes=VMEM_LIMIT
        ),
        cost_estimate=pl.CostEstimate(flops=23 * 10**9, bytes_accessed=35 * 10**6, transcendentals=4 * 10**6),
        name="expert_stage",
    )(rows, ups, gates, w_in, b_in, w_out, b_out)


def pair_slots(routes, priority, valid, experts, capacity):
    labels = jnp.arange(experts, dtype=jnp.int32)
    hot = ((routes[:, :, None] == labels) & (valid[:, None, None] == 1)).astype(F32)
    ahead = (priority[None, :] < priority[:, None]).astype(LOW)
    both = hot.reshape(routes.shape[0], 2 * experts).astype(LOW)
    earlier = dot(ahead, both).reshape(routes.shape[0], 2, experts)
    filled = jnp.sum(hot[:, 0], axis=0)
    first = jnp.sum(earlier[:, 0] * hot[:, 0], axis=1)
    second = jnp.sum((earlier[:, 1] + filled) * hot[:, 1], axis=1)
    place = jnp.stack([first, second], axis=1).astype(jnp.int32)
    kept = (place < capacity) & (valid[:, None] == 1)
    return jnp.where(kept, routes * capacity + place, -1)


def per_device(
    dims,
    tokens, segment_ids, patch_valid, routes, priority, gain_attn, shift_attn, w_qkv, query_bias, value_bias,
    w_proj, proj_bias, gain_moe, shift_moe, w_router, w_in, in_bias, w_out, out_bias, cotangent,
):
    count, model = tokens.shape
    experts = w_router.shape[1]
    capacity = (210 * count + 100 * experts - 1) // (100 * experts)
    shard_rows = gain_attn.shape[0]
    vectors = jnp.stack(
        [gain_attn, shift_attn, query_bias, value_bias, proj_bias, gain_moe, shift_moe], axis=1
    )
    pack = jnp.concatenate(
        [w_qkv, w_proj, w_router, vectors, jnp.zeros((shard_rows, PAIR - 7 - experts), LOW)], axis=1
    )
    params = gather_params(dims, pack)

    slots = pair_slots(routes, priority[0], patch_valid[0], experts, capacity)
    slot_ids = jnp.arange(experts * capacity, dtype=jnp.int32)[:, None]
    hit_a = slot_ids == slots[:, 0][None, :]
    hit_b = slot_ids == slots[:, 1][None, :]
    dispatch = (hit_a | hit_b).astype(LOW)
    swap = functools.partial(lax.all_to_all, axis_name="wide", split_axis=0, concat_axis=0, tiled=True)
    up_rows = dot(dispatch, cotangent).astype(LOW).reshape(experts, capacity, model)
    ups = swap(up_rows).reshape(-1, model)
    full_in = lax.all_gather(w_in[0], "narrow", axis=0, tiled=False)
    full_out = lax.all_gather(w_out[0], "narrow", axis=0, tiled=False)
    full_in_bias = lax.all_gather(in_bias, "narrow", axis=1, tiled=True)

    (normed, queries, keys, values, attended, lse_rows, middle, moe_low, probs, gates, vecs) = attention_forward(
        experts, tokens, params, segment_ids, patch_valid, routes
    )
    gate_slot = jnp.sum(
        jnp.where(hit_a, gates[:, 0][None, :], 0.0) + jnp.where(hit_b, gates[:, 1][None, :], 0.0), axis=1
    )
    rows = swap(dot(dispatch, moe_low).astype(LOW).reshape(experts, capacity, model)).reshape(-1, model)
    gate_rows = swap(gate_slot.reshape(experts, capacity)).reshape(-1, 1)

    y, dx, gate_grad, hidden, pre_grad, bias_grad, out_bias_grad, weighted = expert_stage(
        rows, ups, gate_rows, full_in, full_in_bias, full_out, out_bias
    )
    token_rows = swap(dx.reshape(-1, capacity, model)).reshape(-1, model)
    gate_slots = swap(gate_grad.reshape(-1, capacity)).reshape(1, -1)
    returned = swap(y.reshape(-1, capacity, model)).reshape(-1, model)

    parts = full_in.shape[0]
    grad_in = dot_tn(pre_grad, rows).reshape(parts, -1, model).astype(LOW)
    grad_out = dot_tn(hidden, weighted).reshape(parts, -1, model).astype(LOW)
    grad_in = lax.psum_scatter(grad_in, "narrow", scatter_dimension=0, tiled=True)[0].astype(F32)
    grad_out = lax.psum_scatter(grad_out, "narrow", scatter_dimension=0, tiled=True)[0].astype(F32)
    grad_in_bias = lax.psum_scatter(bias_grad[0], "narrow", scatter_dimension=0, tiled=True)
    grad_out_bias = lax.psum(out_bias_grad, "narrow")

    grads, tokens_grad = attention_backward(
        experts, tokens,
        (normed, queries, keys, values, attended, lse_rows, middle, moe_low, probs, vecs),
        params, segment_ids, patch_valid, routes, slots, token_rows, gate_slots, cotangent,
    )
    shares = scatter_grads(dims, grads)

    picked_a = lax.dot_general(hit_a.astype(LOW), returned, (((0,), (0,)), ((), ())), preferred_element_type=F32)
    picked_b = lax.dot_general(hit_b.astype(LOW), returned, (((0,), (0,)), ((), ())), preferred_element_type=F32)
    block_out = (middle + gates[:, 0:1] * picked_a + gates[:, 1:2] * picked_b).astype(LOW)

    at = 4 * model + experts
    vector = lambda i: shares[:, at + i]
    return (
        block_out,
        tokens_grad,
        vector(0),
        vector(1),
        shares[:, : 3 * model],
        vector(2),
        vector(3),
        shares[:, 3 * model : 4 * model],
        vector(4),
        vector(5),
        vector(6),
        shares[:, 4 * model : at],
        jnp.transpose(grad_in)[None],
        grad_in_bias[None],
        grad_out[None],
        grad_out_bias,
    )


def solution(mesh):
    dims = grid_of(mesh.shape["wide"], mesh.shape["narrow"])
    every = ("wide", "narrow")
    rows, vector = P(every, None), P(every)
    return jax.shard_map(
        functools.partial(per_device, dims),
        mesh=mesh,
        in_specs=(
            rows, rows, rows, rows, rows, vector, vector, rows, vector, vector, rows, vector, vector, vector,
            rows, P("wide", None, "narrow"), P("wide", "narrow"), P("wide", "narrow", None), P("wide", None), rows,
        ),
        out_specs=(
            rows, rows, vector, vector, rows, vector, vector, rows, vector, vector, vector, rows,
            P("wide", None, "narrow"), P("wide", "narrow"), P("wide", "narrow", None), P("wide", None),
        ),
        check_vma=False,
    )
```

```python
import functools

import jax
import jax.numpy as jnp
from jax import lax
from jax.experimental import pallas as pl
from jax.experimental.pallas import tpu as pltpu
from jax.sharding import PartitionSpec as P

HEAD = 64
PAIR = 2 * HEAD
EPSILON = 1e-06
MASKED = -1000000000.0
MESH = pl.DeviceIdType.MESH
LOW = jnp.bfloat16
F32 = jnp.float32
VMEM_LIMIT = 58 * 1024 * 1024


def dot(a, b):
    return jnp.dot(a, b, preferred_element_type=F32)


def dot_nt(a, b):
    return lax.dot_general(a, b, (((1,), (1,)), ((), ())), preferred_element_type=F32)


def dot_tn(a, b):
    return lax.dot_general(a, b, (((0,), (0,)), ((), ())), preferred_element_type=F32)


def grid_of(wide, narrow):
    along_x = 1 << ((wide.bit_length() - 1) // 2)
    return wide // along_x, along_x, narrow // 2, 2


def place_of(dims):
    depth, across, rows, cores = dims
    wide, narrow = lax.axis_index("wide"), lax.axis_index("narrow")
    return wide // across, wide % across, narrow // cores, narrow % cores


def device_at(dims, z, x, y, c):
    depth, across, rows, cores = dims
    return (z * across + x, y * cores + c)


def greet(peers):
    barrier = pltpu.get_barrier_semaphore()
    for peer in peers:
        pl.semaphore_signal(barrier, inc=1, device_id=peer, device_id_type=MESH)
    pl.semaphore_wait(barrier, len(peers))


def neighbours(dims):
    depth, across, rows, cores = dims
    z, x, y, c = place_of(dims)
    peers = [device_at(dims, (z + d) % depth, x, y, c) for d in range(1, depth)]
    peers += [device_at(dims, z, (x + d) % across, y, c) for d in range(1, across)]
    peers += [device_at(dims, z, x, (y + d) % rows, c) for d in range(1, rows)]
    peers += [device_at(dims, z, x, y, 1 - c)]
    return peers


def scatter_kernel(
    dims, cut, grads, out, mine, r1, r2a, r2b, r3x, r3y, r4, out_a, out_b, out_z,
    s1, q1, s2a, q2a, s2b, q2b, s3x, q3x, s3y, q3y, s4, q4, local,
):
    depth, across, rows, cores = dims
    z, x, y, c = place_of(dims)
    width = grads.shape[-1]
    rest = width - cut

    def send(src, dst, ssem, rsem, to):
        copy = pltpu.make_async_remote_copy(
            src_ref=src, dst_ref=dst, send_sem=ssem, recv_sem=rsem, device_id=to, device_id_type=MESH
        )
        copy.start()
        return copy

    greet(neighbours(dims))
    order = [*range(1, depth), 0]
    first, keeps = {}, {}
    for dz in order:
        planes = pl.ds(((z + dz) % depth) * across, across)
        first[dz] = send(
            grads.at[planes, :, 1 - c], r1.at[dz], s1.at[dz], q1.at[dz],
            device_at(dims, z, x, y, 1 - c),
        )
        keeps[dz] = pltpu.make_async_copy(grads.at[planes, :, c], mine.at[dz], local.at[dz])
        keeps[dz].start()
    corner_a, corner_b, side_x, side_y, last = {}, {}, {}, {}, {}

    def total(*terms):
        acc = terms[0].astype(F32)
        for term in terms[1:]:
            acc = acc + term.astype(F32)
        return acc

    def begin(dz):
        keeps[dz].wait()
        first[dz].wait_recv()
        for a in range(across):
            for b in range(rows):
                mine[dz, a, b] = total(mine[dz, a, b], r1[dz, a, b]).astype(LOW)
        for dx in range(1, across):
            for dy in range(1, rows):
                at = (dz * (across - 1) + dx - 1) * (rows - 1) + dy - 1
                block = mine.at[dz, (x + dx) % across, (y + dy) % rows]
                corner_a[dz, dx, dy] = send(
                    block.at[:, pl.ds(0, cut)], r2a.at[at], s2a.at[at], q2a.at[at],
                    device_at(dims, z, x, (y + dy) % rows, c),
                )
                corner_b[dz, dx, dy] = send(
                    block.at[:, pl.ds(cut, rest)], r2b.at[at], s2b.at[at], q2b.at[at],
                    device_at(dims, z, (x + dx) % across, y, c),
                )

    def middle(dz):
        for dx in range(1, across):
            at = dz * (across - 1) + dx - 1
            block = mine.at[dz, (x + dx) % across, y]
            arrived = []
            for dy in range(1, rows):
                corner_a[dz, dx, dy].wait_recv()
                arrived.append(r2a[at * (rows - 1) + dy - 1])
            out_a[at, :, pl.ds(0, cut)] = total(block[:, pl.ds(0, cut)], *arrived).astype(LOW)
            out_a[at, :, pl.ds(cut, rest)] = block[:, pl.ds(cut, rest)]
            side_x[dz, dx] = send(
                out_a.at[at], r3x.at[at], s3x.at[at], q3x.at[at],
                device_at(dims, z, (x + dx) % across, y, c),
            )
        for dy in range(1, rows):
            at = dz * (rows - 1) + dy - 1
            block = mine.at[dz, x, (y + dy) % rows]
            arrived = []
            for dx in range(1, across):
                corner_b[dz, dx, dy].wait_recv()
                arrived.append(r2b[(dz * (across - 1) + dx - 1) * (rows - 1) + dy - 1])
            out_b[at, :, pl.ds(0, cut)] = block[:, pl.ds(0, cut)]
            out_b[at, :, pl.ds(cut, rest)] = total(block[:, pl.ds(cut, rest)], *arrived).astype(LOW)
            side_y[dz, dy] = send(
                out_b.at[at], r3y.at[at], s3y.at[at], q3y.at[at],
                device_at(dims, z, x, (y + dy) % rows, c),
            )

    def end(dz):
        arrived = []
        for dx in range(1, across):
            side_x[dz, dx].wait_recv()
            arrived.append(r3x[dz * (across - 1) + dx - 1])
        for dy in range(1, rows):
            side_y[dz, dy].wait_recv()
            arrived.append(r3y[dz * (rows - 1) + dy - 1])
        summed = total(mine[dz, x, y], *arrived)
        if dz:
            out_z[dz - 1] = summed.astype(LOW)
            last[dz] = send(
                out_z.at[dz - 1], r4.at[dz - 1], s4.at[dz - 1], q4.at[dz - 1],
                device_at(dims, (z + dz) % depth, x, y, c),
            )
        else:
            out[...] = summed

    for step in range(depth + 2):
        if step < depth:
            begin(order[step])
        if 0 <= step - 1 < depth:
            middle(order[step - 1])
        if 0 <= step - 2 < depth:
            end(order[step - 2])
    for dz in range(1, depth):
        last[dz].wait_recv()
        out[...] += r4[dz - 1].astype(F32)
    for group in (first, corner_a, corner_b, side_x, side_y, last):
        for copy in group.values():
            copy.wait_send()


def scatter_grads(dims, grads):
    depth, across, rows, cores = dims
    wide = depth * across
    height, width = grads.shape[0] // (wide * rows * cores), grads.shape[1]
    cut = (width // 256) * 128
    grads = grads.reshape(wide, rows, cores, height, width)
    n_x, n_y = depth * (across - 1), depth * (rows - 1)
    n_c = n_x * (rows - 1)
    sems = []
    for size in (depth, n_c, n_c, n_x, n_y, depth - 1):
        sems += [pltpu.SemaphoreType.DMA((size,))] * 2
    return pl.pallas_call(
        functools.partial(scatter_kernel, dims, cut),
        out_shape=jax.ShapeDtypeStruct((height, width), F32),
        in_specs=[pl.BlockSpec(memory_space=pl.ANY)],
        out_specs=pl.BlockSpec(memory_space=pltpu.VMEM),
        scratch_shapes=[
            pltpu.VMEM((depth, across, rows, height, width), LOW),
            pltpu.VMEM((depth, across, rows, height, width), LOW),
            pltpu.VMEM((n_c, height, cut), LOW),
            pltpu.VMEM((n_c, height, width - cut), LOW),
            pltpu.VMEM((n_x, height, width), LOW),
            pltpu.VMEM((n_y, height, width), LOW),
            pltpu.VMEM((depth - 1, height, width), LOW),
            pltpu.VMEM((n_x, height, width), LOW),
            pltpu.VMEM((n_y, height, width), LOW),
            pltpu.VMEM((depth - 1, height, width), LOW),
            *sems,
            pltpu.SemaphoreType.DMA((depth,)),
        ],
        compiler_params=pltpu.CompilerParams(
            collective_id=1, has_side_effects=True, vmem_limit_bytes=VMEM_LIMIT
        ),
        name="scatter_grads",
    )(grads)


def norm_parts(values):
    center = jnp.mean(values, axis=-1, keepdims=True)
    offset = values - center
    spread = jnp.mean(offset * offset, axis=-1, keepdims=True)
    scale = lax.rsqrt(spread + EPSILON)
    return offset * scale, scale


def column_of(row):
    return jnp.transpose(jnp.broadcast_to(row, (PAIR, row.shape[1])))[:, 0:1]


def front_kernel(
    dims, experts, capacity, gathered, shard, tokens, seg_row, valid_row, routes, priority, cotangent, w_out, b_in, *rest
):
    depth, across, rows, cores = dims
    wide, narrow = depth * across, rows * cores
    (
        params, normed, q_out, k_out, v_out, attended, lse_rows, middle, moe_low, probs_out, gates_out, vecs,
        slots_out, slot_rows, ups, full_b_in,
    ) = rest[:16]
    side_out = rest[16 : 15 + rows]
    (
        total, bias, lse, up_send,
        s1, r1, sx, rx, sy, ry, sa, ra, sb, rb, sc, rc, s_up, r_up, s_w, r_w, s_b, r_b, local,
    ) = rest[15 + rows :]
    z, x, y, c = place_of(dims)
    me, n = z * across + x, y * cores + c
    count, model = tokens.shape
    stride = ups.shape[1]
    lanes = lax.broadcasted_iota(jnp.int32, (count, PAIR), 1)

    def remote(src, dst, ssem, rsem, to):
        return pltpu.make_async_remote_copy(
            src_ref=src, dst_ref=dst, send_sem=ssem, recv_sem=rsem, device_id=to, device_id_type=MESH
        )

    def send(src, dst, ssem, rsem, to):
        copy = remote(src, dst, ssem, rsem, to)
        copy.start()
        return copy

    peers = [((me + d) % wide, n) for d in range(1, wide)]
    peers += [(me, (n + d) % narrow) for d in range(1, narrow)]
    greet(peers)

    first, by_x, by_y, half_a, half_b, by_core = {}, {}, {}, {}, {}, {}
    keeps = []
    if not gathered:
        width = shard.shape[1]
        cut = (width // 256) * 128

        def block(dz, dx, dy, core):
            at = ((z - dz) % depth) * across + (x - dx) % across
            return params.at[(at * rows + (y - dy) % rows) * cores + core]

        own = block(0, 0, 0, c)
        keeps.append(pltpu.make_async_copy(shard, own, local.at[0]))
        keeps[-1].start()
        for dz in range(1, depth):
            first[dz] = send(
                shard, own, s1.at[dz - 1], r1.at[dz - 1], device_at(dims, (z + dz) % depth, x, y, c)
            )

    def to_core(dz, dx, dy):
        at = (dz * across + dx) * rows + dy
        src = shard if (dz, dx, dy) == (0, 0, 0) else block(dz, dx, dy, c)
        by_core[at] = send(
            src, block(dz, dx, dy, c), sc.at[at], rc.at[at], device_at(dims, z, x, y, 1 - c)
        )

    def spread(dz):
        if dz:
            first[dz].wait_recv()
        src = block(dz, 0, 0, c) if dz else shard
        for dx in range(1, across):
            at = dz * (across - 1) + dx - 1
            by_x[dz, dx] = send(
                src, block(dz, 0, 0, c), sx.at[at], rx.at[at],
                device_at(dims, z, (x + dx) % across, y, c),
            )
        for dy in range(1, rows):
            at = dz * (rows - 1) + dy - 1
            by_y[dz, dy] = send(
                src, block(dz, 0, 0, c), sy.at[at], ry.at[at],
                device_at(dims, z, x, (y + dy) % rows, c),
            )
        to_core(dz, 0, 0)

    def corner(dz):
        for dx in range(1, across):
            by_x[dz, dx].wait_recv()
            part = block(dz, dx, 0, c).at[:, pl.ds(0, cut)]
            for dy in range(1, rows):
                at = (dz * (across - 1) + dx - 1) * (rows - 1) + dy - 1
                half_a[dz, dx, dy] = send(
                    part, part, sa.at[at], ra.at[at], device_at(dims, z, x, (y + dy) % rows, c)
                )
            to_core(dz, dx, 0)
        for dy in range(1, rows):
            by_y[dz, dy].wait_recv()
            part = block(dz, 0, dy, c).at[:, pl.ds(cut, width - cut)]
            for dx in range(1, across):
                at = (dz * (across - 1) + dx - 1) * (rows - 1) + dy - 1
                half_b[dz, dx, dy] = send(
                    part, part, sb.at[at], rb.at[at], device_at(dims, z, (x + dx) % across, y, c)
                )
            to_core(dz, 0, dy)

    def finish(dz):
        for dx in range(1, across):
            for dy in range(1, rows):
                half_a[dz, dx, dy].wait_recv()
                half_b[dz, dx, dy].wait_recv()
                to_core(dz, dx, dy)

    if not gathered:
        spread(0)
    b_copies = []
    for d in range(1, narrow):
        b_copies.append(send(b_in, full_b_in.at[n], s_b.at[d], r_b.at[d], (me, (n + d) % narrow)))
    keeps.append(pltpu.make_async_copy(b_in, full_b_in.at[n], local.at[1]))
    keeps[-1].start()

    half = PAIR // 2
    valid = valid_row[...].astype(F32)
    valid_col = column_of(valid)
    rank_row = priority[...].astype(F32)
    ahead = jnp.where(rank_row < column_of(rank_row), 1.0, 0.0).astype(LOW)
    first_at, second_at = routes[:, 0:1], routes[:, 1:2]
    hit_first, hit_second = lanes == first_at, lanes == second_at + half
    hot = jnp.where(hit_first | hit_second, valid_col, 0.0)
    earlier = dot(ahead, hot.astype(LOW))
    filled = pltpu.roll(jnp.sum(hot, axis=0, keepdims=True), half, 1)
    filled = jnp.broadcast_to(jnp.where(lanes[0:1] >= half, filled, 0.0), (8, PAIR))[0:1]
    earlier = earlier + filled
    place_a = jnp.sum(jnp.where(hit_first, earlier, 0.0), axis=1, keepdims=True).astype(jnp.int32)
    place_b = jnp.sum(jnp.where(hit_second, earlier, 0.0), axis=1, keepdims=True).astype(jnp.int32)
    kept_a = (place_a < capacity) & (valid_col > 0.5)
    kept_b = (place_b < capacity) & (valid_col > 0.5)
    slot_a = jnp.where(kept_a, first_at * stride + place_a, -1)
    slot_b = jnp.where(kept_b, second_at * stride + place_b, -1)
    slots = jnp.where(lanes == 0, slot_a, slot_b)
    slots_out[...] = slots
    slot_rows[...] = jnp.transpose(slots.astype(F32))[0:8].astype(jnp.int32)

    segments = seg_row[...].astype(F32)
    keys_at = lax.broadcasted_iota(jnp.int32, (count, count), 1)
    rows_at = lax.broadcasted_iota(jnp.int32, (count, count), 0)
    allowed = (column_of(segments) == segments) & ((valid > 0.5) | (keys_at == rows_at))
    bias[...] = jnp.where(allowed, 0.0, MASKED)
    xhat, _ = norm_parts(tokens[...].astype(F32))
    total[...] = xhat
    lse[...] = jnp.zeros_like(lse)

    row_at = lax.broadcasted_iota(jnp.int32, (stride, count), 0)

    def up_copy(d, to):
        return remote(up_send.at[to], ups.at[me], s_up.at[d], r_up.at[d], (to, n))

    def rows_for(expert):
        start = expert * stride
        hit = (slot_rows[0:1] - start == row_at) | (slot_rows[1:2] - start == row_at)
        return dot(jnp.where(hit, 1.0, 0.0).astype(LOW), cotangent[...]).astype(LOW)

    def dispatch(k, carry):
        d = (k + wide // 2 - 1) % (wide - 1) + 1
        to = (me + d) % wide
        up_send[to] = rows_for(to)
        up_copy(d, to).start()
        return carry

    if not gathered:
        for step in range(1, depth):
            spread(step)
            corner(step - 1)
            if step >= 2:
                finish(step - 2)
        lax.fori_loop(0, (wide - 1) // 2, dispatch, 0)
        corner(depth - 1)
        finish(depth - 2)
        lax.fori_loop((wide - 1) // 2, wide - 1, dispatch, 0)
        finish(depth - 1)
    else:
        lax.fori_loop(0, wide - 1, dispatch, 0)
        keeps.append(pltpu.make_async_copy(shard, params, local.at[0]))
        keeps[-1].start()
    up_send[me] = rows_for(me)
    keep_up = pltpu.make_async_copy(up_send.at[me], ups.at[me], local.at[2])
    keep_up.start()
    for copy in by_core.values():
        copy.wait_recv()
    for copy in keeps:
        copy.wait()
    w_copies = []
    for dy in range(1, rows):
        w_copies.append(
            send(
                w_out, side_out[dy - 1], s_w.at[dy - 1], r_w.at[dy - 1],
                device_at(dims, z, x, (y + dy) % rows, c),
            )
        )


    def columns(at):
        return params[:, at] if gathered else params[:, :, at].reshape(model, PAIR)

    small = columns(pl.ds(4 * model, PAIR))
    vecs[...] = jnp.transpose(small.astype(F32))[experts : experts + 8]
    normed[...] = (total[...] * vecs[0:1] + vecs[1:2]).astype(LOW)

    def attend(pair, carry):
        at = lambda which: pl.ds(pl.multiple_of(which * model + pair * PAIR, PAIR), PAIR)
        here = at(0)
        source = normed[...]
        queries = (dot(source, columns(at(0))) + vecs[2:3, here]).astype(LOW) * LOW(HEAD**-0.5)
        keys = dot(source, columns(at(1))).astype(LOW)
        values = (dot(source, columns(at(2))) + vecs[3:4, here]).astype(LOW)
        q_out[:, here] = queries
        k_out[:, here] = keys
        v_out[:, here] = values
        mixed = None
        for part in range(2):
            side = (lanes < HEAD) if part == 0 else (lanes >= HEAD)
            own_keys = jnp.where(side, keys, LOW(0))
            own_values = jnp.where(side, values, LOW(0))
            scores = dot_nt(queries, own_keys) + bias[...]
            peak = jnp.max(scores, axis=1, keepdims=True)
            raised = jnp.exp(scores - peak)
            row_total = jnp.sum(raised, axis=1, keepdims=True)
            attn = (raised * (1.0 / row_total)).astype(LOW)
            piece = dot(attn, own_values)
            mixed = piece if mixed is None else mixed + piece
            lse[...] = jnp.where(lanes == 2 * pair + part, peak + jnp.log(row_total), lse[...])
        mixed = mixed.astype(LOW)
        attended[:, here] = mixed
        return carry

    lax.fori_loop(0, model // PAIR, attend, 0)

    def project(pair, carry):
        here = pl.ds(pl.multiple_of(pair * PAIR, PAIR), PAIR)
        there = pl.ds(pl.multiple_of(3 * model + pair * PAIR, PAIR), PAIR)
        total[:, here] = dot(attended[...], columns(there))
        return carry

    lax.fori_loop(0, model // PAIR, project, 0)
    lse_rows[...] = jnp.transpose(lse[...])
    mid = tokens[...].astype(F32) + (total[...] + vecs[4:5])
    middle[...] = mid
    xhat, _ = norm_parts(mid)
    low = (xhat * vecs[5:6] + vecs[6:7]).astype(LOW)
    moe_low[...] = low
    logits = jnp.where(lanes < experts, dot(low, columns(pl.ds(4 * model, PAIR))), -jnp.inf)
    raised = jnp.exp(logits - jnp.max(logits, axis=1, keepdims=True))
    probs = raised / jnp.sum(raised, axis=1, keepdims=True)
    probs_out[...] = probs
    gate_a = jnp.sum(jnp.where(lanes == first_at, probs, 0.0), axis=1, keepdims=True)
    gate_b = jnp.sum(jnp.where(lanes == second_at, probs, 0.0), axis=1, keepdims=True)
    gates_out[...] = jnp.where(lanes == 0, gate_a, gate_b)

    def settle(k, carry):
        d = k + 1
        up_copy(d, (me + d) % wide).wait_send()
        up_copy(d, (me - d + wide) % wide).wait_recv()
        return carry

    lax.fori_loop(0, wide - 1, settle, 0)
    keep_up.wait()
    for copy in w_copies + b_copies:
        copy.wait()
    for group in (first, by_x, by_y, half_a, half_b, by_core):
        for copy in group.values():
            copy.wait_send()


def front_stage(
    dims, experts, capacity, stride, gathered, shard, tokens, segment_ids, patch_valid, routes, priority,
    cotangent, w_out, in_bias,
):
    depth, across, rows, cores = dims
    wide, narrow = depth * across, rows * cores
    count, model = tokens.shape
    any_, vmem = pl.BlockSpec(memory_space=pl.ANY), pl.BlockSpec(memory_space=pltpu.VMEM)
    low = lambda *shape: jax.ShapeDtypeStruct(shape, LOW)
    f32 = lambda *shape: jax.ShapeDtypeStruct(shape, F32)
    i32 = lambda *shape: jax.ShapeDtypeStruct(shape, jnp.int32)
    height, width = shard.shape
    full = (height, width) if gathered else (wide * narrow, height, width)
    corners = depth * (across - 1) * (rows - 1)
    sems = []
    for size in (
        depth - 1, depth * (across - 1), depth * (rows - 1), corners, corners, depth * across * rows,
        wide, rows - 1, narrow,
    ):
        sems += [pltpu.SemaphoreType.DMA((size,))] * 2
    outs = pl.pallas_call(
        functools.partial(front_kernel, dims, experts, capacity, gathered),
        out_shape=(
            low(*full), low(count, model), low(count, model), low(count, model), low(count, model),
            low(count, model), f32(PAIR, count), f32(count, model), low(count, model), f32(count, PAIR),
            f32(count, PAIR), f32(8, model), i32(count, PAIR), i32(8, count), low(wide, stride, model),
            f32(narrow, 1, in_bias.shape[1]), *[low(*w_out.shape)] * (rows - 1),
        ),
        in_specs=[any_] + [vmem] * 6 + [any_] * 2,
        out_specs=[vmem] * 14 + [any_] * (1 + rows),
        scratch_shapes=[
            pltpu.VMEM((count, model), F32),
            pltpu.VMEM((count, count), F32),
            pltpu.VMEM((count, PAIR), F32),
            pltpu.VMEM((wide, stride, model), LOW),
            *sems,
            pltpu.SemaphoreType.DMA((3,)),
        ],
        compiler_params=pltpu.CompilerParams(
            collective_id=0, has_side_effects=True, vmem_limit_bytes=VMEM_LIMIT
        ),
        cost_estimate=pl.CostEstimate(flops=7 * 10**9, bytes_accessed=20 * 10**6, transcendentals=4 * 10**6),
        name="front_stage",
    )(shard, tokens, segment_ids, patch_valid, routes, priority, cotangent, w_out, in_bias)
    params = outs[0] if gathered else outs[0].reshape(wide * narrow * height, width)
    return params, outs[1:12], outs[12:16], outs[16:]


def norm_back(grad, gain, xhat, scale):
    scaled = grad * gain
    mean_a = jnp.mean(scaled, axis=-1, keepdims=True)
    mean_b = jnp.mean(scaled * xhat, axis=-1, keepdims=True)
    return scale * (scaled - mean_a - xhat * mean_b)


def bwd_kernel(
    experts, tokens, normed, queries, keys, values, attended, lse_rows, middle, moe_low, probs, vecs,
    wq, wk, wv, wp, small, seg_col, seg_row, valid_col, routes, slots, token_rows, gate_slots, cotangent,
    grads, tokens_grad,
    bias, normed_t, branch, middle_grad, total, sums, moe_total, router,
):
    pair = pl.program_id(0)
    count, model = tokens.shape
    lanes = lax.broadcasted_iota(jnp.int32, (count, PAIR), 1)

    @pl.when(pair == 0)
    def _():
        keys_at = lax.broadcasted_iota(jnp.int32, (count, count), 0)
        rows_at = lax.broadcasted_iota(jnp.int32, (count, count), 1)
        allowed = (seg_col[...] == seg_row[...]) & ((valid_col[...] == 1) | (keys_at == rows_at))
        bias[...] = jnp.where(allowed, 0.0, MASKED)
        normed_t[...] = jnp.transpose(normed[...])
        total[...] = jnp.zeros_like(total)
        sums[...] = jnp.zeros_like(sums)
        total_slots = token_rows.shape[0]
        slot_at = lax.broadcasted_iota(jnp.int32, (count, total_slots), 1)
        hit_a = slot_at == slots[:, 0:1]
        hit_b = slot_at == slots[:, 1:2]
        picked = jnp.where(hit_a | hit_b, 1.0, 0.0).astype(LOW)
        moe_total[...] = dot(picked, token_rows[...])
        grad_a = jnp.sum(jnp.where(hit_a, gate_slots[...], 0.0), axis=1, keepdims=True)
        grad_b = jnp.sum(jnp.where(hit_b, gate_slots[...], 0.0), axis=1, keepdims=True)
        prob_grad = jnp.where(lanes == routes[:, 0:1], grad_a, 0.0) + jnp.where(
            lanes == routes[:, 1:2], grad_b, 0.0
        )
        own = probs[...]
        logit_grad = (own * (prob_grad - jnp.sum(prob_grad * own, axis=1, keepdims=True))).astype(LOW)
        router[...] = dot_tn(moe_low[...], logit_grad)
        moe_grad = moe_total[...] + dot_nt(logit_grad, small[...])
        xhat, scale = norm_parts(middle[...])
        sums[5:6] = jnp.sum(moe_grad * xhat, axis=0, keepdims=True)
        sums[6:7] = jnp.sum(moe_grad, axis=0, keepdims=True)
        mid = cotangent[...].astype(F32) + norm_back(moe_grad, vecs[5:6], xhat, scale)
        middle_grad[...] = mid
        low = mid.astype(LOW)
        branch[...] = low
        sums[4:5] = jnp.sum(low.astype(F32), axis=0, keepdims=True)

    here = pl.ds(pl.multiple_of(pair * PAIR, PAIR), PAIR)
    upward = branch[...]
    grad_mixed = dot_nt(upward, wp[...]).astype(LOW)
    grads[here, 3 * model : 4 * model] = dot_tn(attended[...], upward).astype(grads.dtype)
    q_pair, k_pair, v_pair = queries[...], keys[...], values[...]
    k_turned = jnp.transpose(k_pair)
    sides = lax.broadcasted_iota(jnp.int32, (PAIR, count), 0)
    q_grad_t, k_grad, v_grad = None, None, None
    for half in range(2):
        side = (lanes < HEAD) if half == 0 else (lanes >= HEAD)
        side_t = (sides < HEAD) if half == 0 else (sides >= HEAD)
        own_keys = jnp.where(side, k_pair, LOW(0))
        own_values = jnp.where(side, v_pair, LOW(0))
        own_queries = jnp.where(side, q_pair, LOW(0))
        own_grads = jnp.where(side, grad_mixed, LOW(0))
        own_turned = jnp.where(side_t, k_turned, LOW(0))
        scores = dot_nt(own_keys, q_pair) + bias[...]
        attn = jnp.exp(scores - lse_rows[pl.ds(2 * pair + half, 1), :])
        attn_grad = dot_nt(own_values, grad_mixed)
        mean = jnp.sum(attn * attn_grad, axis=0, keepdims=True)
        score_grad = (attn * (attn_grad - mean)).astype(LOW)
        v_part = dot(attn.astype(LOW), own_grads)
        k_part = dot(score_grad, own_queries)
        q_part = dot(own_turned, score_grad)
        if half == 0:
            q_grad_t, k_grad, v_grad = q_part, k_part, v_part
        else:
            q_grad_t, k_grad, v_grad = q_grad_t + q_part, k_grad + k_part, v_grad + v_part
    q_grad = (jnp.transpose(q_grad_t) * HEAD**-0.5).astype(LOW)
    k_grad = k_grad.astype(LOW)
    v_grad = v_grad.astype(LOW)
    sums[2:3, here] = jnp.sum(q_grad.astype(F32), axis=0, keepdims=True)
    sums[3:4, here] = jnp.sum(v_grad.astype(F32), axis=0, keepdims=True)
    source = normed_t[...]
    for which, part in enumerate((q_grad, k_grad, v_grad)):
        at = pl.ds(pl.multiple_of(which * model + pair * PAIR, PAIR), PAIR)
        grads[:, at] = dot(source, part).astype(grads.dtype)
    total[...] += dot_nt(q_grad, wq[...]) + dot_nt(k_grad, wk[...]) + dot_nt(v_grad, wv[...])

    @pl.when(pair == pl.num_programs(0) - 1)
    def _():
        grad = total[...]
        xhat, scale = norm_parts(tokens[...].astype(F32))
        sums[0:1] = jnp.sum(grad * xhat, axis=0, keepdims=True)
        sums[1:2] = jnp.sum(grad, axis=0, keepdims=True)
        tokens_grad[...] = (middle_grad[...] + norm_back(grad, vecs[0:1], xhat, scale)).astype(LOW)
        stacked = jnp.concatenate([sums[...], jnp.zeros((PAIR - 8, model), F32)], axis=0)
        turned = pltpu.roll(jnp.transpose(stacked), experts, 1)
        wide_lanes = lax.broadcasted_iota(jnp.int32, (model, PAIR), 1)
        grads[:, 4 * model :] = jnp.where(wide_lanes < experts, router[...], turned).astype(grads.dtype)


def attention_backward(
    experts, tokens, saved, params, segment_ids, patch_valid, routes, slots, token_rows, gate_slots, cotangent
):
    normed, queries, keys, values, attended, lse_rows, middle, moe_low, probs, vecs = saved
    count, model = tokens.shape
    pairs = model // PAIR
    total_slots = token_rows.shape[0]
    full = lambda shape: pl.BlockSpec(shape, lambda p: (0,) * len(shape))
    column = lambda first: pl.BlockSpec((model, PAIR), lambda p: (0, first + p))
    moving = pl.BlockSpec((count, PAIR), lambda p: (0, p))
    return pl.pallas_call(
        functools.partial(bwd_kernel, experts),
        grid=(pairs,),
        out_shape=(
            jax.ShapeDtypeStruct((model, 4 * model + PAIR), LOW),
            jax.ShapeDtypeStruct((count, model), LOW),
        ),
        in_specs=[
            full((count, model)),
            full((count, model)),
            moving, moving, moving, moving,
            full((PAIR, count)),
            full((count, model)),
            full((count, model)),
            full((count, PAIR)),
            full((8, model)),
            column(0),
            column(pairs),
            column(2 * pairs),
            pl.BlockSpec((PAIR, model), lambda p: (p, 3)),
            pl.BlockSpec((model, PAIR), lambda p: (0, 4 * pairs)),
            full((count, 1)),
            full((1, count)),
            full((count, 1)),
            full((count, 2)),
            full((count, PAIR)),
            full((total_slots, model)),
            full((1, total_slots)),
            full((count, model)),
        ],
        out_specs=[full((model, 4 * model + PAIR)), full((count, model))],
        scratch_shapes=[
            pltpu.VMEM((count, count), F32),
            pltpu.VMEM((model, count), LOW),
            pltpu.VMEM((count, model), LOW),
            pltpu.VMEM((count, model), F32),
            pltpu.VMEM((count, model), F32),
            pltpu.VMEM((8, model), F32),
            pltpu.VMEM((count, model), F32),
            pltpu.VMEM((model, PAIR), F32),
        ],
        compiler_params=pltpu.CompilerParams(
            dimension_semantics=("arbitrary",), vmem_limit_bytes=VMEM_LIMIT
        ),
        cost_estimate=pl.CostEstimate(flops=14 * 10**9, bytes_accessed=25 * 10**6, transcendentals=4 * 10**6),
        name="attention_backward",
    )(
        tokens, normed, queries, keys, values, attended, lse_rows, middle, moe_low, probs, vecs,
        params, params, params, params, params,
        segment_ids.reshape(count, 1), segment_ids, patch_valid.reshape(count, 1), routes, slots,
        token_rows, gate_slots, cotangent,
    )


def gelu_and_slope(v):
    root = 0.7978845608028654
    cubic = 0.044715
    square = v * v
    bend = jnp.tanh(root * v * (1.0 + cubic * square))
    slope = 0.5 * (1.0 + bend) + 0.5 * v * (1.0 - bend * bend) * root * (1.0 + 3.0 * cubic * square)
    return 0.5 * v * (1.0 + bend), slope


def moe_kernel(
    dims, moe_low, slot_rows, slot_cols, gates, ups, b_in, b_out, w_in, w_out, *rest
):
    depth, across, rows, cores = dims
    wide = depth * across
    narrow = rows * cores
    side_out = rest[: rows - 1]
    rest = rest[rows - 1 :]
    token_rows, gate_slots, y_out, own_grad = rest[:4]
    side_grad = rest[4 : 3 + rows]
    own_extra = rest[3 + rows]
    side_extra = rest[4 + rows : 3 + 2 * rows]
    (
        full_in, full_out, x_send, x_here, g_send, g_here, dx_send, h_send, hidden, pre_grad, weighted,
        x_turned, w_turned, grad_send, grad_here, extra, extra_here,
        local, s_y, r_y, s_in, r_in, s_out, r_out, s_x, r_x, s_g, r_g, s_dx, r_dx, s_h, r_h, s_w, r_w, s_e, r_e,
    ) = rest[3 + 2 * rows :]
    z, x, y, c = place_of(dims)
    me, n = z * across + x, y * cores + c
    count, model = moe_low.shape
    capacity = x_send.shape[1]
    gate_width = g_send.shape[2]
    ff = full_in.shape[2]
    other = device_at(dims, z, x, y, 1 - c)

    def remote(src, dst, ssem, rsem, to):
        return pltpu.make_async_remote_copy(
            src_ref=src, dst_ref=dst, send_sem=ssem, recv_sem=rsem, device_id=to, device_id_type=MESH
        )

    along_y = [device_at(dims, z, x, (y + i) % rows, c) for i in range(1, rows)]
    greet([((me + d) % wide, n) for d in range(1, wide)] + [other] + along_y)

    ups_at = [((y - i) % rows) * cores + c for i in range(rows)]
    from_y, in_passes, out_loads, out_passes = [], [], [], []
    for i, h in enumerate(ups_at):
        if i:
            from_y.append(remote(w_in.at[0], full_in.at[n], s_y.at[i - 1], r_y.at[i - 1], along_y[i - 1]))
        src_out = w_out.at[0] if i == 0 else side_out[i - 1].at[0]
        out_loads.append(pltpu.make_async_copy(src_out, full_out.at[h], local.at[i]))
        out_passes.append(remote(src_out, full_out.at[h], s_out.at[i], r_out.at[i], other))
        src_in = w_in.at[0] if i == 0 else full_in.at[h]
        in_passes.append(remote(src_in, full_in.at[h], s_in.at[i], r_in.at[i], other))
    in_load = pltpu.make_async_copy(w_in.at[0], full_in.at[n], local.at[rows])
    for copy in from_y + out_loads + out_passes:
        copy.start()

    slot_a, slot_b = slot_cols[:, 0:1], slot_cols[:, 1:2]
    gate_a, gate_b = gates[:, 0:1], gates[:, 1:2]
    row_at = lax.broadcasted_iota(jnp.int32, (capacity, count), 0)
    lane_at = lax.broadcasted_iota(jnp.int32, (count, gate_width), 1)
    source = moe_low[...]

    def rows_for(expert):
        first = expert * capacity
        hit = (slot_rows[0:1] - first == row_at) | (slot_rows[1:2] - first == row_at)
        picked = dot(jnp.where(hit, 1.0, 0.0).astype(LOW), source).astype(LOW)
        inside = lane_at < capacity
        hit_a = (slot_a - first == lane_at) & inside
        hit_b = (slot_b - first == lane_at) & inside
        gate = jnp.where(hit_a, gate_a, 0.0) + jnp.where(hit_b, gate_b, 0.0)
        return picked, jnp.sum(gate, axis=0, keepdims=True)

    def x_copy(d, to):
        return remote(x_send.at[to], x_here.at[me], s_x.at[d], r_x.at[d], (to, n))

    def g_copy(d, to):
        return remote(g_send.at[to], g_here.at[me], s_g.at[d], r_g.at[d], (to, n))

    def dx_copy(d, to):
        return remote(dx_send.at[to], token_rows.at[me], s_dx.at[d], r_dx.at[d], (to, n))

    def h_copy(d, to):
        return remote(h_send.at[to], gate_slots.at[me], s_h.at[d], r_h.at[d], (to, n))

    def dispatch(k, carry):
        d = (k + wide // 2 - 1) % (wide - 1) + 1
        to = (me + d) % wide
        picked, gate = rows_for(to)
        x_send[to] = picked
        g_send[to] = gate
        x_copy(d, to).start()
        g_copy(d, to).start()
        return carry

    lax.fori_loop(0, wide - 1, dispatch, 0)
    in_load.start()
    in_passes[0].start()
    picked, gate = rows_for(me)
    x_here[me] = picked
    g_here[me] = gate
    extra[...] = jnp.zeros_like(extra)
    out_bias = b_out[...].astype(F32)
    for copy in out_loads:
        copy.wait()
    for copy in out_passes:
        copy.wait_recv()

    def backs(k, carry):
        two = pl.ds(2 * k, 2)
        up = ups[two].reshape(2 * capacity, model)
        for h in range(narrow):
            back = dot_nt(up, full_out[h]).astype(LOW)
            pre_grad[two, :, h * ff : (h + 1) * ff] = back.reshape(2, capacity, ff)
        return carry

    lax.fori_loop(0, wide // 2, backs, 0)
    for i in range(1, rows):
        from_y[i - 1].wait_recv()
        in_passes[i].start()
    in_load.wait()
    for copy in in_passes:
        copy.wait_recv()

    def expert(src):
        own = x_here[src]
        up = ups[src]
        gate = jnp.transpose(jnp.broadcast_to(g_here[src], (PAIR, gate_width)))[:capacity, 0:1]
        weigh = (gate * up.astype(F32)).astype(LOW)
        weighted[src] = weigh
        back_total = jnp.sum(up.astype(F32) * out_bias, axis=1, keepdims=True)
        dx = None
        for h in range(narrow):
            pre = dot(own, full_in[h]) + b_in[h]
            back = pre_grad[src, :, h * ff : (h + 1) * ff].astype(F32)
            value, slope = gelu_and_slope(pre)
            low = value.astype(LOW)
            hidden[src, :, h * ff : (h + 1) * ff] = low
            back_total += jnp.sum(low.astype(F32) * back, axis=1, keepdims=True)
            grad = (slope * (gate * back)).astype(LOW)
            pre_grad[src, :, h * ff : (h + 1) * ff] = grad
            extra[h, 0:1, :ff] += jnp.sum(grad.astype(F32), axis=0, keepdims=True)
            part = dot_nt(grad, full_in[h])
            dx = part if dx is None else dx + part
        dx_send[src] = dx.astype(LOW)
        spread = jnp.broadcast_to(back_total, (capacity, PAIR))
        spread = jnp.concatenate([spread, jnp.zeros((gate_width - capacity, PAIR), F32)], axis=0)
        h_send[src] = jnp.transpose(spread)[0:1]

    expert(me)
    keep_rows = pltpu.make_async_copy(dx_send.at[me], token_rows.at[me], local.at[rows + 1])
    keep_gate = pltpu.make_async_copy(h_send.at[me], gate_slots.at[me], local.at[rows + 2])
    keep_rows.start()
    keep_gate.start()

    def serve(k, carry):
        d = jnp.where(k % 2 == 0, k // 2 + 1, wide - (k + 1) // 2)
        src = (me - d + wide) % wide
        x_copy(d, src).wait_recv()
        g_copy(d, src).wait_recv()
        expert(src)
        dx_copy(d, src).start()
        h_copy(d, src).start()
        return carry

    lax.fori_loop(0, wide - 1, serve, 0)

    def outputs(src, carry):
        total = None
        for h in range(narrow):
            part = dot(hidden[src, :, h * ff : (h + 1) * ff], full_out[h])
            total = part if total is None else total + part
        x_send[src] = (total + out_bias).astype(LOW)
        return carry

    def sent(k, carry):
        to = (me + k + 1) % wide
        x_copy(k + 1, to).wait_send()
        g_copy(k + 1, to).wait_send()
        return carry

    lax.fori_loop(0, wide - 1, sent, 0)
    lax.fori_loop(0, wide, outputs, 0)
    keep_y = pltpu.make_async_copy(x_send, y_out, local.at[rows + 3])
    keep_y.start()

    all_rows = wide * capacity
    x_turned[...] = jnp.transpose(x_here[...].reshape(all_rows, model))
    w_turned[...] = jnp.transpose(weighted[...].reshape(all_rows, model))
    bias_grad = jnp.sum(weighted[...].reshape(all_rows, model).astype(F32), axis=0, keepdims=True)
    for h in range(narrow):
        extra[h, 1:2] = bias_grad

    def grad_of(h):
        lanes = pl.ds(pl.multiple_of(h * ff, PAIR), ff)
        grad_in = dot(x_turned[...], pre_grad[:, :, lanes].reshape(all_rows, ff))
        grad_out = dot(w_turned[...], hidden[:, :, lanes].reshape(all_rows, ff))
        return grad_in, grad_out

    swaps = []
    for i in range(rows):
        at = (y + i) % rows
        h = at * cores + 1 - c
        grad_in, grad_out = grad_of(h)
        grad_send[i, 0] = grad_in.astype(LOW)
        grad_send[i, 1] = grad_out.astype(LOW)
        swaps.append(remote(grad_send.at[i], grad_here.at[i], s_w.at[i], r_w.at[i], other))
        swaps.append(remote(extra.at[h], extra_here.at[i], s_e.at[i], r_e.at[i], other))
        swaps[-2].start()
        swaps[-1].start()
    keep_grads = []
    for i in range(rows):
        at = (y + i) % rows
        grad_in, grad_out = grad_of(at * cores + c)
        swaps[2 * i].wait_recv()
        swaps[2 * i + 1].wait_recv()
        target = own_grad if i == 0 else side_grad[i - 1]
        target_extra = own_extra if i == 0 else side_extra[i - 1]
        grad_here[i, 0] = (grad_in + grad_here[i, 0].astype(F32)).astype(LOW)
        grad_here[i, 1] = (grad_out + grad_here[i, 1].astype(F32)).astype(LOW)
        keep_grads.append(pltpu.make_async_copy(grad_here.at[i], target, local.at[rows + 4 + i]))
        keep_grads[-1].start()
        target_extra[...] = extra[at * cores + c] + extra_here[i]

    def finish(k, carry):
        d = k + 1
        back = (me - d + wide) % wide
        dx_copy(d, back).wait_recv()
        h_copy(d, back).wait_recv()
        dx_copy(d, back).wait_send()
        h_copy(d, back).wait_send()
        return carry

    lax.fori_loop(0, wide - 1, finish, 0)
    for copy in from_y + in_passes + out_passes + swaps:
        copy.wait_send()
    for copy in [keep_rows, keep_gate, keep_y] + keep_grads:
        copy.wait()


def moe_stage(dims, capacity, moe_low, slot_rows, slots, gates, ups, b_in, b_out, w_in, w_out, side_out):
    depth, across, rows, cores = dims
    wide, narrow = depth * across, rows * cores
    count, model = moe_low.shape
    ff = w_in.shape[2]
    gate_width = -(-capacity // PAIR) * PAIR
    any_, vmem = pl.BlockSpec(memory_space=pl.ANY), pl.BlockSpec(memory_space=pltpu.VMEM)
    low = lambda *shape: jax.ShapeDtypeStruct(shape, LOW)
    f32 = lambda *shape: jax.ShapeDtypeStruct(shape, F32)
    sem = lambda size: [pltpu.SemaphoreType.DMA((size,))] * 2
    outs = pl.pallas_call(
        functools.partial(moe_kernel, dims),
        out_shape=(
            low(wide, capacity, model), f32(wide, 1, gate_width), low(wide, capacity, model),
            *[low(2, model, ff)] * rows, *[f32(8, model)] * rows,
        ),
        in_specs=[vmem] * 7 + [any_] * (1 + rows),
        out_specs=[any_] * (3 + rows) + [vmem] * rows,
        scratch_shapes=[
            pltpu.VMEM((narrow, model, ff), LOW),
            pltpu.VMEM((narrow, ff, model), LOW),
            pltpu.VMEM((wide, capacity, model), LOW),
            pltpu.VMEM((wide, capacity, model), LOW),
            pltpu.VMEM((wide, 1, gate_width), F32),
            pltpu.VMEM((wide, 1, gate_width), F32),
            pltpu.VMEM((wide, capacity, model), LOW),
            pltpu.VMEM((wide, 1, gate_width), F32),
            pltpu.VMEM((wide, capacity, narrow * ff), LOW),
            pltpu.VMEM((wide, capacity, narrow * ff), LOW),
            pltpu.VMEM((wide, capacity, model), LOW),
            pltpu.VMEM((model, wide * capacity), LOW),
            pltpu.VMEM((model, wide * capacity), LOW),
            pltpu.VMEM((rows, 2, model, ff), LOW),
            pltpu.VMEM((rows, 2, model, ff), LOW),
            pltpu.VMEM((narrow, 8, model), F32),
            pltpu.VMEM((rows, 8, model), F32),
            pltpu.SemaphoreType.DMA((2 * rows + 4,)),
            *sem(rows), *sem(rows), *sem(rows), *sem(wide), *sem(wide), *sem(wide), *sem(wide), *sem(rows), *sem(rows),
        ],
        compiler_params=pltpu.CompilerParams(
            collective_id=2, has_side_effects=True, vmem_limit_bytes=60 * 1024 * 1024
        ),
        cost_estimate=pl.CostEstimate(flops=36 * 10**9, bytes_accessed=25 * 10**6, transcendentals=4 * 10**6),
        name="moe_stage",
    )(moe_low, slot_rows, slots, gates, ups, b_in, b_out, w_in, w_out, *side_out)
    return outs[:3], outs[3 : 3 + rows], outs[3 + rows :]


def per_device(
    dims,
    tokens, segment_ids, patch_valid, routes, priority, gain_attn, shift_attn, w_qkv, query_bias, value_bias,
    w_proj, proj_bias, gain_moe, shift_moe, w_router, w_in, in_bias, w_out, out_bias, cotangent,
):
    count, model = tokens.shape
    experts = w_router.shape[1]
    capacity = (210 * count + 100 * experts - 1) // (100 * experts)
    shard_rows = gain_attn.shape[0]
    vectors = jnp.stack(
        [gain_attn, shift_attn, query_bias, value_bias, proj_bias, gain_moe, shift_moe], axis=1
    )
    pack = jnp.concatenate(
        [w_qkv, w_proj, w_router, vectors, jnp.zeros((shard_rows, PAIR - 7 - experts), LOW)], axis=1
    )
    depth, across, rows, cores = dims
    stride = -(-capacity // 16) * 16
    gathered = shard_rows % 8 != 0
    if gathered:
        pack = lax.all_gather(pack, ("wide", "narrow"), axis=0, tiled=True)
    params, saved, (slots, slot_rows, ups, full_b_in), side_out = front_stage(
        dims, experts, capacity, stride, gathered, pack, tokens, segment_ids, patch_valid, routes, priority,
        cotangent, w_out, in_bias.astype(F32),
    )
    normed, queries, keys, values, attended, lse_rows, middle, moe_low, probs, gates, vecs = saved
    (token_rows, gate_slots, y), weight_grads, extras = moe_stage(
        dims, stride, moe_low, slot_rows, slots, gates, ups, full_b_in, out_bias, w_in, w_out, side_out
    )
    swap = functools.partial(lax.all_to_all, axis_name="wide", split_axis=0, concat_axis=0, tiled=True)
    steps = [
        [(y * cores + c, (y + d) % rows * cores + c) for y in range(rows) for c in range(cores)]
        for d in range(1, rows)
    ]
    slot_ids = jnp.arange(experts * stride, dtype=jnp.int32)
    hit_a = slots[:, 0:1] == slot_ids
    hit_b = slots[:, 1:2] == slot_ids
    returned = swap(y).reshape(-1, model)
    pair_grad = weight_grads[0].astype(F32)
    bias_rows = extras[0]
    for step, grad, extra in zip(steps, weight_grads[1:], extras[1:]):
        pair_grad = pair_grad + lax.ppermute(grad, "narrow", step).astype(F32)
        bias_rows = bias_rows + lax.ppermute(extra, "narrow", step)

    grads, tokens_grad = attention_backward(
        experts, tokens,
        (normed, queries, keys, values, attended, lse_rows, middle, moe_low, probs, vecs),
        params, segment_ids, patch_valid, routes, slots, token_rows.reshape(-1, model),
        gate_slots[:, 0, :stride].reshape(1, -1), cotangent,
    )
    shares = scatter_grads(dims, grads)

    picked_a, picked_b = dot(hit_a.astype(LOW), returned), dot(hit_b.astype(LOW), returned)
    block_out = (middle + gates[:, 0:1] * picked_a + gates[:, 1:2] * picked_b).astype(LOW)

    at = 4 * model + experts
    vector = lambda i: shares[:, at + i]
    return (
        block_out,
        tokens_grad,
        vector(0),
        vector(1),
        shares[:, : 3 * model],
        vector(2),
        vector(3),
        shares[:, 3 * model : 4 * model],
        vector(4),
        vector(5),
        vector(6),
        shares[:, 4 * model : at],
        pair_grad[0][None],
        bias_rows[0:1, : w_in.shape[2]],
        jnp.transpose(pair_grad[1])[None],
        bias_rows[1:2],
    )


def solution(mesh):
    dims = grid_of(mesh.shape["wide"], mesh.shape["narrow"])
    every = ("wide", "narrow")
    rows, vector = P(every, None), P(every)
    return jax.shard_map(
        functools.partial(per_device, dims),
        mesh=mesh,
        in_specs=(
            rows, rows, rows, rows, rows, vector, vector, rows, vector, vector, rows, vector, vector, vector,
            rows, P("wide", None, "narrow"), P("wide", "narrow"), P("wide", "narrow", None), P("wide", None), rows,
        ),
        out_specs=(
            rows, rows, vector, vector, rows, vector, vector, rows, vector, vector, vector, rows,
            P("wide", None, "narrow"), P("wide", "narrow"), P("wide", "narrow", None), P("wide", None),
        ),
        check_vma=False,
    )
```

```python
import functools

import jax
import jax.numpy as jnp
from jax import lax
from jax.experimental import pallas as pl
from jax.experimental.pallas import tpu as pltpu
from jax.sharding import PartitionSpec as P

HEAD = 64
PAIR = 2 * HEAD
EPSILON = 1e-06
MASKED = -1000000000.0
MESH = pl.DeviceIdType.MESH
LOW = jnp.bfloat16
F32 = jnp.float32
PIECES = 8
VMEM_LIMIT = 58 * 1024 * 1024


def dot(a, b):
    return jnp.dot(a, b, preferred_element_type=F32)


def dot_nt(a, b):
    return lax.dot_general(a, b, (((1,), (1,)), ((), ())), preferred_element_type=F32)


def dot_tn(a, b):
    return lax.dot_general(a, b, (((0,), (0,)), ((), ())), preferred_element_type=F32)


def grid_of(wide, narrow):
    along_x = 1 << ((wide.bit_length() - 1) // 2)
    return wide // along_x, along_x, narrow // 2, 2


def place_of(dims):
    depth, across, rows, cores = dims
    wide, narrow = lax.axis_index("wide"), lax.axis_index("narrow")
    return wide // across, wide % across, narrow // cores, narrow % cores


def device_at(dims, z, x, y, c):
    depth, across, rows, cores = dims
    return (z * across + x, y * cores + c)


def greet(peers):
    barrier = pltpu.get_barrier_semaphore()
    for peer in peers:
        pl.semaphore_signal(barrier, inc=1, device_id=peer, device_id_type=MESH)
    pl.semaphore_wait(barrier, len(peers))


def neighbours(dims):
    depth, across, rows, cores = dims
    z, x, y, c = place_of(dims)
    peers = [device_at(dims, (z + d) % depth, x, y, c) for d in range(1, depth)]
    peers += [device_at(dims, z, (x + d) % across, y, c) for d in range(1, across)]
    peers += [device_at(dims, z, x, (y + d) % rows, c) for d in range(1, rows)]
    peers += [device_at(dims, z, x, y, 1 - c)]
    return peers


def norm_parts(values):
    center = jnp.mean(values, axis=-1, keepdims=True)
    offset = values - center
    spread = jnp.mean(offset * offset, axis=-1, keepdims=True)
    scale = lax.rsqrt(spread + EPSILON)
    return offset * scale, scale


def column_of(row):
    return jnp.transpose(jnp.broadcast_to(row, (PAIR, row.shape[1])))[:, 0:1]


def front_kernel(
    dims, experts, capacity, gathered, heads, *rest
):
    depth, across, rows, cores = dims
    wide, narrow = depth * across, rows * cores
    pack_refs, rest = rest[:heads], rest[heads:]
    tokens, seg_row, valid_row, routes, priority, cotangent, w_out, b_in = rest[:8]
    rest = rest[8:]
    (
        params, normed_t, q_out, k_out, v_out, attended_t, lse_rows, middle, moe_low, moe_low_t, probs_out, gates_out, vecs,
        bias_t, slots_out, slot_rows, full_b_in, ups,
    ) = rest[:18]
    side_out = rest[18 : 17 + rows]
    (
        normed, attended, total, bias, lse, up_send, b_send, shard, turn, blank,
        s1, r1, sx, rx, sy, ry, sa, ra, sb, rb, sc, rc, s_up, r_up, s_w, r_w, s_b, r_b, local, blanks,
    ) = rest[17 + rows :]
    z, x, y, c = place_of(dims)
    me, n = z * across + x, y * cores + c
    count, model = tokens.shape
    stride = ups.shape[1]
    lanes = lax.broadcasted_iota(jnp.int32, (count, PAIR), 1)

    def remote(src, dst, ssem, rsem, to):
        return pltpu.make_async_remote_copy(
            src_ref=src, dst_ref=dst, send_sem=ssem, recv_sem=rsem, device_id=to, device_id_type=MESH
        )

    def send(src, dst, ssem, rsem, to):
        copy = remote(src, dst, ssem, rsem, to)
        copy.start()
        return copy

    if not gathered:
        w_qkv, w_proj, router_t, vectors = pack_refs
        packs = [
            pltpu.make_async_copy(w_qkv, shard.at[:, pl.ds(0, 3 * model)], local.at[3]),
            pltpu.make_async_copy(w_proj, shard.at[:, pl.ds(3 * model, model)], local.at[4]),
        ]
        for copy in packs:
            copy.start()
        height = shard.shape[0]
        turn[...] = jnp.zeros_like(turn)
        turn[0:experts, 0:height] = router_t[...].astype(F32)
        turn[experts : experts + 7, 0:height] = vectors[...].astype(F32)
        shard[:, 4 * model : 4 * model + PAIR] = jnp.transpose(turn[...])[0:height].astype(LOW)
    b_send[...] = b_in[...].astype(F32)
    peers = [((me + d) % wide, n) for d in range(1, wide)]
    peers += [(me, (n + d) % narrow) for d in range(1, narrow)]
    greet(peers)
    if not gathered:
        for copy in packs:
            copy.wait()

    first, by_x, by_y, half_a, half_b, by_core = {}, {}, {}, {}, {}, {}
    keeps = []
    if not gathered:
        width = shard.shape[1]
        cut = (width // 256) * 128

        def block(dz, dx, dy, core):
            at = ((z - dz) % depth) * across + (x - dx) % across
            return params.at[(at * rows + (y - dy) % rows) * cores + core]

        own = block(0, 0, 0, c)
        keeps.append(pltpu.make_async_copy(shard, own, local.at[0]))
        keeps[-1].start()
        for dz in range(1, depth):
            first[dz] = send(
                shard, own, s1.at[dz - 1], r1.at[dz - 1], device_at(dims, (z + dz) % depth, x, y, c)
            )

    def to_core(dz, dx, dy):
        at = (dz * across + dx) * rows + dy
        src = shard if (dz, dx, dy) == (0, 0, 0) else block(dz, dx, dy, c)
        by_core[at] = send(
            src, block(dz, dx, dy, c), sc.at[at], rc.at[at], device_at(dims, z, x, y, 1 - c)
        )

    def spread(dz):
        if dz:
            first[dz].wait_recv()
        src = block(dz, 0, 0, c) if dz else shard
        for dx in range(1, across):
            at = dz * (across - 1) + dx - 1
            by_x[dz, dx] = send(
                src, block(dz, 0, 0, c), sx.at[at], rx.at[at],
                device_at(dims, z, (x + dx) % across, y, c),
            )
        for dy in range(1, rows):
            at = dz * (rows - 1) + dy - 1
            by_y[dz, dy] = send(
                src, block(dz, 0, 0, c), sy.at[at], ry.at[at],
                device_at(dims, z, x, (y + dy) % rows, c),
            )
        to_core(dz, 0, 0)

    def corner(dz):
        for dx in range(1, across):
            by_x[dz, dx].wait_recv()
            part = block(dz, dx, 0, c).at[:, pl.ds(0, cut)]
            for dy in range(1, rows):
                at = (dz * (across - 1) + dx - 1) * (rows - 1) + dy - 1
                half_a[dz, dx, dy] = send(
                    part, part, sa.at[at], ra.at[at], device_at(dims, z, x, (y + dy) % rows, c)
                )
            to_core(dz, dx, 0)
        for dy in range(1, rows):
            by_y[dz, dy].wait_recv()
            part = block(dz, 0, dy, c).at[:, pl.ds(cut, width - cut)]
            for dx in range(1, across):
                at = (dz * (across - 1) + dx - 1) * (rows - 1) + dy - 1
                half_b[dz, dx, dy] = send(
                    part, part, sb.at[at], rb.at[at], device_at(dims, z, (x + dx) % across, y, c)
                )
            to_core(dz, 0, dy)

    def finish(dz):
        for dx in range(1, across):
            for dy in range(1, rows):
                half_a[dz, dx, dy].wait_recv()
                half_b[dz, dx, dy].wait_recv()
                to_core(dz, dx, dy)

    if not gathered:
        spread(0)
    b_copies = []
    for d in range(1, narrow):
        b_copies.append(send(b_send, full_b_in.at[n], s_b.at[d], r_b.at[d], (me, (n + d) % narrow)))
    keeps.append(pltpu.make_async_copy(b_send, full_b_in.at[n], local.at[1]))
    keeps[-1].start()
    w_copies = []

    piece = w_out.shape[1] // PIECES

    def weight_piece(i):
        for dy in range(1, rows):
            at = (dy - 1) * PIECES + i
            part = pl.ds(i * piece, piece)
            to = device_at(dims, z, x, (y + dy) % rows, c)
            w_copies.append(send(w_out.at[:, part], side_out[dy - 1].at[:, part], s_w.at[at], r_w.at[at], to))

    used = -(-capacity // 8) * 8
    fills = []
    if used < stride:
        blank[...] = jnp.zeros_like(blank)
        for w in range(wide):
            fills.append(pltpu.make_async_copy(blank, ups.at[w, pl.ds(used, stride - used)], blanks.at[w]))
            fills[-1].start()

    half = PAIR // 2
    valid = valid_row[...].astype(F32)
    valid_col = column_of(valid)
    rank_row = priority[...].astype(F32)
    ahead = jnp.where(rank_row < column_of(rank_row), 1.0, 0.0).astype(LOW)
    first_at = column_of(routes[0:1].astype(F32)).astype(jnp.int32)
    second_at = column_of(routes[1:2].astype(F32)).astype(jnp.int32)
    hit_first, hit_second = lanes == first_at, lanes == second_at + half
    hot = jnp.where(hit_first | hit_second, valid_col, 0.0)
    earlier = dot(ahead, hot.astype(LOW))
    filled = pltpu.roll(jnp.sum(hot, axis=0, keepdims=True), half, 1)
    filled = jnp.broadcast_to(jnp.where(lanes[0:1] >= half, filled, 0.0), (8, PAIR))[0:1]
    earlier = earlier + filled
    place_a = jnp.sum(jnp.where(hit_first, earlier, 0.0), axis=1, keepdims=True).astype(jnp.int32)
    place_b = jnp.sum(jnp.where(hit_second, earlier, 0.0), axis=1, keepdims=True).astype(jnp.int32)
    kept_a = (place_a < capacity) & (valid_col > 0.5)
    kept_b = (place_b < capacity) & (valid_col > 0.5)
    slot_a = jnp.where(kept_a, first_at * stride + place_a, -1)
    slot_b = jnp.where(kept_b, second_at * stride + place_b, -1)
    slots = jnp.where(lanes == 0, slot_a, slot_b)
    slots_out[...] = jnp.where(lanes < 2, slots, jnp.where(lanes == 2, first_at, second_at))
    slot_rows[...] = jnp.transpose(slots.astype(F32))[0:8].astype(jnp.int32)

    segments = seg_row[...].astype(F32)
    keys_at = lax.broadcasted_iota(jnp.int32, (count, count), 1)
    rows_at = lax.broadcasted_iota(jnp.int32, (count, count), 0)
    allowed = (column_of(segments) == segments) & ((valid > 0.5) | (keys_at == rows_at))
    bias[...] = jnp.where(allowed, 0.0, MASKED)
    xhat, _ = norm_parts(tokens[...].astype(F32))
    total[...] = xhat
    lse[...] = jnp.zeros_like(lse)

    row_at = lax.broadcasted_iota(jnp.int32, (stride, count), 0)

    def up_copy(d, to):
        body = pl.ds(0, used)
        return remote(up_send.at[to, body], ups.at[me, body], s_up.at[d], r_up.at[d], (to, n))

    def rows_for(expert):
        start = expert * stride
        hit = (slot_rows[0:1] - start == row_at) | (slot_rows[1:2] - start == row_at)
        return dot(jnp.where(hit, 1.0, 0.0).astype(LOW), cotangent[...]).astype(LOW)

    def dispatch(k, carry):
        d = (k + wide // 2 - 1) % (wide - 1) + 1
        to = (me + d) % wide
        up_send[to] = rows_for(to)
        up_copy(d, to).start()
        return carry

    if not gathered:
        for step in range(1, depth):
            spread(step)
            corner(step - 1)
            if step >= 2:
                finish(step - 2)
        lax.fori_loop(0, (wide - 1) // 2, dispatch, 0)
        corner(depth - 1)
        finish(depth - 2)
        lax.fori_loop((wide - 1) // 2, wide - 1, dispatch, 0)
        finish(depth - 1)
    else:
        lax.fori_loop(0, wide - 1, dispatch, 0)
        keeps.append(pltpu.make_async_copy(pack_refs[0], params, local.at[0]))
        keeps[-1].start()
    for i in range(PIECES):
        weight_piece(i)
    bias_t[...] = jnp.where(
        (column_of(segments) == segments) & ((valid_col > 0.5) | (keys_at == rows_at)), 0.0, MASKED
    )
    up_send[me] = rows_for(me)
    body = pl.ds(0, used)
    keep_up = pltpu.make_async_copy(up_send.at[me, body], ups.at[me, body], local.at[2])
    keep_up.start()
    for copy in by_core.values():
        copy.wait_recv()
    for copy in keeps:
        copy.wait()


    def columns(at):
        return params[:, at] if gathered else params[:, :, at].reshape(model, PAIR)

    small = columns(pl.ds(4 * model, PAIR))
    vecs[...] = jnp.transpose(small.astype(F32))[experts : experts + 8]
    normed[...] = (total[...] * vecs[0:1] + vecs[1:2]).astype(LOW)

    def attend(pair, carry):
        at = lambda which: pl.ds(pl.multiple_of(which * model + pair * PAIR, PAIR), PAIR)
        here = at(0)
        source = normed[...]
        queries = (dot(source, columns(at(0))) + vecs[2:3, here]).astype(LOW) * LOW(HEAD**-0.5)
        keys = dot(source, columns(at(1))).astype(LOW)
        values = (dot(source, columns(at(2))) + vecs[3:4, here]).astype(LOW)
        q_out[:, here] = queries
        k_out[:, here] = keys
        v_out[:, here] = values
        mixed = None
        for part in range(2):
            side = (lanes < HEAD) if part == 0 else (lanes >= HEAD)
            own_keys = jnp.where(side, keys, LOW(0))
            own_values = jnp.where(side, values, LOW(0))
            scores = dot_nt(queries, own_keys) + bias[...]
            peak = jnp.max(scores, axis=1, keepdims=True)
            raised = jnp.exp(scores - peak)
            row_total = jnp.sum(raised, axis=1, keepdims=True)
            attn = (raised * (1.0 / row_total)).astype(LOW)
            piece = dot(attn, own_values)
            mixed = piece if mixed is None else mixed + piece
            lse[...] = jnp.where(lanes == 2 * pair + part, peak + jnp.log(row_total), lse[...])
        mixed = mixed.astype(LOW)
        attended[:, here] = mixed
        return carry

    lax.fori_loop(0, model // PAIR, attend, 0)

    def project(pair, carry):
        here = pl.ds(pl.multiple_of(pair * PAIR, PAIR), PAIR)
        there = pl.ds(pl.multiple_of(3 * model + pair * PAIR, PAIR), PAIR)
        total[:, here] = dot(attended[...], columns(there))
        return carry

    lax.fori_loop(0, model // PAIR, project, 0)
    lse_rows[...] = jnp.transpose(lse[...])
    normed_t[...] = jnp.transpose(normed[...])
    attended_t[...] = jnp.transpose(attended[...])
    mid = tokens[...].astype(F32) + (total[...] + vecs[4:5])
    middle[...] = mid
    xhat, _ = norm_parts(mid)
    low = (xhat * vecs[5:6] + vecs[6:7]).astype(LOW)
    moe_low[...] = low
    moe_low_t[...] = jnp.transpose(low)
    logits = jnp.where(lanes < experts, dot(low, columns(pl.ds(4 * model, PAIR))), -jnp.inf)
    raised = jnp.exp(logits - jnp.max(logits, axis=1, keepdims=True))
    probs = raised / jnp.sum(raised, axis=1, keepdims=True)
    probs_out[...] = probs
    gate_a = jnp.sum(jnp.where(lanes == first_at, probs, 0.0), axis=1, keepdims=True)
    gate_b = jnp.sum(jnp.where(lanes == second_at, probs, 0.0), axis=1, keepdims=True)
    gates_out[...] = jnp.where(lanes == 0, gate_a, gate_b)

    def settle(k, carry):
        d = k + 1
        up_copy(d, (me + d) % wide).wait_send()
        up_copy(d, (me - d + wide) % wide).wait_recv()
        return carry

    lax.fori_loop(0, wide - 1, settle, 0)
    keep_up.wait()
    for copy in w_copies + b_copies + fills:
        copy.wait()
    for group in (first, by_x, by_y, half_a, half_b, by_core):
        for copy in group.values():
            copy.wait_send()


def front_stage(
    dims, experts, capacity, stride, gathered, pack, tokens, segment_ids, patch_valid, routes, priority,
    cotangent, w_out, in_bias,
):
    depth, across, rows, cores = dims
    wide, narrow = depth * across, rows * cores
    count, model = tokens.shape
    used = -(-capacity // 8) * 8
    any_, vmem = pl.BlockSpec(memory_space=pl.ANY), pl.BlockSpec(memory_space=pltpu.VMEM)
    low = lambda *shape: jax.ShapeDtypeStruct(shape, LOW)
    f32 = lambda *shape: jax.ShapeDtypeStruct(shape, F32)
    i32 = lambda *shape: jax.ShapeDtypeStruct(shape, jnp.int32)
    width = 4 * model + PAIR
    height = model if gathered else pack[0].shape[0]
    full = (height, width) if gathered else (wide * narrow, height, width)
    packed = 1 if gathered else height
    corners = depth * (across - 1) * (rows - 1)
    sems = []
    for size in (
        depth - 1, depth * (across - 1), depth * (rows - 1), corners, corners, depth * across * rows,
        wide, (rows - 1) * PIECES, narrow,
    ):
        sems += [pltpu.SemaphoreType.DMA((size,))] * 2
    outs = pl.pallas_call(
        functools.partial(front_kernel, dims, experts, capacity, gathered, len(pack)),
        out_shape=(
            low(*full), low(model, count), low(count, model), low(count, model), low(count, model),
            low(model, count), f32(PAIR, count), f32(count, model), low(count, model), low(model, count),
            f32(count, PAIR), f32(count, PAIR), f32(8, model), f32(count, count), i32(count, PAIR), i32(8, count),
            f32(narrow, 1, in_bias.shape[1]), low(wide, stride, model), *[low(*w_out.shape)] * (rows - 1),
        ),
        in_specs=([any_] if gathered else [any_, any_, vmem, vmem]) + [vmem] * 6 + [any_, vmem],
        out_specs=[vmem] * 17 + [any_] * rows,
        scratch_shapes=[
            pltpu.VMEM((count, model), LOW),
            pltpu.VMEM((count, model), LOW),
            pltpu.VMEM((count, model), F32),
            pltpu.VMEM((count, count), F32),
            pltpu.VMEM((count, PAIR), F32),
            pltpu.VMEM((wide, stride, model), LOW),
            pltpu.VMEM((1, in_bias.shape[1]), F32),
            pltpu.VMEM((packed, width), LOW),
            pltpu.VMEM((PAIR, PAIR), F32),
            pltpu.VMEM((max(stride - used, 8), model), LOW),
            *sems,
            pltpu.SemaphoreType.DMA((5,)),
            pltpu.SemaphoreType.DMA((wide,)),
        ],
        compiler_params=pltpu.CompilerParams(
            collective_id=0, has_side_effects=True, vmem_limit_bytes=VMEM_LIMIT
        ),
        cost_estimate=pl.CostEstimate(flops=7 * 10**9, bytes_accessed=20 * 10**6, transcendentals=4 * 10**6),
        name="front_stage",
    )(*pack, tokens, segment_ids, patch_valid, jnp.transpose(routes), priority, cotangent, w_out, in_bias)
    params = outs[0] if gathered else outs[0].reshape(wide * narrow * height, width)
    return params, outs[1:14], outs[14:18], outs[18:]


def norm_back(grad, gain, xhat, scale):
    scaled = grad * gain
    mean_a = jnp.mean(scaled, axis=-1, keepdims=True)
    mean_b = jnp.mean(scaled * xhat, axis=-1, keepdims=True)
    return scale * (scaled - mean_a - xhat * mean_b)


def back_kernel(dims, used, experts, gathered, *rest):
    depth, across, rows, cores = dims
    wide, narrow = depth * across, rows * cores
    (
        tokens, normed_t, queries, keys, values, attended_t, lse_rows, middle, _, moe_low_t, probs, gates, vecs, bias,
        weights, slots, token_rows, gate_slots, cotangent, y_rows,
    ) = rest[:20]
    side_grad = rest[20 : 19 + rows]
    rest = rest[19 + rows :]
    if gathered:
        block_out, tokens_grad, grad_here, group = rest[:4]
        rest = rest[4:]
    else:
        block_out, tokens_grad, grad_here, out_qkv, out_proj, out_router, *out_vecs = rest[:13]
        group, n1, n2, n3, n4 = rest[13:18]
        rest = rest[18:]
    branch, middle_grad, total, sums, router, parts, y_here = rest[:7]
    s_y, q_y, s_g, q_g, local = rest[7:12]
    z, x, y, c = place_of(dims)
    me, n = z * across + x, y * cores + c
    count, model = tokens.shape
    stride = y_here.shape[1]
    pairs = model // PAIR
    per = 3 * PAIR
    n_proj = model // per
    small_at = n_proj + pairs
    lanes = lax.broadcasted_iota(jnp.int32, (count, PAIR), 1)

    def remote(src, dst, ssem, rsem, to):
        return pltpu.make_async_remote_copy(
            src_ref=src, dst_ref=dst, send_sem=ssem, recv_sem=rsem, device_id=to, device_id_type=MESH
        )

    peers = [((me + d) % wide, n) for d in range(1, wide)]
    peers += [device_at(dims, z, x, (y + d) % rows, c) for d in range(1, rows)]
    peers += [device_at(dims, z, x, y, 1 - c)]
    body = pl.ds(0, used)
    if used < stride:
        y_here[:, used:stride] = jnp.zeros((wide, stride - used, model), LOW)
    greet(peers)

    def y_copy(d, to):
        return remote(y_rows.at[to, body], y_here.at[me, body], s_y.at[d], q_y.at[d], (to, n))

    def give(k, carry):
        d = (k + wide // 2 - 1) % (wide - 1) + 1
        y_copy(d, (me + d) % wide).start()
        return carry

    lax.fori_loop(0, wide - 1 - pairs, give, 0)
    keep_y = pltpu.make_async_copy(y_rows.at[me, body], y_here.at[me, body], local.at[0])
    keep_y.start()
    piece = grad_here.shape[2] // PIECES

    def g_copies(i):
        copies = []
        for dy in range(1, rows):
            at = (dy - 1) * PIECES + i
            part = pl.ds(i * piece, piece)
            to = device_at(dims, z, x, (y + dy) % rows, c)
            copies.append(remote(side_grad[dy - 1].at[:, part], grad_here.at[dy - 1, :, part], s_g.at[at], q_g.at[at], to))
        return copies

    def give_grad(i):
        for copy in g_copies(i):
            copy.start()

    for i in range(PIECES - pairs):
        give_grad(i)

    if not gathered:
        s1, q1, s2, q2, s3, q3, s4, q4 = rest[12:20]
        height = group.shape[-2]

    def put(g, third, value):
        at = pl.ds(third * PAIR, PAIR)
        value = value.astype(LOW)
        if gathered:
            group[g, :, at] = value
        else:
            group[g, :, :, :, :, :, at] = value.reshape(depth, across, rows, cores, height, PAIR)

    def span(g):
        return pl.ds(0, PAIR) if isinstance(g, int) and g == small_at else pl.ds(0, per)

    def hop_core(g):
        return remote(
            group.at[g, :, :, :, 1 - c, :, span(g)], n1.at[g, :, :, :, :, span(g)], s1.at[g], q1.at[g],
            device_at(dims, z, x, y, 1 - c),
        )

    def hop_x(g, dx):
        at = g * (across - 1) + dx - 1
        return remote(
            n1.at[g, :, (x + dx) % across, :, :, span(g)], n2.at[at, :, :, :, span(g)],
            s2.at[at], q2.at[at], device_at(dims, z, (x + dx) % across, y, c),
        )

    def hop_y(g, dy):
        at = g * (rows - 1) + dy - 1
        return remote(
            n2.at[g * (across - 1), :, (y + dy) % rows, :, span(g)], n3.at[at, :, :, span(g)],
            s3.at[at], q3.at[at], device_at(dims, z, x, (y + dy) % rows, c),
        )

    def hop_z(g, dz):
        at = g * (depth - 1) + dz - 1
        return remote(
            n3.at[g * (rows - 1), (z + dz) % depth, :, span(g)], n4.at[at, :, span(g)],
            s4.at[at], q4.at[at], device_at(dims, (z + dz) % depth, x, y, c),
        )

    def start(g):
        if not gathered:
            hop_core(g).start()

    def begin(g):
        if gathered:
            return
        hop_core(g).wait_recv()
        w = span(g)
        n1[g, :, :, :, :, w] = (
            group[g, :, :, :, c, :, w].astype(F32) + n1[g, :, :, :, :, w].astype(F32)
        ).astype(LOW)
        for dx in range(1, across):
            hop_x(g, dx).start()

    def middle_of(g):
        if gathered:
            return
        w = span(g)
        at = g * (across - 1)
        acc = n1[g, :, x, :, :, w].astype(F32)
        for dx in range(1, across):
            hop_x(g, dx).wait_recv()
            acc = acc + n2[at + dx - 1, :, :, :, w].astype(F32)
        n2[at, :, :, :, w] = acc.astype(LOW)
        for dy in range(1, rows):
            hop_y(g, dy).start()

    def end(g):
        if gathered:
            return
        w = span(g)
        at = g * (rows - 1)
        for dy in range(1, rows):
            hop_y(g, dy).wait_recv()
        acc = n2[g * (across - 1), :, y, :, w].astype(F32)
        for dy in range(1, rows):
            acc = acc + n3[at + dy - 1, :, :, w].astype(F32)
        n3[at, :, :, w] = acc.astype(LOW)
        for dz in range(1, depth):
            hop_z(g, dz).start()

    def last(g):
        w = span(g)
        acc = n3[g * (rows - 1), z, :, w].astype(F32)
        for dz in range(1, depth):
            hop_z(g, dz).wait_recv()
            acc = acc + n4[g * (depth - 1) + dz - 1, :, w].astype(F32)
        return acc

    total[...] = jnp.zeros_like(total)
    sums[...] = jnp.zeros_like(sums)
    slot_a, slot_b = slots[:, 0:1], slots[:, 1:2]
    slot_at = lax.broadcasted_iota(jnp.int32, (count, wide * stride), 1)
    third = PAIR // 4
    lane_at = lax.broadcasted_iota(jnp.int32, (stride, PAIR), 1)

    def split(w, carry):
        value = column_of(gate_slots[w])[0:stride]
        high = value.astype(LOW).astype(F32)
        mid = (value - high).astype(LOW).astype(F32)
        low = value - high - mid
        row = jnp.where(lane_at == w, high, 0.0) + jnp.where(lane_at == third + w, mid, 0.0)
        parts[w] = (row + jnp.where(lane_at == 2 * third + w, low, 0.0)).astype(LOW)
        return carry

    lax.fori_loop(0, wide, split, 0)
    picks = jnp.where((slot_at == slot_a) | (slot_at == slot_b), 1.0, 0.0).astype(LOW)
    picked = dot(picks, parts[...].reshape(wide * stride, PAIR))
    prob_grad = picked + pltpu.roll(picked, PAIR - third, 1) + pltpu.roll(picked, PAIR - 2 * third, 1)
    own = probs[...]
    prob_grad = jnp.where(lanes < experts, prob_grad, 0.0)
    logit_grad = (own * (prob_grad - jnp.sum(prob_grad * own, axis=1, keepdims=True))).astype(LOW)
    router[...] = dot(moe_low_t[...], logit_grad)
    moe_grad = dot(picks, token_rows[...].reshape(wide * stride, model)) + dot_nt(
        logit_grad, weights[:, 4 * model : 4 * model + PAIR]
    )
    xhat, scale = norm_parts(middle[...])
    sums[5:6] = jnp.sum(moe_grad * xhat, axis=0, keepdims=True)
    sums[6:7] = jnp.sum(moe_grad, axis=0, keepdims=True)
    mid = cotangent[...].astype(F32) + norm_back(moe_grad, vecs[5:6], xhat, scale)
    middle_grad[...] = mid
    branch[...] = mid.astype(LOW)
    sums[4:5] = jnp.sum(branch[...].astype(F32), axis=0, keepdims=True)
    for g in range(n_proj):
        for third_at in range(3):
            at = (g * 3 + third_at) * PAIR
            put(g, third_at, dot(attended_t[...], branch[:, at : at + PAIR]))
        start(g)
    begin(0)

    sides = lax.broadcasted_iota(jnp.int32, (PAIR, count), 0)

    def attend(pair, carry):
        at = lambda which: pl.ds(pl.multiple_of(which * model + pair * PAIR, PAIR), PAIR)
        here = at(0)
        grad_mixed = dot_nt(branch[...], weights[here, 3 * model : 4 * model]).astype(LOW)
        q_pair, k_pair, v_pair = queries[:, here], keys[:, here], values[:, here]
        k_turned = jnp.transpose(k_pair)
        q_grad_t, k_grad, v_grad = None, None, None
        for part in range(2):
            side = (lanes < HEAD) if part == 0 else (lanes >= HEAD)
            side_t = (sides < HEAD) if part == 0 else (sides >= HEAD)
            own_keys = jnp.where(side, k_pair, LOW(0))
            own_values = jnp.where(side, v_pair, LOW(0))
            own_queries = jnp.where(side, q_pair, LOW(0))
            own_grads = jnp.where(side, grad_mixed, LOW(0))
            own_turned = jnp.where(side_t, k_turned, LOW(0))
            scores = dot_nt(own_keys, q_pair) + bias[...]
            attn = jnp.exp(scores - lse_rows[pl.ds(2 * pair + part, 1), :])
            attn_grad = dot_nt(own_values, grad_mixed)
            mean = jnp.sum(attn * attn_grad, axis=0, keepdims=True)
            score_grad = (attn * (attn_grad - mean)).astype(LOW)
            v_part = dot(attn.astype(LOW), own_grads)
            k_part = dot(score_grad, own_queries)
            q_part = dot(own_turned, score_grad)
            if part == 0:
                q_grad_t, k_grad, v_grad = q_part, k_part, v_part
            else:
                q_grad_t, k_grad, v_grad = q_grad_t + q_part, k_grad + k_part, v_grad + v_part
        q_grad = (jnp.transpose(q_grad_t) * HEAD**-0.5).astype(LOW)
        k_grad = k_grad.astype(LOW)
        v_grad = v_grad.astype(LOW)
        sums[2:3, here] = jnp.sum(q_grad.astype(F32), axis=0, keepdims=True)
        sums[3:4, here] = jnp.sum(v_grad.astype(F32), axis=0, keepdims=True)
        source = normed_t[...]
        g = pair + n_proj
        for which, piece in enumerate((q_grad, k_grad, v_grad)):
            put(g, which, dot(source, piece))
        start(g)
        lax.fori_loop(wide - 1 - pairs + pair, wide - pairs + pair, give, 0)
        give_grad(PIECES - pairs + pair)
        total[...] += (
            dot_nt(q_grad, weights[:, at(0)]) + dot_nt(k_grad, weights[:, at(1)]) + dot_nt(v_grad, weights[:, at(2)])
        )
        if not gathered:
            begin(g - 1)

            @pl.when(g >= 3)
            def _():
                middle_of(g - 3)

            @pl.when(g >= 4)
            def _():
                end(g - 4)

        return carry

    lax.fori_loop(0, pairs, attend, 0)
    grad = total[...]
    xhat, scale = norm_parts(tokens[...].astype(F32))
    sums[0:1] = jnp.sum(grad * xhat, axis=0, keepdims=True)
    sums[1:2] = jnp.sum(grad, axis=0, keepdims=True)
    stacked = jnp.concatenate([sums[...], jnp.zeros((PAIR - 8, model), F32)], axis=0)
    turned = pltpu.roll(jnp.transpose(stacked), experts, 1)
    wide_lanes = lax.broadcasted_iota(jnp.int32, (model, PAIR), 1)
    put(small_at, 0, jnp.where(wide_lanes < experts, router[...], turned))
    start(small_at)
    begin(small_at - 1)
    middle_of(small_at - 3)
    end(small_at - 4)
    tokens_grad[...] = (middle_grad[...] + norm_back(grad, vecs[0:1], xhat, scale)).astype(LOW)
    begin(small_at)
    middle_of(small_at - 2)
    end(small_at - 3)
    middle_of(small_at - 1)
    middle_of(small_at)
    end(small_at - 2)
    end(small_at - 1)
    end(small_at)

    def taken(k, carry):
        d = k + 1
        y_copy(d, (me + d) % wide).wait_send()
        y_copy(d, (me - d + wide) % wide).wait_recv()
        return carry

    lax.fori_loop(0, wide - 1, taken, 0)
    keep_y.wait()
    returned = y_here[...].reshape(wide * stride, model)
    mixed = gates[:, 0:1] * dot(jnp.where(slot_at == slot_a, 1.0, 0.0).astype(LOW), returned)
    mixed += gates[:, 1:2] * dot(jnp.where(slot_at == slot_b, 1.0, 0.0).astype(LOW), returned)
    block_out[...] = (middle[...] + mixed).astype(LOW)
    if not gathered:
        for g in range(n_proj):
            out_proj[:, g * per : (g + 1) * per] = last(g)
        for pair in range(pairs):
            summed = last(n_proj + pair)
            for which in range(3):
                at = which * model + pair * PAIR
                out_qkv[:, at : at + PAIR] = summed[:, which * PAIR : (which + 1) * PAIR]
        summed = last(small_at)
        out_router[...] = summed[:, 0:experts]
        square = jnp.concatenate([summed, jnp.zeros((PAIR - height, PAIR), F32)], axis=0)
        turned = jnp.transpose(square)
        for i, ref in enumerate(out_vecs):
            ref[...] = turned[experts + i : experts + i + 1, 0:height]
        for g in range(small_at + 1):
            hop_core(g).wait_send()
            for dx in range(1, across):
                hop_x(g, dx).wait_send()
            for dy in range(1, rows):
                hop_y(g, dy).wait_send()
            for dz in range(1, depth):
                hop_z(g, dz).wait_send()
    for i in range(PIECES):
        for copy in g_copies(i):
            copy.wait()


def back_stage(
    dims, used, experts, gathered, tokens, saved, params, slots, token_rows, gate_slots, cotangent, y_rows, side_grads,
):
    depth, across, rows, cores = dims
    wide, narrow = depth * across, rows * cores
    count, model = tokens.shape
    stride = y_rows.shape[1]
    per = 3 * PAIR
    groups = model // per + model // PAIR + 1
    height = model // (wide * narrow)
    any_, vmem = pl.BlockSpec(memory_space=pl.ANY), pl.BlockSpec(memory_space=pltpu.VMEM)
    low = lambda *shape: jax.ShapeDtypeStruct(shape, LOW)
    f32 = lambda *shape: jax.ShapeDtypeStruct(shape, F32)
    sem = lambda size: [pltpu.SemaphoreType.DMA((size,))] * 2
    outs = [low(count, model), low(count, model), low(rows - 1, *side_grads[0].shape)]
    buffers, sems = [], []
    if gathered:
        outs.append(low(groups, model, per))
    else:
        outs += [f32(height, 3 * model), f32(height, model), f32(height, experts), *[f32(1, height)] * 7]
        buffers = [
            pltpu.VMEM((groups, depth, across, rows, cores, height, per), LOW),
            pltpu.VMEM((groups, depth, across, rows, height, per), LOW),
            pltpu.VMEM((groups * (across - 1), depth, rows, height, per), LOW),
            pltpu.VMEM((groups * (rows - 1), depth, height, per), LOW),
            pltpu.VMEM((groups * (depth - 1), height, per), LOW),
        ]
        sems = [
            *sem(groups), *sem(groups * (across - 1)), *sem(groups * (rows - 1)), *sem(groups * (depth - 1)),
        ]
    return pl.pallas_call(
        functools.partial(back_kernel, dims, used, experts, gathered),
        out_shape=tuple(outs),
        in_specs=[vmem] * 8 + [any_] + [vmem] * 10 + [any_] * rows,
        out_specs=[vmem] * 2 + [any_] + [vmem] * (len(outs) - 3),
        scratch_shapes=[
            *buffers,
            pltpu.VMEM((count, model), LOW),
            pltpu.VMEM((count, model), F32),
            pltpu.VMEM((count, model), F32),
            pltpu.VMEM((8, model), F32),
            pltpu.VMEM((model, PAIR), F32),
            pltpu.VMEM((wide, stride, PAIR), LOW),
            pltpu.VMEM((wide, stride, model), LOW),
            *sem(wide), *sem((rows - 1) * PIECES),
            pltpu.SemaphoreType.DMA((1,)),
            *sems,
        ],
        compiler_params=pltpu.CompilerParams(
            collective_id=1, has_side_effects=True, vmem_limit_bytes=60 * 1024 * 1024
        ),
        cost_estimate=pl.CostEstimate(flops=16 * 10**9, bytes_accessed=40 * 10**6, transcendentals=4 * 10**6),
        name="back_stage",
    )(
        tokens, *saved, params, slots, token_rows, gate_slots, cotangent, y_rows, *side_grads
    )


def tail_kernel(count, *refs):
    inputs, own, others = refs[:count], refs[count], refs[count + 1]
    outputs, grad_in, grad_out = refs[count + 2 : 2 * count + 2], refs[2 * count + 2], refs[2 * count + 3]
    terms, first, second, sems, loads, brings = refs[2 * count + 4 : 2 * count + 10]
    held = refs[2 * count + 10 :]
    rows = terms.shape[0]
    arrivals = [
        pltpu.make_async_copy(own if i == 0 else others.at[i - 1], terms.at[i], loads.at[i]) for i in range(rows)
    ]
    bring = [pltpu.make_async_copy(src, dst, brings.at[i]) for i, (src, dst) in enumerate(zip(inputs, held))]
    copies = [pltpu.make_async_copy(src, dst, sems.at[i]) for i, (src, dst) in enumerate(zip(held, outputs))]
    for copy in bring + arrivals:
        copy.start()
    for into, out in zip(bring, copies):
        into.wait()
        out.start()
    for copy in arrivals:
        copy.wait()

    def total(which):
        acc = terms[0, which].astype(F32)
        for i in range(1, rows):
            acc = acc + terms[i, which].astype(F32)
        return acc

    first[0] = total(0)
    copies.append(pltpu.make_async_copy(first, grad_in, sems.at[count]))
    copies[-1].start()
    second[0] = jnp.transpose(total(1))
    copies.append(pltpu.make_async_copy(second, grad_out, sems.at[count + 1]))
    copies[-1].start()
    for copy in copies:
        copy.wait()


def tail_stage(arrays, own, others):
    any_ = pl.BlockSpec(memory_space=pl.ANY)
    _, model, ff = own.shape
    count = len(arrays)
    shapes = [jax.ShapeDtypeStruct(a.shape, a.dtype) for a in arrays]
    shapes += [jax.ShapeDtypeStruct((1, model, ff), F32), jax.ShapeDtypeStruct((1, ff, model), F32)]
    rows = others.shape[0] + 1
    return pl.pallas_call(
        functools.partial(tail_kernel, count),
        out_shape=tuple(shapes),
        in_specs=[any_] * (count + 2),
        out_specs=[any_] * (count + 2),
        scratch_shapes=[
            pltpu.VMEM((rows, 2, model, ff), LOW),
            pltpu.VMEM((1, model, ff), F32),
            pltpu.VMEM((1, ff, model), F32),
            pltpu.SemaphoreType.DMA((count + 2,)),
            pltpu.SemaphoreType.DMA((rows,)),
            pltpu.SemaphoreType.DMA((count,)),
            *[pltpu.VMEM(a.shape, a.dtype) for a in arrays],
        ],
        compiler_params=pltpu.CompilerParams(vmem_limit_bytes=58 * 1024 * 1024),
        name="results",
    )(*arrays, own, others)


def gelu_and_slope(v):
    root = 0.7978845608028654
    cubic = 0.044715
    square = v * v
    half = 0.5 * jnp.tanh(v * (root + (root * cubic) * square)) + 0.5
    value = v * half
    slope = half + value * ((1.0 - half) * (2.0 * root + (6.0 * root * cubic) * square))
    return value, slope


def moe_kernel(
    dims, used, moe_low, slot_rows, slot_cols, gates, ups, b_in, b_out, w_in, w_out, *rest
):
    depth, across, rows, cores = dims
    wide = depth * across
    narrow = rows * cores
    side_out = rest[: rows - 1]
    rest = rest[rows - 1 :]
    token_rows, gate_slots, y_out, in_bias_grad, out_bias_grad = rest[:5]
    own_grad = rest[5]
    side_grad = rest[6 : 5 + rows]
    (
        full_in, full_out, x_send, x_here, g_send, g_here, dx_send, h_send, hidden, pre_grad, weighted,
        x_turned, w_turned, grad_send, grad_here, extra, extra_here, extra_y, blank,
        local, blanks, s_wy, r_wy, s_ey, r_ey, s_in, r_in, s_out, r_out, s_x, r_x, s_g, r_g, s_dx, r_dx, s_h, r_h, s_w, r_w, s_e, r_e,
    ) = rest[5 + rows :]
    z, x, y, c = place_of(dims)
    me, n = z * across + x, y * cores + c
    count, model = moe_low.shape
    capacity = x_send.shape[1]
    gate_width = g_send.shape[2]
    ff = full_in.shape[2]
    other = device_at(dims, z, x, y, 1 - c)

    def remote(src, dst, ssem, rsem, to):
        return pltpu.make_async_remote_copy(
            src_ref=src, dst_ref=dst, send_sem=ssem, recv_sem=rsem, device_id=to, device_id_type=MESH
        )

    along_y = [device_at(dims, z, x, (y + i) % rows, c) for i in range(1, rows)]
    body = pl.ds(0, used)
    if used < capacity:
        x_here[:, used:capacity] = jnp.zeros((wide, capacity - used, model), LOW)
        blank[...] = jnp.zeros_like(blank)
    greet([((me + d) % wide, n) for d in range(1, wide)] + [other] + along_y)
    fills = []
    if used < capacity:
        for w in range(wide):
            fills.append(pltpu.make_async_copy(blank, token_rows.at[w, pl.ds(used, capacity - used)], blanks.at[w]))

    held = [((y - i) % rows) * cores + c for i in range(rows)]
    from_y, in_passes, out_loads, out_passes = [], [], [], []
    for i, h in enumerate(held):
        src_out = w_out.at[0] if i == 0 else side_out[i - 1].at[0]
        out_loads.append(pltpu.make_async_copy(src_out, full_out.at[h], local.at[i]))
        out_passes.append(remote(src_out, full_out.at[h], s_out.at[i], r_out.at[i], other))
        if i:
            from_y.append(remote(w_in.at[0], full_in.at[n], s_wy.at[i - 1], r_wy.at[i - 1], along_y[i - 1]))
        src_in = w_in.at[0] if i == 0 else full_in.at[h]
        in_passes.append(remote(src_in, full_in.at[h], s_in.at[i], r_in.at[i], other))
    in_load = pltpu.make_async_copy(w_in.at[0], full_in.at[n], local.at[rows])
    for copy in from_y + out_loads + out_passes:
        copy.start()

    slot_a, slot_b = slot_cols[:, 0:1], slot_cols[:, 1:2]
    gate_a, gate_b = gates[:, 0:1], gates[:, 1:2]
    row_at = lax.broadcasted_iota(jnp.int32, (capacity, count), 0)
    lane_at = lax.broadcasted_iota(jnp.int32, (count, gate_width), 1)
    source = moe_low[...]

    def rows_for(expert):
        first = expert * capacity
        hit = (slot_rows[0:1] - first == row_at) | (slot_rows[1:2] - first == row_at)
        picked = dot(jnp.where(hit, 1.0, 0.0).astype(LOW), source).astype(LOW)
        inside = lane_at < capacity
        hit_a = (slot_a - first == lane_at) & inside
        hit_b = (slot_b - first == lane_at) & inside
        gate = jnp.where(hit_a, gate_a, 0.0) + jnp.where(hit_b, gate_b, 0.0)
        return picked, jnp.sum(gate, axis=0, keepdims=True)

    def x_copy(d, to):
        return remote(x_send.at[to, body], x_here.at[me, body], s_x.at[d], r_x.at[d], (to, n))

    def g_copy(d, to):
        return remote(g_send.at[to], g_here.at[me], s_g.at[d], r_g.at[d], (to, n))

    def dx_copy(d, to):
        return remote(dx_send.at[to, body], token_rows.at[me, body], s_dx.at[d], r_dx.at[d], (to, n))

    def h_copy(d, to):
        return remote(h_send.at[to], gate_slots.at[me], s_h.at[d], r_h.at[d], (to, n))

    def dispatch(k, carry):
        d = (k + wide // 2 - 1) % (wide - 1) + 1
        to = (me + d) % wide
        picked, gate = rows_for(to)
        x_send[to] = picked
        g_send[to] = gate
        x_copy(d, to).start()
        g_copy(d, to).start()
        return carry

    lax.fori_loop(0, wide - 1, dispatch, 0)
    in_load.start()
    in_passes[0].start()
    for copy in fills:
        copy.start()
    picked, gate = rows_for(me)
    x_here[me] = picked
    g_here[me] = gate
    extra[...] = jnp.zeros_like(extra)
    out_bias = b_out[...].astype(F32)
    for copy in out_loads:
        copy.wait()

    def backs_of(places):
        def backs(k, carry):
            two = pl.ds(2 * k, 2)
            up = ups[two].reshape(2 * capacity, model)
            for h in places:
                lanes = pl.ds(pl.multiple_of(h * ff, PAIR), ff)
                pre_grad[two, :, lanes] = dot_nt(up, full_out[h]).astype(LOW).reshape(2, capacity, ff)
            return carry

        return backs

    lax.fori_loop(0, wide // 2, backs_of([i * cores + c for i in range(rows)]), 0)
    for copy in out_passes:
        copy.wait_recv()
    lax.fori_loop(0, wide // 2, backs_of([i * cores + 1 - c for i in range(rows)]), 0)
    for i in range(1, rows):
        from_y[i - 1].wait_recv()
        in_passes[i].start()
    in_load.wait()
    for copy in in_passes:
        copy.wait_recv()

    def expert(src):
        own = x_here[src]
        up = ups[src]
        gate = jnp.transpose(jnp.broadcast_to(g_here[src], (PAIR, gate_width)))[:capacity, 0:1]
        weigh = (gate * up.astype(F32)).astype(LOW)
        weighted[src] = weigh
        back_total = jnp.sum(up.astype(F32) * out_bias, axis=1, keepdims=True)
        dx = None
        for h in range(narrow):
            pre = dot(own, full_in[h]) + b_in[h]
            back = pre_grad[src, :, h * ff : (h + 1) * ff].astype(F32)
            value, slope = gelu_and_slope(pre)
            low = value.astype(LOW)
            hidden[src, :, h * ff : (h + 1) * ff] = low
            back_total += jnp.sum(value * back, axis=1, keepdims=True)
            wide_grad = slope * (gate * back)
            grad = wide_grad.astype(LOW)
            pre_grad[src, :, h * ff : (h + 1) * ff] = grad
            extra[h, 0:1, :ff] += jnp.sum(wide_grad, axis=0, keepdims=True)
            part = dot_nt(grad, full_in[h])
            dx = part if dx is None else dx + part
        dx_send[src] = dx.astype(LOW)
        spread = jnp.broadcast_to(back_total, (capacity, PAIR))
        spread = jnp.concatenate([spread, jnp.zeros((gate_width - capacity, PAIR), F32)], axis=0)
        h_send[src] = jnp.transpose(spread)[0:1]

    expert(me)
    keep_rows = pltpu.make_async_copy(dx_send.at[me, body], token_rows.at[me, body], local.at[2 * rows])
    keep_gate = pltpu.make_async_copy(h_send.at[me], gate_slots.at[me], local.at[2 * rows + 1])
    keep_rows.start()
    keep_gate.start()

    def serve(k, carry):
        d = jnp.where(k % 2 == 0, k // 2 + 1, wide - (k + 1) // 2)
        src = (me - d + wide) % wide
        x_copy(d, src).wait_recv()
        g_copy(d, src).wait_recv()
        expert(src)
        dx_copy(d, src).start()
        h_copy(d, src).start()
        return carry

    lax.fori_loop(0, wide - 1, serve, 0)

    all_rows = wide * capacity
    x_turned[...] = jnp.transpose(x_here[...].reshape(all_rows, model))
    w_turned[...] = jnp.transpose(weighted[...].reshape(all_rows, model))
    bias_grad = jnp.sum(weighted[...].reshape(all_rows, model).astype(F32), axis=0, keepdims=True)
    for h in range(narrow):
        extra[h, 1:2] = bias_grad

    def grad_of(h):
        lanes = pl.ds(pl.multiple_of(h * ff, PAIR), ff)
        grad_in = dot(x_turned[...], pre_grad[:, :, lanes].reshape(all_rows, ff))
        grad_out = dot(w_turned[...], hidden[:, :, lanes].reshape(all_rows, ff))
        return grad_in, grad_out

    order = [*range(1, rows), 0]
    swaps, by_y, keep_grads = {}, {}, []
    for i in order:
        at = (y + i) % rows
        h = at * cores + 1 - c
        grad_in, grad_out = grad_of(h)
        grad_send[i, 0] = grad_in.astype(LOW)
        grad_send[i, 1] = grad_out.astype(LOW)
        swaps[i] = (
            remote(grad_send.at[i], grad_here.at[i], s_w.at[i], r_w.at[i], other),
            remote(extra.at[h], extra_here.at[i], s_e.at[i], r_e.at[i], other),
        )
        for copy in swaps[i]:
            copy.start()
        h = at * cores + c
        grad_in, grad_out = grad_of(h)
        for copy in swaps[i]:
            copy.wait_recv()
        grad_here[i, 0] = (grad_in + grad_here[i, 0].astype(F32)).astype(LOW)
        grad_here[i, 1] = (grad_out + grad_here[i, 1].astype(F32)).astype(LOW)
        extra_here[i] = extra_here[i] + extra[h]
        if i:
            by_y[i] = remote(
                extra_here.at[i], extra_y.at[i - 1], s_ey.at[i - 1], r_ey.at[i - 1], along_y[i - 1]
            )
            by_y[i].start()
        target = own_grad if i == 0 else side_grad[i - 1]
        keep_grads.append(pltpu.make_async_copy(grad_here.at[i], target, local.at[2 * rows + 3 + i]))
        keep_grads[-1].start()

    def outputs(src, carry):
        total = None
        for h in range(narrow):
            part = dot(hidden[src, :, h * ff : (h + 1) * ff], full_out[h])
            total = part if total is None else total + part
        x_send[src] = (total + out_bias).astype(LOW)
        return carry

    def sent(k, carry):
        to = (me + k + 1) % wide
        x_copy(k + 1, to).wait_send()
        g_copy(k + 1, to).wait_send()
        return carry

    lax.fori_loop(0, wide - 1, sent, 0)
    lax.fori_loop(0, wide, outputs, 0)
    keep_y = pltpu.make_async_copy(x_send, y_out, local.at[2 * rows + 2])
    keep_y.start()
    bias_rows = extra_here[0]
    for i in range(1, rows):
        by_y[i].wait_recv()
        bias_rows = bias_rows + extra_y[i - 1]
    in_bias_grad[...] = bias_rows[0:1, :ff]
    out_bias_grad[...] = bias_rows[1:2]

    def finish(k, carry):
        d = k + 1
        back = (me - d + wide) % wide
        dx_copy(d, back).wait_recv()
        h_copy(d, back).wait_recv()
        dx_copy(d, back).wait_send()
        h_copy(d, back).wait_send()
        return carry

    lax.fori_loop(0, wide - 1, finish, 0)
    pairs = [copy for i in range(rows) for copy in swaps[i]] + [by_y[i] for i in range(1, rows)]
    for copy in from_y + in_passes + out_passes + pairs:
        copy.wait_send()
    for copy in fills:
        copy.wait()
    for copy in [keep_rows, keep_gate, keep_y] + keep_grads:
        copy.wait()


def moe_stage(dims, used, capacity, moe_low, slot_rows, slots, gates, ups, b_in, b_out, w_in, w_out, side_out):
    depth, across, rows, cores = dims
    wide, narrow = depth * across, rows * cores
    count, model = moe_low.shape
    ff = w_in.shape[2]
    gate_width = -(-capacity // PAIR) * PAIR
    any_, vmem = pl.BlockSpec(memory_space=pl.ANY), pl.BlockSpec(memory_space=pltpu.VMEM)
    low = lambda *shape: jax.ShapeDtypeStruct(shape, LOW)
    f32 = lambda *shape: jax.ShapeDtypeStruct(shape, F32)
    sem = lambda size: [pltpu.SemaphoreType.DMA((size,))] * 2
    outs = pl.pallas_call(
        functools.partial(moe_kernel, dims, used),
        out_shape=(
            low(wide, capacity, model), f32(wide, 1, gate_width), low(wide, capacity, model),
            f32(1, ff), f32(1, model), *[low(2, model, ff)] * rows,
        ),
        in_specs=[vmem] * 7 + [any_] * (1 + rows),
        out_specs=[any_] * 3 + [vmem] * 2 + [any_] * rows,
        scratch_shapes=[
            pltpu.VMEM((narrow, model, ff), LOW),
            pltpu.VMEM((narrow, ff, model), LOW),
            pltpu.VMEM((wide, capacity, model), LOW),
            pltpu.VMEM((wide, capacity, model), LOW),
            pltpu.VMEM((wide, 1, gate_width), F32),
            pltpu.VMEM((wide, 1, gate_width), F32),
            pltpu.VMEM((wide, capacity, model), LOW),
            pltpu.VMEM((wide, 1, gate_width), F32),
            pltpu.VMEM((wide, capacity, narrow * ff), LOW),
            pltpu.VMEM((wide, capacity, narrow * ff), LOW),
            pltpu.VMEM((wide, capacity, model), LOW),
            pltpu.VMEM((model, wide * capacity), LOW),
            pltpu.VMEM((model, wide * capacity), LOW),
            pltpu.VMEM((rows, 2, model, ff), LOW),
            pltpu.VMEM((rows, 2, model, ff), LOW),
            pltpu.VMEM((narrow, 8, model), F32),
            pltpu.VMEM((rows, 8, model), F32),
            pltpu.VMEM((rows - 1, 8, model), F32),
            pltpu.VMEM((max(capacity - used, 8), model), LOW),
            pltpu.SemaphoreType.DMA((3 * rows + 3,)),
            pltpu.SemaphoreType.DMA((wide,)),
            *sem(rows), *sem(rows), *sem(rows), *sem(rows), *sem(wide), *sem(wide), *sem(wide), *sem(wide), *sem(rows), *sem(rows),
        ],
        compiler_params=pltpu.CompilerParams(
            collective_id=2, has_side_effects=True, vmem_limit_bytes=60 * 1024 * 1024
        ),
        cost_estimate=pl.CostEstimate(flops=36 * 10**9, bytes_accessed=25 * 10**6, transcendentals=4 * 10**6),
        name="moe_stage",
    )(moe_low, slot_rows, slots, gates, ups, b_in, b_out, w_in, w_out, *side_out)
    return outs[:3], outs[3:5], outs[5:]


def per_device(
    dims,
    tokens, segment_ids, patch_valid, routes, priority, gain_attn, shift_attn, w_qkv, query_bias, value_bias,
    w_proj, proj_bias, gain_moe, shift_moe, w_router, w_in, in_bias, w_out, out_bias, cotangent,
):
    count, model = tokens.shape
    experts = w_router.shape[1]
    capacity = (210 * count + 100 * experts - 1) // (100 * experts)
    shard_rows = gain_attn.shape[0]
    vectors = jnp.stack([gain_attn, shift_attn, query_bias, value_bias, proj_bias, gain_moe, shift_moe])
    stride = -(-capacity // 16) * 16
    gathered = shard_rows % 8 != 0
    every = ("wide", "narrow")
    if gathered:
        empty = jnp.zeros((shard_rows, PAIR - 7 - experts), LOW)
        pack = jnp.concatenate([w_qkv, w_proj, w_router, jnp.transpose(vectors), empty], axis=1)
        pack = [lax.all_gather(pack, every, axis=0, tiled=True)]
    else:
        pack = [w_qkv, w_proj, jnp.transpose(w_router), vectors]
    params, saved, (slots, slot_rows, full_b_in, ups), side_out = front_stage(
        dims, experts, capacity, stride, gathered, pack, tokens, segment_ids, patch_valid, routes, priority,
        cotangent, w_out, in_bias,
    )
    moe_low, gates = saved[7], saved[10]
    used = -(-capacity // 8) * 8
    (token_rows, gate_slots, y_rows), bias_grads, (own_grad, *side_grads) = moe_stage(
        dims, used, stride, moe_low, slot_rows, slots, gates, ups, full_b_in, out_bias, w_in, w_out, side_out
    )
    outs = back_stage(
        dims, used, experts, gathered, tokens, saved, params, slots, token_rows, gate_slots, cotangent, y_rows, side_grads,
    )
    settled = tail_stage([*outs[:2], *outs[3:], *bias_grads], own_grad, outs[2])
    outs, (grad_in_bias, grad_out_bias, grad_w_in, grad_w_out) = settled[:-4], settled[-4:]
    block_out, tokens_grad = outs[:2]
    if gathered:
        groups = lax.psum_scatter(outs[2].astype(F32), every, scatter_dimension=1, tiled=True)
        n_proj = model // (3 * PAIR)
        grad_proj = jnp.concatenate(list(groups[:n_proj]), axis=1)
        by_head = groups[n_proj:-1].reshape(-1, shard_rows, 3, PAIR)
        grad_qkv = by_head.transpose(1, 2, 0, 3).reshape(shard_rows, -1)
        grad_router = groups[-1, :, :experts]
        vector = [groups[-1, :, experts + i] for i in range(7)]
    else:
        grad_qkv, grad_proj, grad_router = outs[2:5]
        vector = [row.reshape(-1) for row in outs[5:]]
    return (
        block_out,
        tokens_grad,
        vector[0],
        vector[1],
        grad_qkv,
        vector[2],
        vector[3],
        grad_proj,
        vector[4],
        vector[5],
        vector[6],
        grad_router,
        grad_w_in,
        grad_in_bias,
        grad_w_out,
        grad_out_bias,
    )


def solution(mesh):
    dims = grid_of(mesh.shape["wide"], mesh.shape["narrow"])
    every = ("wide", "narrow")
    rows, vector = P(every, None), P(every)
    return jax.shard_map(
        functools.partial(per_device, dims),
        mesh=mesh,
        in_specs=(
            rows, rows, rows, rows, rows, vector, vector, rows, vector, vector, rows, vector, vector, vector,
            rows, P("wide", None, "narrow"), P("wide", "narrow"), P("wide", "narrow", None), P("wide", None), rows,
        ),
        out_specs=(
            rows, rows, vector, vector, rows, vector, vector, rows, vector, vector, vector, rows,
            P("wide", None, "narrow"), P("wide", "narrow"), P("wide", "narrow", None), P("wide", None),
        ),
        check_vma=False,
    )
```

```python
import functools

import jax
import jax.numpy as jnp
from jax import lax
from jax.experimental import pallas as pl
from jax.experimental.pallas import tpu as pltpu
from jax.sharding import PartitionSpec as P

HEAD = 64
PAIR = 2 * HEAD
EPSILON = 1e-06
MASKED = -1000000000.0
MESH = pl.DeviceIdType.MESH
LOW = jnp.bfloat16
F32 = jnp.float32
PIECES = 8
EARLY = 2
VMEM_LIMIT = 58 * 1024 * 1024


def dot(a, b):
    return jnp.dot(a, b, preferred_element_type=F32)


def dot_nt(a, b):
    return lax.dot_general(a, b, (((1,), (1,)), ((), ())), preferred_element_type=F32)


def dot_tn(a, b):
    return lax.dot_general(a, b, (((0,), (0,)), ((), ())), preferred_element_type=F32)


def grid_of(wide, narrow):
    along_x = 1 << ((wide.bit_length() - 1) // 2)
    return wide // along_x, along_x, narrow // 2, 2


def place_of(dims):
    depth, across, rows, cores = dims
    wide, narrow = lax.axis_index("wide"), lax.axis_index("narrow")
    return wide // across, wide % across, narrow // cores, narrow % cores


def device_at(dims, z, x, y, c):
    depth, across, rows, cores = dims
    return (z * across + x, y * cores + c)


def ahead_of(dims, d):
    depth, across, rows, cores = dims
    z, x, y, c = place_of(dims)
    return (z + d // across) % depth * across + (x + d % across) % across


def behind_of(dims, d):
    depth, across, rows, cores = dims
    z, x, y, c = place_of(dims)
    return (z + depth - d // across) % depth * across + (x + across - d % across) % across


def greet(peers):
    barrier = pltpu.get_barrier_semaphore()
    for peer in peers:
        pl.semaphore_signal(barrier, inc=1, device_id=peer, device_id_type=MESH)
    pl.semaphore_wait(barrier, len(peers))


def neighbours(dims):
    depth, across, rows, cores = dims
    z, x, y, c = place_of(dims)
    peers = [device_at(dims, (z + d) % depth, x, y, c) for d in range(1, depth)]
    peers += [device_at(dims, z, (x + d) % across, y, c) for d in range(1, across)]
    peers += [device_at(dims, z, x, (y + d) % rows, c) for d in range(1, rows)]
    peers += [device_at(dims, z, x, y, 1 - c)]
    return peers


def norm_parts(values):
    center = jnp.mean(values, axis=-1, keepdims=True)
    offset = values - center
    spread = jnp.mean(offset * offset, axis=-1, keepdims=True)
    scale = lax.rsqrt(spread + EPSILON)
    return offset * scale, scale


def column_of(row):
    return jnp.transpose(jnp.broadcast_to(row, (PAIR, row.shape[1])))[:, 0:1]


def front_kernel(
    dims, experts, capacity, gathered, heads, *rest
):
    depth, across, rows, cores = dims
    wide, narrow = depth * across, rows * cores
    pack_refs, rest = rest[:heads], rest[heads:]
    tokens, seg_row, valid_row, routes, priority, cotangent, w_out, b_in = rest[:8]
    rest = rest[8:]
    (
        params, normed_t, q_out, k_out, v_out, attended_t, lse_rows, middle, moe_low, moe_low_t, probs_out, gates_out, vecs,
        bias_t, slots_out, slot_rows, full_b_in, ups,
    ) = rest[:18]
    side_out = rest[18 : 17 + rows]
    (
        normed, attended, total, bias, lse, up_send, b_send, shard, turn, blank,
        s1, r1, sx, rx, sy, ry, sa, ra, sb, rb, sc, rc, s_up, r_up, s_w, r_w, s_b, r_b, local, blanks,
    ) = rest[17 + rows :]
    z, x, y, c = place_of(dims)
    me, n = z * across + x, y * cores + c
    count, model = tokens.shape
    stride = ups.shape[1]
    lanes = lax.broadcasted_iota(jnp.int32, (count, PAIR), 1)

    def remote(src, dst, ssem, rsem, to):
        return pltpu.make_async_remote_copy(
            src_ref=src, dst_ref=dst, send_sem=ssem, recv_sem=rsem, device_id=to, device_id_type=MESH
        )

    def send(src, dst, ssem, rsem, to):
        copy = remote(src, dst, ssem, rsem, to)
        copy.start()
        return copy

    if not gathered:
        w_qkv, w_proj, router_t, vectors = pack_refs
        packs = [
            pltpu.make_async_copy(w_qkv, shard.at[:, pl.ds(0, 3 * model)], local.at[3]),
            pltpu.make_async_copy(w_proj, shard.at[:, pl.ds(3 * model, model)], local.at[4]),
        ]
        for copy in packs:
            copy.start()
        height = shard.shape[0]
        turn[...] = jnp.zeros_like(turn)
        turn[0:experts, 0:height] = router_t[...].astype(F32)
        turn[experts : experts + 7, 0:height] = vectors[...].astype(F32)
        shard[:, 4 * model : 4 * model + PAIR] = jnp.transpose(turn[...])[0:height].astype(LOW)
    b_send[...] = b_in[...].astype(F32)
    peers = [((me + d) % wide, n) for d in range(1, wide)]
    peers += [(me, (n + d) % narrow) for d in range(1, narrow)]
    greet(peers)
    if not gathered:
        for copy in packs:
            copy.wait()

    first, by_x, by_y, half_a, half_b, by_core = {}, {}, {}, {}, {}, {}
    keeps = []
    if not gathered:
        width = shard.shape[1]
        cut = (width // 256) * 128

        def block(dz, dx, dy, core):
            at = ((z - dz) % depth) * across + (x - dx) % across
            return params.at[(at * rows + (y - dy) % rows) * cores + core]

        own = block(0, 0, 0, c)
        keeps.append(pltpu.make_async_copy(shard, own, local.at[0]))
        keeps[-1].start()
        for dz in range(1, depth):
            first[dz] = send(
                shard, own, s1.at[dz - 1], r1.at[dz - 1], device_at(dims, (z + dz) % depth, x, y, c)
            )

    def to_core(dz, dx, dy):
        at = (dz * across + dx) * rows + dy
        src = shard if (dz, dx, dy) == (0, 0, 0) else block(dz, dx, dy, c)
        by_core[at] = send(
            src, block(dz, dx, dy, c), sc.at[at], rc.at[at], device_at(dims, z, x, y, 1 - c)
        )

    def spread(dz):
        if dz:
            first[dz].wait_recv()
        src = block(dz, 0, 0, c) if dz else shard
        for dx in range(1, across):
            at = dz * (across - 1) + dx - 1
            by_x[dz, dx] = send(
                src, block(dz, 0, 0, c), sx.at[at], rx.at[at],
                device_at(dims, z, (x + dx) % across, y, c),
            )
        for dy in range(1, rows):
            at = dz * (rows - 1) + dy - 1
            by_y[dz, dy] = send(
                src, block(dz, 0, 0, c), sy.at[at], ry.at[at],
                device_at(dims, z, x, (y + dy) % rows, c),
            )
        to_core(dz, 0, 0)

    def corner(dz):
        for dx in range(1, across):
            by_x[dz, dx].wait_recv()
            part = block(dz, dx, 0, c).at[:, pl.ds(0, cut)]
            for dy in range(1, rows):
                at = (dz * (across - 1) + dx - 1) * (rows - 1) + dy - 1
                half_a[dz, dx, dy] = send(
                    part, part, sa.at[at], ra.at[at], device_at(dims, z, x, (y + dy) % rows, c)
                )
            to_core(dz, dx, 0)
        for dy in range(1, rows):
            by_y[dz, dy].wait_recv()
            part = block(dz, 0, dy, c).at[:, pl.ds(cut, width - cut)]
            for dx in range(1, across):
                at = (dz * (across - 1) + dx - 1) * (rows - 1) + dy - 1
                half_b[dz, dx, dy] = send(
                    part, part, sb.at[at], rb.at[at], device_at(dims, z, (x + dx) % across, y, c)
                )
            to_core(dz, 0, dy)

    def finish(dz):
        for dx in range(1, across):
            for dy in range(1, rows):
                half_a[dz, dx, dy].wait_recv()
                half_b[dz, dx, dy].wait_recv()
                to_core(dz, dx, dy)

    if not gathered:
        spread(0)
    b_copies = []
    for d in range(1, narrow):
        b_copies.append(send(b_send, full_b_in.at[n], s_b.at[d], r_b.at[d], (me, (n + d) % narrow)))
    keeps.append(pltpu.make_async_copy(b_send, full_b_in.at[n], local.at[1]))
    keeps[-1].start()
    w_copies = []

    piece = w_out.shape[1] // PIECES

    def weight_piece(i):
        for dy in range(1, rows):
            at = (dy - 1) * PIECES + i
            part = pl.ds(i * piece, piece)
            to = device_at(dims, z, x, (y + dy) % rows, c)
            w_copies.append(send(w_out.at[:, part], side_out[dy - 1].at[:, part], s_w.at[at], r_w.at[at], to))

    used = -(-capacity // 8) * 8
    fills = []
    if used < stride:
        blank[...] = jnp.zeros_like(blank)
        for w in range(wide):
            fills.append(pltpu.make_async_copy(blank, ups.at[w, pl.ds(used, stride - used)], blanks.at[w]))
            fills[-1].start()

    half = PAIR // 2
    valid = valid_row[...].astype(F32)
    valid_col = column_of(valid)
    rank_row = priority[...].astype(F32)
    ahead = jnp.where(rank_row < column_of(rank_row), 1.0, 0.0).astype(LOW)
    first_at = column_of(routes[0:1].astype(F32)).astype(jnp.int32)
    second_at = column_of(routes[1:2].astype(F32)).astype(jnp.int32)
    hit_first, hit_second = lanes == first_at, lanes == second_at + half
    hot = jnp.where(hit_first | hit_second, valid_col, 0.0)
    earlier = dot(ahead, hot.astype(LOW))
    filled = pltpu.roll(jnp.sum(hot, axis=0, keepdims=True), half, 1)
    filled = jnp.broadcast_to(jnp.where(lanes[0:1] >= half, filled, 0.0), (8, PAIR))[0:1]
    earlier = earlier + filled
    place_a = jnp.sum(jnp.where(hit_first, earlier, 0.0), axis=1, keepdims=True).astype(jnp.int32)
    place_b = jnp.sum(jnp.where(hit_second, earlier, 0.0), axis=1, keepdims=True).astype(jnp.int32)
    kept_a = (place_a < capacity) & (valid_col > 0.5)
    kept_b = (place_b < capacity) & (valid_col > 0.5)
    slot_a = jnp.where(kept_a, first_at * stride + place_a, -1)
    slot_b = jnp.where(kept_b, second_at * stride + place_b, -1)
    slots = jnp.where(lanes == 0, slot_a, slot_b)
    slots_out[...] = jnp.where(lanes < 2, slots, jnp.where(lanes == 2, first_at, second_at))
    slot_rows[...] = jnp.transpose(slots.astype(F32))[0:8].astype(jnp.int32)

    segments = seg_row[...].astype(F32)
    keys_at = lax.broadcasted_iota(jnp.int32, (count, count), 1)
    rows_at = lax.broadcasted_iota(jnp.int32, (count, count), 0)
    allowed = (column_of(segments) == segments) & ((valid > 0.5) | (keys_at == rows_at))
    bias[...] = jnp.where(allowed, 0.0, MASKED)
    xhat, _ = norm_parts(tokens[...].astype(F32))
    total[...] = xhat
    lse[...] = jnp.zeros_like(lse)

    row_at = lax.broadcasted_iota(jnp.int32, (stride, count), 0)

    def up_copy(d, to):
        body = pl.ds(0, used)
        return remote(up_send.at[to, body], ups.at[me, body], s_up.at[d], r_up.at[d], (to, n))

    def rows_for(expert):
        start = expert * stride
        hit = (slot_rows[0:1] - start == row_at) | (slot_rows[1:2] - start == row_at)
        return dot(jnp.where(hit, 1.0, 0.0).astype(LOW), cotangent[...]).astype(LOW)

    def give(d):
        to = ahead_of(dims, d)
        up_send[to] = rows_for(to)
        up_copy(d, to).start()

    def dispatch(k, carry):
        give(k + 1)
        return carry

    if not gathered:
        for step in range(1, depth):
            spread(step)
            corner(step - 1)
            if step >= 2:
                finish(step - 2)
        same_x = [(j + depth // 2 - 1) % (depth - 1) + 1 for j in range(depth - 1)]
        for j in same_x:
            give(across * j)
        corner(depth - 1)
        for i in range(PIECES):
            weight_piece(i)
        finish(depth - 2)
        finish(depth - 1)
        for d in range(1, wide):
            if d % across:
                give(d)
    else:
        lax.fori_loop(0, wide - 1, dispatch, 0)
        keeps.append(pltpu.make_async_copy(pack_refs[0], params, local.at[0]))
        keeps[-1].start()
        for i in range(PIECES):
            weight_piece(i)
    bias_t[...] = jnp.where(
        (column_of(segments) == segments) & ((valid_col > 0.5) | (keys_at == rows_at)), 0.0, MASKED
    )
    up_send[me] = rows_for(me)
    body = pl.ds(0, used)
    keep_up = pltpu.make_async_copy(up_send.at[me, body], ups.at[me, body], local.at[2])
    keep_up.start()
    for copy in by_core.values():
        copy.wait_recv()
    for copy in keeps:
        copy.wait()


    def columns(at):
        return params[:, at] if gathered else params[:, :, at].reshape(model, at.size)

    small = columns(pl.ds(4 * model, PAIR))
    vecs[...] = jnp.transpose(small.astype(F32))[experts : experts + 8]
    normed[...] = (total[...] * vecs[0:1] + vecs[1:2]).astype(LOW)

    def attend(pair, carry):
        at = lambda which: pl.ds(pl.multiple_of(which * model + pair * PAIR, PAIR), PAIR)
        here = at(0)
        source = normed[...]
        three = dot(source, jnp.concatenate([columns(at(0)), columns(at(1)), columns(at(2))], axis=1))
        queries = (three[:, :PAIR] + vecs[2:3, here]).astype(LOW) * LOW(HEAD**-0.5)
        keys = three[:, PAIR : 2 * PAIR].astype(LOW)
        values = (three[:, 2 * PAIR :] + vecs[3:4, here]).astype(LOW)
        q_out[:, here] = queries
        k_out[:, here] = keys
        v_out[:, here] = values
        mixed = None
        for part in range(2):
            side = (lanes < HEAD) if part == 0 else (lanes >= HEAD)
            own_keys = jnp.where(side, keys, LOW(0))
            own_values = jnp.where(side, values, LOW(0))
            scores = dot_nt(queries, own_keys) + bias[...]
            peak = jnp.max(scores, axis=1, keepdims=True)
            raised = jnp.exp(scores - peak)
            row_total = jnp.sum(raised, axis=1, keepdims=True)
            attn = (raised * (1.0 / row_total)).astype(LOW)
            piece = dot(attn, own_values)
            mixed = piece if mixed is None else mixed + piece
            lse[...] = jnp.where(lanes == 2 * pair + part, peak + jnp.log(row_total), lse[...])
        mixed = mixed.astype(LOW)
        attended[:, here] = mixed
        return carry

    lax.fori_loop(0, model // PAIR, attend, 0)

    def project(k, carry):
        here = pl.ds(pl.multiple_of(k * 2 * PAIR, PAIR), 2 * PAIR)
        there = pl.ds(pl.multiple_of(3 * model + k * 2 * PAIR, PAIR), 2 * PAIR)
        total[:, here] = dot(attended[...], columns(there))
        return carry

    lax.fori_loop(0, model // (2 * PAIR), project, 0)
    lse_rows[...] = jnp.transpose(lse[...])
    normed_t[...] = jnp.transpose(normed[...])
    attended_t[...] = jnp.transpose(attended[...])
    mid = tokens[...].astype(F32) + (total[...] + vecs[4:5])
    middle[...] = mid
    xhat, _ = norm_parts(mid)
    low = (xhat * vecs[5:6] + vecs[6:7]).astype(LOW)
    moe_low[...] = low
    moe_low_t[...] = jnp.transpose(low)
    logits = jnp.where(lanes < experts, dot(low, columns(pl.ds(4 * model, PAIR))), -jnp.inf)
    raised = jnp.exp(logits - jnp.max(logits, axis=1, keepdims=True))
    probs = raised / jnp.sum(raised, axis=1, keepdims=True)
    probs_out[...] = probs
    gate_a = jnp.sum(jnp.where(lanes == first_at, probs, 0.0), axis=1, keepdims=True)
    gate_b = jnp.sum(jnp.where(lanes == second_at, probs, 0.0), axis=1, keepdims=True)
    gates_out[...] = jnp.where(lanes == 0, gate_a, gate_b)

    def settle(k, carry):
        d = k + 1
        up_copy(d, ahead_of(dims, d)).wait_send()
        up_copy(d, behind_of(dims, d)).wait_recv()
        return carry

    lax.fori_loop(0, wide - 1, settle, 0)
    keep_up.wait()
    for copy in w_copies + b_copies + fills:
        copy.wait()
    for group in (first, by_x, by_y, half_a, half_b, by_core):
        for copy in group.values():
            copy.wait_send()


def front_stage(
    dims, experts, capacity, stride, gathered, pack, tokens, segment_ids, patch_valid, routes, priority,
    cotangent, w_out, in_bias,
):
    depth, across, rows, cores = dims
    wide, narrow = depth * across, rows * cores
    count, model = tokens.shape
    used = -(-capacity // 8) * 8
    any_, vmem = pl.BlockSpec(memory_space=pl.ANY), pl.BlockSpec(memory_space=pltpu.VMEM)
    low = lambda *shape: jax.ShapeDtypeStruct(shape, LOW)
    f32 = lambda *shape: jax.ShapeDtypeStruct(shape, F32)
    i32 = lambda *shape: jax.ShapeDtypeStruct(shape, jnp.int32)
    width = 4 * model + PAIR
    height = model if gathered else pack[0].shape[0]
    full = (height, width) if gathered else (wide * narrow, height, width)
    packed = 1 if gathered else height
    corners = depth * (across - 1) * (rows - 1)
    sems = []
    for size in (
        depth - 1, depth * (across - 1), depth * (rows - 1), corners, corners, depth * across * rows,
        wide, (rows - 1) * PIECES, narrow,
    ):
        sems += [pltpu.SemaphoreType.DMA((size,))] * 2
    outs = pl.pallas_call(
        functools.partial(front_kernel, dims, experts, capacity, gathered, len(pack)),
        out_shape=(
            low(*full), low(model, count), low(count, model), low(count, model), low(count, model),
            low(model, count), f32(PAIR, count), f32(count, model), low(count, model), low(model, count),
            f32(count, PAIR), f32(count, PAIR), f32(8, model), f32(count, count), i32(count, PAIR), i32(8, count),
            f32(narrow, 1, in_bias.shape[1]), low(wide, stride, model), *[low(*w_out.shape)] * (rows - 1),
        ),
        in_specs=([any_] if gathered else [any_, any_, vmem, vmem]) + [vmem] * 6 + [any_, vmem],
        out_specs=[vmem] * 17 + [any_] * rows,
        scratch_shapes=[
            pltpu.VMEM((count, model), LOW),
            pltpu.VMEM((count, model), LOW),
            pltpu.VMEM((count, model), F32),
            pltpu.VMEM((count, count), F32),
            pltpu.VMEM((count, PAIR), F32),
            pltpu.VMEM((wide, stride, model), LOW),
            pltpu.VMEM((1, in_bias.shape[1]), F32),
            pltpu.VMEM((packed, width), LOW),
            pltpu.VMEM((PAIR, PAIR), F32),
            pltpu.VMEM((max(stride - used, 8), model), LOW),
            *sems,
            pltpu.SemaphoreType.DMA((5,)),
            pltpu.SemaphoreType.DMA((wide,)),
        ],
        compiler_params=pltpu.CompilerParams(
            collective_id=0, has_side_effects=True, vmem_limit_bytes=VMEM_LIMIT
        ),
        cost_estimate=pl.CostEstimate(flops=7 * 10**9, bytes_accessed=20 * 10**6, transcendentals=4 * 10**6),
        name="front_stage",
    )(*pack, tokens, segment_ids, patch_valid, jnp.transpose(routes), priority, cotangent, w_out, in_bias)
    params = outs[0] if gathered else outs[0].reshape(wide * narrow * height, width)
    return params, outs[1:14], outs[14:18], outs[18:]


def norm_back(grad, gain, xhat, scale):
    scaled = grad * gain
    mean_a = jnp.mean(scaled, axis=-1, keepdims=True)
    mean_b = jnp.mean(scaled * xhat, axis=-1, keepdims=True)
    return scale * (scaled - mean_a - xhat * mean_b)


def back_kernel(dims, used, experts, gathered, *rest):
    depth, across, rows, cores = dims
    wide, narrow = depth * across, rows * cores
    (
        tokens, normed_t, queries, keys, values, attended_t, lse_rows, middle, _, moe_low_t, probs, gates, vecs, bias,
        weights, slots, token_rows, gate_slots, cotangent, y_rows,
    ) = rest[:20]
    side_grad = rest[20 : 19 + rows]
    rest = rest[19 + rows :]
    if gathered:
        block_out, tokens_grad, grad_here, group = rest[:4]
        rest = rest[4:]
    else:
        block_out, tokens_grad, grad_here, out_qkv, out_proj, out_router, *out_vecs = rest[:13]
        group, n1, n2, n3, n4 = rest[13:18]
        rest = rest[18:]
    branch, middle_grad, qkv_grad, sums, router, parts, y_here = rest[:7]
    s_y, q_y, s_g, q_g, local = rest[7:12]
    z, x, y, c = place_of(dims)
    me, n = z * across + x, y * cores + c
    count, model = tokens.shape
    stride = y_here.shape[1]
    pairs = model // PAIR
    per = 3 * PAIR
    n_proj = model // per
    small_at = n_proj + pairs
    lanes = lax.broadcasted_iota(jnp.int32, (count, PAIR), 1)

    def remote(src, dst, ssem, rsem, to):
        return pltpu.make_async_remote_copy(
            src_ref=src, dst_ref=dst, send_sem=ssem, recv_sem=rsem, device_id=to, device_id_type=MESH
        )

    peers = [((me + d) % wide, n) for d in range(1, wide)]
    peers += [device_at(dims, z, x, (y + d) % rows, c) for d in range(1, rows)]
    peers += [device_at(dims, z, x, y, 1 - c)]
    body = pl.ds(0, used)
    if used < stride:
        y_here[:, used:stride] = jnp.zeros((wide, stride - used, model), LOW)
    greet(peers)

    def y_copy(d, to):
        return remote(y_rows.at[to, body], y_here.at[me, body], s_y.at[d], q_y.at[d], (to, n))

    def give(k, carry):
        d = (k + wide // 2 - 1) % (wide - 1) + 1
        y_copy(d, ahead_of(dims, d)).start()
        return carry

    lax.fori_loop(0, wide - 1 - pairs, give, 0)
    keep_y = pltpu.make_async_copy(y_rows.at[me, body], y_here.at[me, body], local.at[0])
    keep_y.start()
    piece = grad_here.shape[1] // PIECES

    def g_copies(i):
        copies = []
        for dy in range(1, rows):
            at = (dy - 1) * PIECES + i
            part = pl.ds(i * piece, piece)
            to = device_at(dims, z, x, (y + dy) % rows, c)
            copies.append(remote(side_grad[dy - 1].at[part], grad_here.at[dy - 1, part], s_g.at[at], q_g.at[at], to))
        return copies

    def give_grad(i):
        for copy in g_copies(i):
            copy.start()

    for i in range(PIECES - pairs):
        give_grad(i)

    if not gathered:
        s1, q1, s2, q2, s3, q3, s4, q4 = rest[12:20]
        height = group.shape[-2]

    def put(g, value):
        at = pl.ds(0, value.shape[1])
        value = value.astype(LOW)
        if gathered:
            group[g, :, at] = value
        else:
            group[g, :, :, :, :, :, at] = value.reshape(depth, across, rows, cores, height, at.size)

    def span(g):
        return pl.ds(0, PAIR) if isinstance(g, int) and g == small_at else pl.ds(0, per)

    def hop_core(g):
        return remote(
            group.at[g, :, :, :, 1 - c, :, span(g)], n1.at[g, :, :, :, :, span(g)], s1.at[g], q1.at[g],
            device_at(dims, z, x, y, 1 - c),
        )

    def hop_x(g, dx):
        at = g * (across - 1) + dx - 1
        return remote(
            n1.at[g, :, (x + dx) % across, :, :, span(g)], n2.at[at, :, :, :, span(g)],
            s2.at[at], q2.at[at], device_at(dims, z, (x + dx) % across, y, c),
        )

    def hop_y(g, dy):
        at = g * (rows - 1) + dy - 1
        return remote(
            n2.at[g * (across - 1), :, (y + dy) % rows, :, span(g)], n3.at[at, :, :, span(g)],
            s3.at[at], q3.at[at], device_at(dims, z, x, (y + dy) % rows, c),
        )

    def hop_z(g, dz):
        at = g * (depth - 1) + dz - 1
        return remote(
            n3.at[g * (rows - 1), (z + dz) % depth, :, span(g)], n4.at[at, :, span(g)],
            s4.at[at], q4.at[at], device_at(dims, (z + dz) % depth, x, y, c),
        )

    def start(g):
        if not gathered:
            hop_core(g).start()

    def begin(g):
        if gathered:
            return
        hop_core(g).wait_recv()
        w = span(g)
        n1[g, :, :, :, :, w] = (
            group[g, :, :, :, c, :, w].astype(F32) + n1[g, :, :, :, :, w].astype(F32)
        ).astype(LOW)
        for dx in range(1, across):
            hop_x(g, dx).start()

    def middle_of(g):
        if gathered:
            return
        w = span(g)
        at = g * (across - 1)
        acc = n1[g, :, x, :, :, w].astype(F32)
        for dx in range(1, across):
            hop_x(g, dx).wait_recv()
            acc = acc + n2[at + dx - 1, :, :, :, w].astype(F32)
        n2[at, :, :, :, w] = acc.astype(LOW)
        for dy in range(1, rows):
            hop_y(g, dy).start()

    def end(g):
        if gathered:
            return
        w = span(g)
        at = g * (rows - 1)
        for dy in range(1, rows):
            hop_y(g, dy).wait_recv()
        acc = n2[g * (across - 1), :, y, :, w].astype(F32)
        for dy in range(1, rows):
            acc = acc + n3[at + dy - 1, :, :, w].astype(F32)
        n3[at, :, :, w] = acc.astype(LOW)
        for dz in range(1, depth):
            hop_z(g, dz).start()

    def last(g):
        w = span(g)
        acc = n3[g * (rows - 1), z, :, w].astype(F32)
        for dz in range(1, depth):
            hop_z(g, dz).wait_recv()
            acc = acc + n4[g * (depth - 1) + dz - 1, :, w].astype(F32)
        return acc

    sums[...] = jnp.zeros_like(sums)
    slot_a, slot_b = slots[:, 0:1], slots[:, 1:2]
    slot_at = lax.broadcasted_iota(jnp.int32, (count, wide * stride), 1)
    third = PAIR // 4
    lane_at = lax.broadcasted_iota(jnp.int32, (stride, PAIR), 1)

    def split(w, carry):
        value = column_of(gate_slots[w])[0:stride]
        high = value.astype(LOW).astype(F32)
        mid = (value - high).astype(LOW).astype(F32)
        low = value - high - mid
        row = jnp.where(lane_at == w, high, 0.0) + jnp.where(lane_at == third + w, mid, 0.0)
        parts[w] = (row + jnp.where(lane_at == 2 * third + w, low, 0.0)).astype(LOW)
        return carry

    lax.fori_loop(0, wide, split, 0)
    picks = jnp.where((slot_at == slot_a) | (slot_at == slot_b), 1.0, 0.0).astype(LOW)
    picked = dot(picks, parts[...].reshape(wide * stride, PAIR))
    prob_grad = picked + pltpu.roll(picked, PAIR - third, 1) + pltpu.roll(picked, PAIR - 2 * third, 1)
    own = probs[...]
    prob_grad = jnp.where(lanes < experts, prob_grad, 0.0)
    logit_grad = (own * (prob_grad - jnp.sum(prob_grad * own, axis=1, keepdims=True))).astype(LOW)
    router[...] = dot(moe_low_t[...], logit_grad)
    moe_grad = dot(picks, token_rows[...].reshape(wide * stride, model)) + dot_nt(
        logit_grad, weights[:, 4 * model : 4 * model + PAIR]
    )
    xhat, scale = norm_parts(middle[...])
    sums[5:6] = jnp.sum(moe_grad * xhat, axis=0, keepdims=True)
    sums[6:7] = jnp.sum(moe_grad, axis=0, keepdims=True)
    mid = cotangent[...].astype(F32) + norm_back(moe_grad, vecs[5:6], xhat, scale)
    middle_grad[...] = mid
    branch[...] = mid.astype(LOW)
    sums[4:5] = jnp.sum(branch[...].astype(F32), axis=0, keepdims=True)
    for g in range(n_proj):
        put(g, dot(attended_t[...], branch[:, g * per : (g + 1) * per]))
        start(g)
    begin(0)

    sides = lax.broadcasted_iota(jnp.int32, (PAIR, count), 0)

    def attend(pair, carry):
        at = lambda which: pl.ds(pl.multiple_of(which * model + pair * PAIR, PAIR), PAIR)
        here = at(0)
        grad_mixed = dot_nt(branch[...], weights[here, 3 * model : 4 * model]).astype(LOW)
        q_pair, k_pair, v_pair = queries[:, here], keys[:, here], values[:, here]
        k_turned = jnp.transpose(k_pair)
        q_grad_t, k_grad, v_grad = None, None, None
        for part in range(2):
            side = (lanes < HEAD) if part == 0 else (lanes >= HEAD)
            side_t = (sides < HEAD) if part == 0 else (sides >= HEAD)
            own_keys = jnp.where(side, k_pair, LOW(0))
            own_values = jnp.where(side, v_pair, LOW(0))
            own_queries = jnp.where(side, q_pair, LOW(0))
            own_grads = jnp.where(side, grad_mixed, LOW(0))
            own_turned = jnp.where(side_t, k_turned, LOW(0))
            scores = dot_nt(own_keys, q_pair) + bias[...]
            attn = jnp.exp(scores - lse_rows[pl.ds(2 * pair + part, 1), :])
            attn_grad = dot_nt(own_values, grad_mixed)
            mean = jnp.sum(attn * attn_grad, axis=0, keepdims=True)
            score_grad = (attn * (attn_grad - mean)).astype(LOW)
            v_part = dot(attn.astype(LOW), own_grads)
            k_part = dot(score_grad, own_queries)
            q_part = dot(own_turned, score_grad)
            if part == 0:
                q_grad_t, k_grad, v_grad = q_part, k_part, v_part
            else:
                q_grad_t, k_grad, v_grad = q_grad_t + q_part, k_grad + k_part, v_grad + v_part
        q_grad = (jnp.transpose(q_grad_t) * HEAD**-0.5).astype(LOW)
        k_grad = k_grad.astype(LOW)
        v_grad = v_grad.astype(LOW)
        sums[2:3, here] = jnp.sum(q_grad.astype(F32), axis=0, keepdims=True)
        sums[3:4, here] = jnp.sum(v_grad.astype(F32), axis=0, keepdims=True)
        g = pair + n_proj
        for which, part in enumerate((q_grad, k_grad, v_grad)):
            qkv_grad[:, at(which)] = part
        put(g, dot(normed_t[...], jnp.concatenate([q_grad, k_grad, v_grad], axis=1)))
        start(g)
        lax.fori_loop(wide - 1 - pairs + pair, wide - pairs + pair, give, 0)
        give_grad(PIECES - pairs + pair)
        if not gathered:
            begin(g - 1)

            @pl.when(g >= 3)
            def _():
                middle_of(g - 3)

            @pl.when(g >= 4)
            def _():
                end(g - 4)

        return carry

    lax.fori_loop(0, pairs, attend, 0)
    begin(small_at - 1)
    grad = dot_nt(qkv_grad[...], weights[:, : 3 * model])
    xhat, scale = norm_parts(tokens[...].astype(F32))
    sums[0:1] = jnp.sum(grad * xhat, axis=0, keepdims=True)
    sums[1:2] = jnp.sum(grad, axis=0, keepdims=True)
    stacked = jnp.concatenate([sums[...], jnp.zeros((PAIR - 8, model), F32)], axis=0)
    turned = pltpu.roll(jnp.transpose(stacked), experts, 1)
    wide_lanes = lax.broadcasted_iota(jnp.int32, (model, PAIR), 1)
    put(small_at, jnp.where(wide_lanes < experts, router[...], turned))
    start(small_at)
    middle_of(small_at - 3)
    end(small_at - 4)
    tokens_grad[...] = (middle_grad[...] + norm_back(grad, vecs[0:1], xhat, scale)).astype(LOW)
    begin(small_at)
    middle_of(small_at - 2)
    end(small_at - 3)
    middle_of(small_at - 1)
    middle_of(small_at)
    end(small_at - 2)
    end(small_at - 1)
    end(small_at)

    def taken(k, carry):
        d = k + 1
        y_copy(d, ahead_of(dims, d)).wait_send()
        y_copy(d, behind_of(dims, d)).wait_recv()
        return carry

    lax.fori_loop(0, wide - 1, taken, 0)
    keep_y.wait()
    returned = y_here[...].reshape(wide * stride, model)
    mixed = gates[:, 0:1] * dot(jnp.where(slot_at == slot_a, 1.0, 0.0).astype(LOW), returned)
    mixed += gates[:, 1:2] * dot(jnp.where(slot_at == slot_b, 1.0, 0.0).astype(LOW), returned)
    block_out[...] = (middle[...] + mixed).astype(LOW)
    if not gathered:
        for g in range(n_proj):
            out_proj[:, g * per : (g + 1) * per] = last(g)
        for pair in range(pairs):
            summed = last(n_proj + pair)
            for which in range(3):
                at = which * model + pair * PAIR
                out_qkv[:, at : at + PAIR] = summed[:, which * PAIR : (which + 1) * PAIR]
        summed = last(small_at)
        square = jnp.concatenate([summed, jnp.zeros((PAIR - height, PAIR), F32)], axis=0)
        turned = jnp.transpose(square)
        out_router[...] = turned[0:experts, 0:height]
        for i, ref in enumerate(out_vecs):
            ref[...] = turned[experts + i : experts + i + 1, 0:height]
        for g in range(small_at + 1):
            hop_core(g).wait_send()
            for dx in range(1, across):
                hop_x(g, dx).wait_send()
            for dy in range(1, rows):
                hop_y(g, dy).wait_send()
            for dz in range(1, depth):
                hop_z(g, dz).wait_send()
    for i in range(PIECES):
        for copy in g_copies(i):
            copy.wait()


def back_stage(
    dims, used, experts, gathered, tokens, saved, params, slots, token_rows, gate_slots, cotangent, y_rows, side_grads,
):
    depth, across, rows, cores = dims
    wide, narrow = depth * across, rows * cores
    count, model = tokens.shape
    stride = y_rows.shape[1]
    per = 3 * PAIR
    groups = model // per + model // PAIR + 1
    height = model // (wide * narrow)
    any_, vmem = pl.BlockSpec(memory_space=pl.ANY), pl.BlockSpec(memory_space=pltpu.VMEM)
    low = lambda *shape: jax.ShapeDtypeStruct(shape, LOW)
    f32 = lambda *shape: jax.ShapeDtypeStruct(shape, F32)
    sem = lambda size: [pltpu.SemaphoreType.DMA((size,))] * 2
    outs = [low(count, model), low(count, model), low(rows - 1, *side_grads[0].shape)]
    buffers, sems = [], []
    if gathered:
        outs.append(low(groups, model, per))
    else:
        outs += [f32(height, 3 * model), f32(height, model), f32(experts, height), *[f32(1, height)] * 7]
        buffers = [
            pltpu.VMEM((groups, depth, across, rows, cores, height, per), LOW),
            pltpu.VMEM((groups, depth, across, rows, height, per), LOW),
            pltpu.VMEM((groups * (across - 1), depth, rows, height, per), LOW),
            pltpu.VMEM((groups * (rows - 1), depth, height, per), LOW),
            pltpu.VMEM((groups * (depth - 1), height, per), LOW),
        ]
        sems = [
            *sem(groups), *sem(groups * (across - 1)), *sem(groups * (rows - 1)), *sem(groups * (depth - 1)),
        ]
    return pl.pallas_call(
        functools.partial(back_kernel, dims, used, experts, gathered),
        out_shape=tuple(outs),
        in_specs=[vmem] * 8 + [any_] + [vmem] * 10 + [any_] * rows,
        out_specs=[vmem] * 2 + [any_] + [vmem] * (len(outs) - 3),
        scratch_shapes=[
            *buffers,
            pltpu.VMEM((count, model), LOW),
            pltpu.VMEM((count, model), F32),
            pltpu.VMEM((count, 3 * model), LOW),
            pltpu.VMEM((8, model), F32),
            pltpu.VMEM((model, PAIR), F32),
            pltpu.VMEM((wide, stride, PAIR), LOW),
            pltpu.VMEM((wide, stride, model), LOW),
            *sem(wide), *sem((rows - 1) * PIECES),
            pltpu.SemaphoreType.DMA((1,)),
            *sems,
        ],
        compiler_params=pltpu.CompilerParams(
            collective_id=1, has_side_effects=True, vmem_limit_bytes=60 * 1024 * 1024
        ),
        cost_estimate=pl.CostEstimate(flops=16 * 10**9, bytes_accessed=40 * 10**6, transcendentals=4 * 10**6),
        name="back_stage",
    )(
        tokens, *saved, params, slots, token_rows, gate_slots, cotangent, y_rows, *side_grads
    )


def tail_kernel(count, *refs):
    inputs, own, other_out, refs = refs[:count], refs[count], refs[count + 1], refs[count + 2 :]
    rows = other_out.shape[0] + 1
    other_in, refs = refs[: rows - 1], refs[rows - 1 :]
    outputs, grad_in, grad_out = refs[:count], refs[count], refs[count + 1]
    terms, first, second, sems, loads, brings = refs[count + 2 : count + 8]
    held = refs[count + 8 :]
    arrivals = [pltpu.make_async_copy(own, terms.at[0], loads.at[0])]
    for i in range(1, rows):
        arrivals.append(pltpu.make_async_copy(other_in[i - 1], terms.at[i, 0], loads.at[2 * i - 1]))
        arrivals.append(pltpu.make_async_copy(other_out.at[i - 1], terms.at[i, 1], loads.at[2 * i]))
    bring = [pltpu.make_async_copy(src, dst, brings.at[i]) for i, (src, dst) in enumerate(zip(inputs, held))]
    copies = [pltpu.make_async_copy(src, dst, sems.at[i]) for i, (src, dst) in enumerate(zip(held, outputs))]
    for copy in bring + arrivals:
        copy.start()
    for into, out in zip(bring, copies):
        into.wait()
        out.start()
    for copy in arrivals:
        copy.wait()

    def total(which):
        acc = terms[0, which].astype(F32)
        for i in range(1, rows):
            acc = acc + terms[i, which].astype(F32)
        return acc

    first[0] = total(0)
    copies.append(pltpu.make_async_copy(first, grad_in, sems.at[count]))
    copies[-1].start()
    second[0] = jnp.transpose(total(1))
    copies.append(pltpu.make_async_copy(second, grad_out, sems.at[count + 1]))
    copies[-1].start()
    for copy in copies:
        copy.wait()


def tail_stage(arrays, own, other_out, other_in):
    any_ = pl.BlockSpec(memory_space=pl.ANY)
    _, model, ff = own.shape
    count = len(arrays)
    shapes = [jax.ShapeDtypeStruct(a.shape, a.dtype) for a in arrays]
    shapes += [jax.ShapeDtypeStruct((1, model, ff), F32), jax.ShapeDtypeStruct((1, ff, model), F32)]
    rows = other_out.shape[0] + 1
    return pl.pallas_call(
        functools.partial(tail_kernel, count),
        out_shape=tuple(shapes),
        in_specs=[any_] * (count + 1 + rows),
        out_specs=[any_] * (count + 2),
        scratch_shapes=[
            pltpu.VMEM((rows, 2, model, ff), LOW),
            pltpu.VMEM((1, model, ff), F32),
            pltpu.VMEM((1, ff, model), F32),
            pltpu.SemaphoreType.DMA((count + 2,)),
            pltpu.SemaphoreType.DMA((2 * rows - 1,)),
            pltpu.SemaphoreType.DMA((count,)),
            *[pltpu.VMEM(a.shape, a.dtype) for a in arrays],
        ],
        compiler_params=pltpu.CompilerParams(vmem_limit_bytes=58 * 1024 * 1024),
        name="results",
    )(*arrays, own, other_out, *other_in)


def gelu_and_slope(v):
    root = 0.7978845608028654
    cubic = 0.044715
    square = v * v
    half = 0.5 * jnp.tanh(v * (root + (root * cubic) * square)) + 0.5
    value = v * half
    slope = half + value * ((1.0 - half) * (2.0 * root + (6.0 * root * cubic) * square))
    return value, slope


def moe_kernel(
    dims, used, moe_low, slot_rows, slot_cols, gates, ups, b_in, b_out, w_in, w_out, *rest
):
    depth, across, rows, cores = dims
    wide = depth * across
    narrow = rows * cores
    side_out = rest[: rows - 1]
    rest = rest[rows - 1 :]
    token_rows, gate_slots, y_out, in_bias_grad, out_bias_grad = rest[:5]
    own_grad = rest[5]
    side_in, side_grad = rest[6 : 5 + rows], rest[5 + rows : 4 + 2 * rows]
    (
        full_in, full_out, x_send, x_here, g_send, g_here, dx_send, h_send, hidden, pre_grad, weighted,
        x_turned, w_turned, grad_send, grad_here, extra, extra_here, extra_y, blank, dx_part, back_part,
        local, blanks, s_wy, r_wy, s_y, r_y, s_ey, r_ey, s_in, r_in, s_out, r_out, s_x, r_x, s_g, r_g, s_dx, r_dx, s_h, r_h, s_w, r_w, s_e, r_e,
    ) = rest[4 + 2 * rows :]
    z, x, y, c = place_of(dims)
    me, n = z * across + x, y * cores + c
    count, model = moe_low.shape
    capacity = x_send.shape[1]
    gate_width = g_send.shape[2]
    ff = full_in.shape[2]
    other = device_at(dims, z, x, y, 1 - c)

    def remote(src, dst, ssem, rsem, to):
        return pltpu.make_async_remote_copy(
            src_ref=src, dst_ref=dst, send_sem=ssem, recv_sem=rsem, device_id=to, device_id_type=MESH
        )

    along_y = [device_at(dims, z, x, (y + i) % rows, c) for i in range(1, rows)]
    body = pl.ds(0, used)
    if used < capacity:
        x_here[:, used:capacity] = jnp.zeros((wide, capacity - used, model), LOW)
        blank[...] = jnp.zeros_like(blank)
    greet([((me + d) % wide, n) for d in range(1, wide)] + [other] + along_y)
    fills = []
    if used < capacity:
        for w in range(wide):
            fills.append(pltpu.make_async_copy(blank, token_rows.at[w, pl.ds(used, capacity - used)], blanks.at[w]))

    held = [((y - i) % rows) * cores + c for i in range(rows)]
    from_y, in_passes, out_loads, out_passes = [], [], [], []
    for i, h in enumerate(held):
        src_out = w_out.at[0] if i == 0 else side_out[i - 1].at[0]
        out_loads.append(pltpu.make_async_copy(src_out, full_out.at[h], local.at[i]))
        out_passes.append(remote(src_out, full_out.at[h], s_out.at[i], r_out.at[i], other))
        if i:
            from_y.append(remote(w_in.at[0], full_in.at[n], s_wy.at[i - 1], r_wy.at[i - 1], along_y[i - 1]))
        src_in = w_in.at[0] if i == 0 else full_in.at[h]
        in_passes.append(remote(src_in, full_in.at[h], s_in.at[i], r_in.at[i], other))
    in_load = pltpu.make_async_copy(w_in.at[0], full_in.at[n], local.at[rows])
    for copy in from_y + out_loads + out_passes:
        copy.start()

    slot_a, slot_b = slot_cols[:, 0:1], slot_cols[:, 1:2]
    gate_a, gate_b = gates[:, 0:1], gates[:, 1:2]
    row_at = lax.broadcasted_iota(jnp.int32, (capacity, count), 0)
    lane_at = lax.broadcasted_iota(jnp.int32, (count, gate_width), 1)
    source = moe_low[...]

    def rows_for(expert):
        first = expert * capacity
        hit = (slot_rows[0:1] - first == row_at) | (slot_rows[1:2] - first == row_at)
        picked = dot(jnp.where(hit, 1.0, 0.0).astype(LOW), source).astype(LOW)
        inside = lane_at < capacity
        hit_a = (slot_a - first == lane_at) & inside
        hit_b = (slot_b - first == lane_at) & inside
        gate = jnp.where(hit_a, gate_a, 0.0) + jnp.where(hit_b, gate_b, 0.0)
        return picked, jnp.sum(gate, axis=0, keepdims=True)

    def x_copy(d, to):
        return remote(x_send.at[to, body], x_here.at[me, body], s_x.at[d], r_x.at[d], (to, n))

    def g_copy(d, to):
        return remote(g_send.at[to], g_here.at[me], s_g.at[d], r_g.at[d], (to, n))

    def dx_copy(d, to):
        return remote(dx_send.at[to, body], token_rows.at[me, body], s_dx.at[d], r_dx.at[d], (to, n))

    def h_copy(d, to):
        return remote(h_send.at[to], gate_slots.at[me], s_h.at[d], r_h.at[d], (to, n))

    def dispatch(k, carry):
        d = (k + wide // 2 - 1) % (wide - 1) + 1
        to = ahead_of(dims, d)
        picked, gate = rows_for(to)
        x_send[to] = picked
        g_send[to] = gate
        x_copy(d, to).start()
        g_copy(d, to).start()
        return carry

    lax.fori_loop(0, wide - 1, dispatch, 0)
    in_load.start()
    in_passes[0].start()
    for copy in fills:
        copy.start()
    picked, gate = rows_for(me)
    x_here[me] = picked
    g_here[me] = gate
    extra[...] = jnp.zeros_like(extra)
    out_bias = b_out[...].astype(F32)
    for copy in out_loads:
        copy.wait()

    def backs_of(places):
        def backs(k, carry):
            two = pl.ds(2 * k, 2)
            up = ups[two].reshape(2 * capacity, model)
            for h in places:
                lanes = pl.ds(pl.multiple_of(h * ff, PAIR), ff)
                pre_grad[two, :, lanes] = dot_nt(up, full_out[h]).astype(LOW).reshape(2, capacity, ff)
            return carry

        return backs

    lax.fori_loop(0, wide // 2, backs_of([i * cores + c for i in range(rows)]), 0)
    for copy in out_passes:
        copy.wait_recv()
    lax.fori_loop(0, wide // 2, backs_of([i * cores + 1 - c for i in range(rows)]), 0)
    in_load.wait()
    in_passes[0].wait_recv()

    def expert(src, places, slot=None, first=True, final=True):
        own = x_here[src]
        up = ups[src]
        gate = jnp.transpose(jnp.broadcast_to(g_here[src], (PAIR, gate_width)))[:capacity, 0:1]
        if first:
            weighted[src] = (gate * up.astype(F32)).astype(LOW)
            back_total = jnp.sum(up.astype(F32) * out_bias, axis=1, keepdims=True)
            dx = None
        else:
            back_total = back_part[slot, :, 0:1]
            dx = dx_part[slot]
        for h in places:
            lanes = pl.ds(h * ff if isinstance(h, int) else pl.multiple_of(h * ff, PAIR), ff)
            pre = dot(own, full_in[h]) + b_in[h]
            back = pre_grad[src, :, lanes].astype(F32)
            value, slope = gelu_and_slope(pre)
            hidden[src, :, lanes] = value.astype(LOW)
            back_total += jnp.sum(value * back, axis=1, keepdims=True)
            wide_grad = slope * (gate * back)
            grad = wide_grad.astype(LOW)
            pre_grad[src, :, lanes] = grad
            extra[h, 0:1, :ff] += jnp.sum(wide_grad, axis=0, keepdims=True)
            part = dot_nt(grad, full_in[h])
            dx = part if dx is None else dx + part
        if final:
            dx_send[src] = dx.astype(LOW)
            spread = jnp.broadcast_to(back_total, (capacity, PAIR))
            spread = jnp.concatenate([spread, jnp.zeros((gate_width - capacity, PAIR), F32)], axis=0)
            h_send[src] = jnp.transpose(spread)[0:1]
        else:
            dx_part[slot] = dx
            back_part[slot] = jnp.broadcast_to(back_total, (capacity, PAIR))

    def source_of(k):
        d = (k + wide // 2 - 1) % (wide - 1) + 1
        return d, behind_of(dims, d)

    def land(k):
        d, src = source_of(k)
        x_copy(d, src).wait_recv()
        g_copy(d, src).wait_recv()
        return src

    def give_back(k):
        d, src = source_of(k)
        dx_copy(d, src).start()
        h_copy(d, src).start()

    near = [y * cores + i for i in range(cores)]
    far = [(y + i) % rows * cores + j for i in range(1, rows) for j in range(cores)]
    early = dx_part.shape[0] - 1
    expert(me, near, 0, final=False)

    def begin(k, carry):
        expert(land(k), near, k + 1, final=False)
        return carry

    lax.fori_loop(0, early, begin, 0)
    for i in range(1, rows):
        from_y[i - 1].wait_recv()
        in_passes[i].start()
    for copy in in_passes[1:]:
        copy.wait_recv()

    def complete(k, carry):
        expert(source_of(k)[1], far, k + 1, first=False)
        return carry

    def serve(k, carry):
        expert(land(k), range(narrow))
        give_back(k - early)
        return carry

    lax.fori_loop(0, early, complete, 0)
    expert(me, far, 0, first=False)
    keep_rows = pltpu.make_async_copy(dx_send.at[me, body], token_rows.at[me, body], local.at[2 * rows])
    keep_gate = pltpu.make_async_copy(h_send.at[me], gate_slots.at[me], local.at[2 * rows + 1])
    keep_rows.start()
    keep_gate.start()
    lax.fori_loop(early, wide - 1, serve, 0)

    def give_rest(k, carry):
        give_back(k)
        return carry

    lax.fori_loop(wide - 1 - early, wide - 1, give_rest, 0)

    all_rows = wide * capacity
    x_turned[...] = jnp.transpose(x_here[...].reshape(all_rows, model))
    w_turned[...] = jnp.transpose(weighted[...].reshape(all_rows, model))
    bias_grad = jnp.sum(weighted[...].reshape(all_rows, model).astype(F32), axis=0, keepdims=True)
    for h in range(narrow):
        extra[h, 1:2] = bias_grad

    def grad_of(which, h):
        lanes = pl.ds(pl.multiple_of(h * ff, PAIR), ff)
        if which == 0:
            return dot(x_turned[...], pre_grad[:, :, lanes].reshape(all_rows, ff))
        return dot(w_turned[...], hidden[:, :, lanes].reshape(all_rows, ff))

    order = [*range(1, rows), 0]
    swaps, by_y, keep_grads = [], [], []
    for i in order:
        at = (y + i) % rows
        kept, given = at * cores + c, at * cores + 1 - c
        for which in range(2):
            k = 2 * i + which
            grad_send[i, which] = grad_of(which, given).astype(LOW)
            swap = remote(grad_send.at[i, which], grad_here.at[i, which], s_w.at[k], r_w.at[k], other)
            swap.start()
            swaps.append(swap)
            if which == 0:
                swap_extra = remote(extra.at[given], extra_here.at[i], s_e.at[i], r_e.at[i], other)
                swap_extra.start()
                swaps.append(swap_extra)
            grad = grad_of(which, kept)
            swap.wait_recv()
            grad_here[i, which] = (grad + grad_here[i, which].astype(F32)).astype(LOW)
            if which == 0:
                swap_extra.wait_recv()
                extra_here[i] = extra_here[i] + extra[kept]
            if i and which == 0:
                by_y.append(
                    remote(grad_here.at[i, 0], side_in[i - 1], s_y.at[i - 1], r_y.at[i - 1], along_y[i - 1])
                )
                by_y[-1].start()
                by_y.append(
                    remote(extra_here.at[i], extra_y.at[i - 1], s_ey.at[i - 1], r_ey.at[i - 1], along_y[i - 1])
                )
                by_y[-1].start()
        source, target = (grad_here.at[i, 1], side_grad[i - 1]) if i else (grad_here.at[0], own_grad)
        keep_grads.append(pltpu.make_async_copy(source, target, local.at[2 * rows + 3 + i]))
        keep_grads[-1].start()

    some = 4

    def outputs(k, carry):
        total = None
        at = pl.ds(k * some, some)
        for h in range(narrow):
            part = dot(hidden[at, :, h * ff : (h + 1) * ff].reshape(some * capacity, ff), full_out[h])
            total = part if total is None else total + part
        x_send[at] = (total + out_bias).astype(LOW).reshape(some, capacity, model)
        return carry

    def sent(k, carry):
        to = ahead_of(dims, k + 1)
        x_copy(k + 1, to).wait_send()
        g_copy(k + 1, to).wait_send()
        return carry

    lax.fori_loop(0, wide - 1, sent, 0)
    lax.fori_loop(0, wide // some, outputs, 0)
    keep_y = pltpu.make_async_copy(x_send, y_out, local.at[2 * rows + 2])
    keep_y.start()
    bias_rows = extra_here[0]
    for copy in by_y:
        copy.wait_recv()
    for i in range(1, rows):
        bias_rows = bias_rows + extra_y[i - 1]
    in_bias_grad[...] = bias_rows[0:1, :ff]
    out_bias_grad[...] = bias_rows[1:2]

    def finish(k, carry):
        d = k + 1
        back = behind_of(dims, d)
        dx_copy(d, back).wait_recv()
        h_copy(d, back).wait_recv()
        dx_copy(d, back).wait_send()
        h_copy(d, back).wait_send()
        return carry

    lax.fori_loop(0, wide - 1, finish, 0)
    for copy in from_y + in_passes + out_passes + swaps + by_y:
        copy.wait_send()
    for copy in fills:
        copy.wait()
    for copy in [keep_rows, keep_gate, keep_y] + keep_grads:
        copy.wait()


def moe_stage(dims, used, capacity, moe_low, slot_rows, slots, gates, ups, b_in, b_out, w_in, w_out, side_out):
    depth, across, rows, cores = dims
    wide, narrow = depth * across, rows * cores
    count, model = moe_low.shape
    ff = w_in.shape[2]
    gate_width = -(-capacity // PAIR) * PAIR
    any_, vmem = pl.BlockSpec(memory_space=pl.ANY), pl.BlockSpec(memory_space=pltpu.VMEM)
    low = lambda *shape: jax.ShapeDtypeStruct(shape, LOW)
    f32 = lambda *shape: jax.ShapeDtypeStruct(shape, F32)
    sem = lambda size: [pltpu.SemaphoreType.DMA((size,))] * 2
    outs = pl.pallas_call(
        functools.partial(moe_kernel, dims, used),
        out_shape=(
            low(wide, capacity, model), f32(wide, 1, gate_width), low(wide, capacity, model),
            f32(1, ff), f32(1, model), low(2, model, ff), *[low(model, ff)] * (2 * rows - 2),
        ),
        in_specs=[vmem] * 7 + [any_] * (1 + rows),
        out_specs=[any_] * 3 + [vmem] * 2 + [any_] * (2 * rows - 1),
        scratch_shapes=[
            pltpu.VMEM((narrow, model, ff), LOW),
            pltpu.VMEM((narrow, ff, model), LOW),
            pltpu.VMEM((wide, capacity, model), LOW),
            pltpu.VMEM((wide, capacity, model), LOW),
            pltpu.VMEM((wide, 1, gate_width), F32),
            pltpu.VMEM((wide, 1, gate_width), F32),
            pltpu.VMEM((wide, capacity, model), LOW),
            pltpu.VMEM((wide, 1, gate_width), F32),
            pltpu.VMEM((wide, capacity, narrow * ff), LOW),
            pltpu.VMEM((wide, capacity, narrow * ff), LOW),
            pltpu.VMEM((wide, capacity, model), LOW),
            pltpu.VMEM((model, wide * capacity), LOW),
            pltpu.VMEM((model, wide * capacity), LOW),
            pltpu.VMEM((rows, 2, model, ff), LOW),
            pltpu.VMEM((rows, 2, model, ff), LOW),
            pltpu.VMEM((narrow, 8, model), F32),
            pltpu.VMEM((rows, 8, model), F32),
            pltpu.VMEM((rows - 1, 8, model), F32),
            pltpu.VMEM((max(capacity - used, 8), model), LOW),
            pltpu.VMEM((1 + min(EARLY, wide - 1), capacity, model), F32),
            pltpu.VMEM((1 + min(EARLY, wide - 1), capacity, PAIR), F32),
            pltpu.SemaphoreType.DMA((3 * rows + 3,)),
            pltpu.SemaphoreType.DMA((wide,)),
            *sem(rows), *sem(rows), *sem(rows), *sem(rows), *sem(rows), *sem(wide), *sem(wide), *sem(wide), *sem(wide), *sem(2 * rows), *sem(rows),
        ],
        compiler_params=pltpu.CompilerParams(
            collective_id=2, has_side_effects=True, vmem_limit_bytes=60 * 1024 * 1024
        ),
        cost_estimate=pl.CostEstimate(flops=36 * 10**9, bytes_accessed=25 * 10**6, transcendentals=4 * 10**6),
        name="moe_stage",
    )(moe_low, slot_rows, slots, gates, ups, b_in, b_out, w_in, w_out, *side_out)
    return outs[:3], outs[3:5], outs[5], outs[6 : 5 + rows], outs[5 + rows :]


def per_device(
    dims,
    tokens, segment_ids, patch_valid, routes, priority, gain_attn, shift_attn, w_qkv, query_bias, value_bias,
    w_proj, proj_bias, gain_moe, shift_moe, w_router, w_in, in_bias, w_out, out_bias, cotangent,
):
    count, model = tokens.shape
    experts = w_router.shape[1]
    capacity = (210 * count + 100 * experts - 1) // (100 * experts)
    shard_rows = gain_attn.shape[0]
    vectors = jnp.stack([gain_attn, shift_attn, query_bias, value_bias, proj_bias, gain_moe, shift_moe])
    stride = -(-capacity // 16) * 16
    gathered = shard_rows % 8 != 0
    every = ("wide", "narrow")
    if gathered:
        empty = jnp.zeros((shard_rows, PAIR - 7 - experts), LOW)
        pack = jnp.concatenate([w_qkv, w_proj, w_router, jnp.transpose(vectors), empty], axis=1)
        pack = [lax.all_gather(pack, every, axis=0, tiled=True)]
    else:
        pack = [w_qkv, w_proj, jnp.transpose(w_router), vectors]
    params, saved, (slots, slot_rows, full_b_in, ups), side_out = front_stage(
        dims, experts, capacity, stride, gathered, pack, tokens, segment_ids, patch_valid, routes, priority,
        cotangent, w_out, in_bias,
    )
    moe_low, gates = saved[7], saved[10]
    used = -(-capacity // 8) * 8
    (token_rows, gate_slots, y_rows), bias_grads, own_grad, other_in, side_grads = moe_stage(
        dims, used, stride, moe_low, slot_rows, slots, gates, ups, full_b_in, out_bias, w_in, w_out, side_out
    )
    outs = back_stage(
        dims, used, experts, gathered, tokens, saved, params, slots, token_rows, gate_slots, cotangent, y_rows, side_grads,
    )
    settled = tail_stage([*outs[:2], *outs[3:], *bias_grads], own_grad, outs[2], other_in)
    outs, (grad_in_bias, grad_out_bias, grad_w_in, grad_w_out) = settled[:-4], settled[-4:]
    block_out, tokens_grad = outs[:2]
    if gathered:
        groups = lax.psum_scatter(outs[2].astype(F32), every, scatter_dimension=1, tiled=True)
        n_proj = model // (3 * PAIR)
        grad_proj = jnp.concatenate(list(groups[:n_proj]), axis=1)
        by_head = groups[n_proj:-1].reshape(-1, shard_rows, 3, PAIR)
        grad_qkv = by_head.transpose(1, 2, 0, 3).reshape(shard_rows, -1)
        grad_router = groups[-1, :, :experts]
        vector = [groups[-1, :, experts + i] for i in range(7)]
    else:
        grad_qkv, grad_proj, grad_router = outs[2:5]
        grad_router = jnp.transpose(grad_router)
        vector = [row.reshape(-1) for row in outs[5:]]
    return (
        block_out,
        tokens_grad,
        vector[0],
        vector[1],
        grad_qkv,
        vector[2],
        vector[3],
        grad_proj,
        vector[4],
        vector[5],
        vector[6],
        grad_router,
        grad_w_in,
        grad_in_bias,
        grad_w_out,
        grad_out_bias,
    )


def solution(mesh):
    dims = grid_of(mesh.shape["wide"], mesh.shape["narrow"])
    every = ("wide", "narrow")
    rows, vector = P(every, None), P(every)
    return jax.shard_map(
        functools.partial(per_device, dims),
        mesh=mesh,
        in_specs=(
            rows, rows, rows, rows, rows, vector, vector, rows, vector, vector, rows, vector, vector, vector,
            rows, P("wide", None, "narrow"), P("wide", "narrow"), P("wide", "narrow", None), P("wide", None), rows,
        ),
        out_specs=(
            rows, rows, vector, vector, rows, vector, vector, rows, vector, vector, vector, rows,
            P("wide", None, "narrow"), P("wide", "narrow"), P("wide", "narrow", None), P("wide", None),
        ),
        check_vma=False,
    )
```

```python
import functools

import jax
import jax.numpy as jnp
from jax import lax
from jax.experimental import pallas as pl
from jax.experimental.pallas import tpu as pltpu
from jax.sharding import PartitionSpec as P

HEAD = 64
PAIR = 2 * HEAD
EPSILON = 1e-06
MASKED = -1000000000.0
MESH = pl.DeviceIdType.MESH
LOW = jnp.bfloat16
F32 = jnp.float32
PIECES = 8
EARLY = 2
VMEM_LIMIT = 58 * 1024 * 1024


def dot(a, b):
    return jnp.dot(a, b, preferred_element_type=F32)


def dot_nt(a, b):
    return lax.dot_general(a, b, (((1,), (1,)), ((), ())), preferred_element_type=F32)


def dot_tn(a, b):
    return lax.dot_general(a, b, (((0,), (0,)), ((), ())), preferred_element_type=F32)


def grid_of(wide, narrow):
    along_x = 1 << ((wide.bit_length() - 1) // 2)
    return wide // along_x, along_x, narrow // 2, 2


def place_of(dims):
    depth, across, rows, cores = dims
    wide, narrow = lax.axis_index("wide"), lax.axis_index("narrow")
    return wide // across, wide % across, narrow // cores, narrow % cores


def device_at(dims, z, x, y, c):
    depth, across, rows, cores = dims
    return (z * across + x, y * cores + c)


def ahead_of(dims, d):
    depth, across, rows, cores = dims
    z, x, y, c = place_of(dims)
    return (z + d // across) % depth * across + (x + d % across) % across


def behind_of(dims, d):
    depth, across, rows, cores = dims
    z, x, y, c = place_of(dims)
    return (z + depth - d // across) % depth * across + (x + across - d % across) % across


def greet(peers):
    barrier = pltpu.get_barrier_semaphore()
    for peer in peers:
        pl.semaphore_signal(barrier, inc=1, device_id=peer, device_id_type=MESH)
    pl.semaphore_wait(barrier, len(peers))


def neighbours(dims):
    depth, across, rows, cores = dims
    z, x, y, c = place_of(dims)
    peers = [device_at(dims, (z + d) % depth, x, y, c) for d in range(1, depth)]
    peers += [device_at(dims, z, (x + d) % across, y, c) for d in range(1, across)]
    peers += [device_at(dims, z, x, (y + d) % rows, c) for d in range(1, rows)]
    peers += [device_at(dims, z, x, y, 1 - c)]
    return peers


def norm_parts(values):
    center = jnp.mean(values, axis=-1, keepdims=True)
    offset = values - center
    spread = jnp.mean(offset * offset, axis=-1, keepdims=True)
    scale = lax.rsqrt(spread + EPSILON)
    return offset * scale, scale


def column_of(row):
    return jnp.transpose(jnp.broadcast_to(row, (PAIR, row.shape[1])))[:, 0:1]


def front_kernel(
    dims, experts, capacity, gathered, heads, *rest
):
    depth, across, rows, cores = dims
    wide, narrow = depth * across, rows * cores
    pack_refs, rest = rest[:heads], rest[heads:]
    tokens, seg_row, valid_row, routes, priority, cotangent, w_out, b_in = rest[:8]
    rest = rest[8:]
    (
        params, normed_t, q_out, k_out, v_out, attended_t, lse_rows, middle, moe_low, moe_low_t, probs_out, gates_out, vecs,
        bias_t, slots_out, slot_rows, full_b_in, ups,
    ) = rest[:18]
    side_out = rest[18 : 17 + rows]
    (
        normed, attended, total, bias, lse, up_send, b_send, shard, turn, blank,
        s1, r1, sx, rx, sy, ry, sa, ra, sb, rb, sc, rc, s_up, r_up, s_w, r_w, s_b, r_b, local, blanks,
    ) = rest[17 + rows :]
    z, x, y, c = place_of(dims)
    me, n = z * across + x, y * cores + c
    count, model = tokens.shape
    stride = ups.shape[1]
    lanes = lax.broadcasted_iota(jnp.int32, (count, PAIR), 1)

    def remote(src, dst, ssem, rsem, to):
        return pltpu.make_async_remote_copy(
            src_ref=src, dst_ref=dst, send_sem=ssem, recv_sem=rsem, device_id=to, device_id_type=MESH
        )

    def send(src, dst, ssem, rsem, to):
        copy = remote(src, dst, ssem, rsem, to)
        copy.start()
        return copy

    if not gathered:
        w_qkv, w_proj, router_t, vectors = pack_refs
        packs = [
            pltpu.make_async_copy(w_qkv, shard.at[:, pl.ds(0, 3 * model)], local.at[3]),
            pltpu.make_async_copy(w_proj, shard.at[:, pl.ds(3 * model, model)], local.at[4]),
        ]
        for copy in packs:
            copy.start()
        height = shard.shape[0]
        turn[...] = jnp.zeros_like(turn)
        turn[0:experts, 0:height] = router_t[...].astype(F32)
        turn[experts : experts + 7, 0:height] = vectors[...].astype(F32)
        shard[:, 4 * model : 4 * model + PAIR] = jnp.transpose(turn[...])[0:height].astype(LOW)
    b_send[...] = b_in[...].astype(F32)
    peers = [((me + d) % wide, n) for d in range(1, wide)]
    peers += [(me, (n + d) % narrow) for d in range(1, narrow)]
    greet(peers)
    if not gathered:
        for copy in packs:
            copy.wait()

    first, by_x, by_y, half_a, half_b, by_core = {}, {}, {}, {}, {}, {}
    keeps = []
    if not gathered:
        width = shard.shape[1]
        cut = (width // 256) * 128

        def block(dz, dx, dy, core):
            at = ((z - dz) % depth) * across + (x - dx) % across
            return params.at[(at * rows + (y - dy) % rows) * cores + core]

        own = block(0, 0, 0, c)
        keeps.append(pltpu.make_async_copy(shard, own, local.at[0]))
        keeps[-1].start()
        for dz in range(1, depth):
            first[dz] = send(
                shard, own, s1.at[dz - 1], r1.at[dz - 1], device_at(dims, (z + dz) % depth, x, y, c)
            )

    def to_core(dz, dx, dy):
        at = (dz * across + dx) * rows + dy
        src = shard if (dz, dx, dy) == (0, 0, 0) else block(dz, dx, dy, c)
        by_core[at] = send(
            src, block(dz, dx, dy, c), sc.at[at], rc.at[at], device_at(dims, z, x, y, 1 - c)
        )

    def spread(dz):
        if dz:
            first[dz].wait_recv()
        src = block(dz, 0, 0, c) if dz else shard
        for dx in range(1, across):
            at = dz * (across - 1) + dx - 1
            by_x[dz, dx] = send(
                src, block(dz, 0, 0, c), sx.at[at], rx.at[at],
                device_at(dims, z, (x + dx) % across, y, c),
            )
        for dy in range(1, rows):
            at = dz * (rows - 1) + dy - 1
            by_y[dz, dy] = send(
                src, block(dz, 0, 0, c), sy.at[at], ry.at[at],
                device_at(dims, z, x, (y + dy) % rows, c),
            )
        to_core(dz, 0, 0)

    def corner(dz):
        for dx in range(1, across):
            by_x[dz, dx].wait_recv()
            part = block(dz, dx, 0, c).at[:, pl.ds(0, cut)]
            for dy in range(1, rows):
                at = (dz * (across - 1) + dx - 1) * (rows - 1) + dy - 1
                half_a[dz, dx, dy] = send(
                    part, part, sa.at[at], ra.at[at], device_at(dims, z, x, (y + dy) % rows, c)
                )
            to_core(dz, dx, 0)
        for dy in range(1, rows):
            by_y[dz, dy].wait_recv()
            part = block(dz, 0, dy, c).at[:, pl.ds(cut, width - cut)]
            for dx in range(1, across):
                at = (dz * (across - 1) + dx - 1) * (rows - 1) + dy - 1
                half_b[dz, dx, dy] = send(
                    part, part, sb.at[at], rb.at[at], device_at(dims, z, (x + dx) % across, y, c)
                )
            to_core(dz, 0, dy)

    def finish(dz):
        for dx in range(1, across):
            for dy in range(1, rows):
                half_a[dz, dx, dy].wait_recv()
                half_b[dz, dx, dy].wait_recv()
                to_core(dz, dx, dy)

    if not gathered:
        spread(0)
    b_copies = []
    for d in range(1, narrow):
        b_copies.append(send(b_send, full_b_in.at[n], s_b.at[d], r_b.at[d], (me, (n + d) % narrow)))
    keeps.append(pltpu.make_async_copy(b_send, full_b_in.at[n], local.at[1]))
    keeps[-1].start()
    w_copies = []

    piece = w_out.shape[1] // PIECES

    def weight_piece(i):
        for dy in range(1, rows):
            at = (dy - 1) * PIECES + i
            part = pl.ds(i * piece, piece)
            to = device_at(dims, z, x, (y + dy) % rows, c)
            w_copies.append(send(w_out.at[:, part], side_out[dy - 1].at[:, part], s_w.at[at], r_w.at[at], to))

    used = -(-capacity // 8) * 8
    fills = []
    if used < stride:
        blank[...] = jnp.zeros_like(blank)
        for w in range(wide):
            fills.append(pltpu.make_async_copy(blank, ups.at[w, pl.ds(used, stride - used)], blanks.at[w]))
            fills[-1].start()

    half = PAIR // 2
    valid = valid_row[...].astype(F32)
    valid_col = column_of(valid)
    rank_row = priority[...].astype(F32)
    ahead = jnp.where(rank_row < column_of(rank_row), 1.0, 0.0).astype(LOW)
    first_at = column_of(routes[0:1].astype(F32)).astype(jnp.int32)
    second_at = column_of(routes[1:2].astype(F32)).astype(jnp.int32)
    hit_first, hit_second = lanes == first_at, lanes == second_at + half
    hot = jnp.where(hit_first | hit_second, valid_col, 0.0)
    earlier = dot(ahead, hot.astype(LOW))
    filled = pltpu.roll(jnp.sum(hot, axis=0, keepdims=True), half, 1)
    filled = jnp.broadcast_to(jnp.where(lanes[0:1] >= half, filled, 0.0), (8, PAIR))[0:1]
    earlier = earlier + filled
    place_a = jnp.sum(jnp.where(hit_first, earlier, 0.0), axis=1, keepdims=True).astype(jnp.int32)
    place_b = jnp.sum(jnp.where(hit_second, earlier, 0.0), axis=1, keepdims=True).astype(jnp.int32)
    kept_a = (place_a < capacity) & (valid_col > 0.5)
    kept_b = (place_b < capacity) & (valid_col > 0.5)
    slot_a = jnp.where(kept_a, first_at * stride + place_a, -1)
    slot_b = jnp.where(kept_b, second_at * stride + place_b, -1)
    slots = jnp.where(lanes == 0, slot_a, slot_b)
    slots_out[...] = jnp.where(lanes < 2, slots, jnp.where(lanes == 2, first_at, second_at))
    slot_rows[...] = jnp.transpose(slots.astype(F32))[0:8].astype(jnp.int32)


    row_at = lax.broadcasted_iota(jnp.int32, (stride, count), 0)

    def up_copy(d, to):
        body = pl.ds(0, used)
        return remote(up_send.at[to, body], ups.at[me, body], s_up.at[d], r_up.at[d], (to, n))

    def rows_for(expert):
        start = expert * stride
        hit = (slot_rows[0:1] - start == row_at) | (slot_rows[1:2] - start == row_at)
        return dot(jnp.where(hit, 1.0, 0.0).astype(LOW), cotangent[...]).astype(LOW)

    def give(d):
        to = ahead_of(dims, d)
        up_send[to] = rows_for(to)
        up_copy(d, to).start()

    def dispatch(k, carry):
        give(k + 1)
        return carry

    if not gathered:
        same_x = [(j + depth // 2 - 1) % (depth - 1) + 1 for j in range(depth - 1)]
        for step in range(1, depth):
            spread(step)
            corner(step - 1)
            if step >= 2:
                finish(step - 2)
        for j in same_x:
            give(across * j)
        corner(depth - 1)
        for i in range(PIECES):
            weight_piece(i)
        finish(depth - 2)
        finish(depth - 1)
        for j in [*same_x, 0]:
            for dx in range(1, across):
                give(across * j + dx)
    else:
        lax.fori_loop(0, wide - 1, dispatch, 0)
        keeps.append(pltpu.make_async_copy(pack_refs[0], params, local.at[0]))
        keeps[-1].start()
        for i in range(PIECES):
            weight_piece(i)
    segments = seg_row[...].astype(F32)
    keys_at = lax.broadcasted_iota(jnp.int32, (count, count), 1)
    rows_at = lax.broadcasted_iota(jnp.int32, (count, count), 0)
    allowed = (column_of(segments) == segments) & ((valid > 0.5) | (keys_at == rows_at))
    bias[...] = jnp.where(allowed, 0.0, MASKED)
    xhat, _ = norm_parts(tokens[...].astype(F32))
    total[...] = xhat
    lse[...] = jnp.zeros_like(lse)
    bias_t[...] = jnp.where(
        (column_of(segments) == segments) & ((valid_col > 0.5) | (keys_at == rows_at)), 0.0, MASKED
    )
    up_send[me] = rows_for(me)
    body = pl.ds(0, used)
    keep_up = pltpu.make_async_copy(up_send.at[me, body], ups.at[me, body], local.at[2])
    keep_up.start()
    for copy in by_core.values():
        copy.wait_recv()
    for copy in keeps:
        copy.wait()


    def columns(at):
        return params[:, at] if gathered else params[:, :, at].reshape(model, at.size)

    small = columns(pl.ds(4 * model, PAIR))
    vecs[...] = jnp.transpose(small.astype(F32))[experts : experts + 8]
    normed[...] = (total[...] * vecs[0:1] + vecs[1:2]).astype(LOW)

    def attend(pair, carry):
        at = lambda which: pl.ds(pl.multiple_of(which * model + pair * PAIR, PAIR), PAIR)
        here = at(0)
        source = normed[...]
        three = dot(source, jnp.concatenate([columns(at(0)), columns(at(1)), columns(at(2))], axis=1))
        queries = (three[:, :PAIR] + vecs[2:3, here]).astype(LOW) * LOW(HEAD**-0.5)
        keys = three[:, PAIR : 2 * PAIR].astype(LOW)
        values = (three[:, 2 * PAIR :] + vecs[3:4, here]).astype(LOW)
        q_out[:, here] = queries
        k_out[:, here] = keys
        v_out[:, here] = values
        mixed = None
        for part in range(2):
            side = (lanes < HEAD) if part == 0 else (lanes >= HEAD)
            own_keys = jnp.where(side, keys, LOW(0))
            own_values = jnp.where(side, values, LOW(0))
            scores = dot_nt(queries, own_keys) + bias[...]
            peak = jnp.max(scores, axis=1, keepdims=True)
            raised = jnp.exp(scores - peak)
            row_total = jnp.sum(raised, axis=1, keepdims=True)
            attn = (raised * (1.0 / row_total)).astype(LOW)
            piece = dot(attn, own_values)
            mixed = piece if mixed is None else mixed + piece
            lse[...] = jnp.where(lanes == 2 * pair + part, peak + jnp.log(row_total), lse[...])
        mixed = mixed.astype(LOW)
        attended[:, here] = mixed
        return carry

    lax.fori_loop(0, model // PAIR, attend, 0)

    def project(k, carry):
        here = pl.ds(pl.multiple_of(k * 2 * PAIR, PAIR), 2 * PAIR)
        there = pl.ds(pl.multiple_of(3 * model + k * 2 * PAIR, PAIR), 2 * PAIR)
        total[:, here] = dot(attended[...], columns(there))
        return carry

    lax.fori_loop(0, model // (2 * PAIR), project, 0)
    lse_rows[...] = jnp.transpose(lse[...])
    normed_t[...] = jnp.transpose(normed[...])
    attended_t[...] = jnp.transpose(attended[...])
    mid = tokens[...].astype(F32) + (total[...] + vecs[4:5])
    middle[...] = mid
    xhat, _ = norm_parts(mid)
    low = (xhat * vecs[5:6] + vecs[6:7]).astype(LOW)
    moe_low[...] = low
    moe_low_t[...] = jnp.transpose(low)
    logits = jnp.where(lanes < experts, dot(low, columns(pl.ds(4 * model, PAIR))), -jnp.inf)
    raised = jnp.exp(logits - jnp.max(logits, axis=1, keepdims=True))
    probs = raised / jnp.sum(raised, axis=1, keepdims=True)
    probs_out[...] = probs
    gate_a = jnp.sum(jnp.where(lanes == first_at, probs, 0.0), axis=1, keepdims=True)
    gate_b = jnp.sum(jnp.where(lanes == second_at, probs, 0.0), axis=1, keepdims=True)
    gates_out[...] = jnp.where(lanes == 0, gate_a, gate_b)

    def settle(k, carry):
        d = k + 1
        up_copy(d, ahead_of(dims, d)).wait_send()
        up_copy(d, behind_of(dims, d)).wait_recv()
        return carry

    lax.fori_loop(0, wide - 1, settle, 0)
    keep_up.wait()
    for copy in w_copies + b_copies + fills:
        copy.wait()
    for group in (first, by_x, by_y, half_a, half_b, by_core):
        for copy in group.values():
            copy.wait_send()


def front_stage(
    dims, experts, capacity, stride, gathered, pack, tokens, segment_ids, patch_valid, routes, priority,
    cotangent, w_out, in_bias,
):
    depth, across, rows, cores = dims
    wide, narrow = depth * across, rows * cores
    count, model = tokens.shape
    used = -(-capacity // 8) * 8
    any_, vmem = pl.BlockSpec(memory_space=pl.ANY), pl.BlockSpec(memory_space=pltpu.VMEM)
    low = lambda *shape: jax.ShapeDtypeStruct(shape, LOW)
    f32 = lambda *shape: jax.ShapeDtypeStruct(shape, F32)
    i32 = lambda *shape: jax.ShapeDtypeStruct(shape, jnp.int32)
    width = 4 * model + PAIR
    height = model if gathered else pack[0].shape[0]
    full = (height, width) if gathered else (wide * narrow, height, width)
    packed = 1 if gathered else height
    corners = depth * (across - 1) * (rows - 1)
    sems = []
    for size in (
        depth - 1, depth * (across - 1), depth * (rows - 1), corners, corners, depth * across * rows,
        wide, (rows - 1) * PIECES, narrow,
    ):
        sems += [pltpu.SemaphoreType.DMA((size,))] * 2
    outs = pl.pallas_call(
        functools.partial(front_kernel, dims, experts, capacity, gathered, len(pack)),
        out_shape=(
            low(*full), low(model, count), low(count, model), low(count, model), low(count, model),
            low(model, count), f32(PAIR, count), f32(count, model), low(count, model), low(model, count),
            f32(count, PAIR), f32(count, PAIR), f32(8, model), f32(count, count), i32(count, PAIR), i32(8, count),
            f32(narrow, 1, in_bias.shape[1]), low(wide, stride, model), *[low(*w_out.shape)] * (rows - 1),
        ),
        in_specs=([any_] if gathered else [any_, any_, vmem, vmem]) + [vmem] * 6 + [any_, vmem],
        out_specs=[vmem] * 17 + [any_] * rows,
        scratch_shapes=[
            pltpu.VMEM((count, model), LOW),
            pltpu.VMEM((count, model), LOW),
            pltpu.VMEM((count, model), F32),
            pltpu.VMEM((count, count), F32),
            pltpu.VMEM((count, PAIR), F32),
            pltpu.VMEM((wide, stride, model), LOW),
            pltpu.VMEM((1, in_bias.shape[1]), F32),
            pltpu.VMEM((packed, width), LOW),
            pltpu.VMEM((PAIR, PAIR), F32),
            pltpu.VMEM((max(stride - used, 8), model), LOW),
            *sems,
            pltpu.SemaphoreType.DMA((5,)),
            pltpu.SemaphoreType.DMA((wide,)),
        ],
        compiler_params=pltpu.CompilerParams(
            collective_id=0, has_side_effects=True, vmem_limit_bytes=VMEM_LIMIT
        ),
        cost_estimate=pl.CostEstimate(flops=7 * 10**9, bytes_accessed=20 * 10**6, transcendentals=4 * 10**6),
        name="front_stage",
    )(*pack, tokens, segment_ids, patch_valid, jnp.transpose(routes), priority, cotangent, w_out, in_bias)
    params = outs[0] if gathered else outs[0].reshape(wide * narrow * height, width)
    return params, outs[1:14], outs[14:18], outs[18:]


def norm_back(grad, gain, xhat, scale):
    scaled = grad * gain
    mean_a = jnp.mean(scaled, axis=-1, keepdims=True)
    mean_b = jnp.mean(scaled * xhat, axis=-1, keepdims=True)
    return scale * (scaled - mean_a - xhat * mean_b)


def back_kernel(dims, used, experts, gathered, *rest):
    depth, across, rows, cores = dims
    wide, narrow = depth * across, rows * cores
    (
        tokens, normed_t, queries, keys, values, attended_t, lse_rows, middle, _, moe_low_t, probs, gates, vecs, bias,
        weights, slots, token_rows, gate_slots, cotangent, y_rows,
    ) = rest[:20]
    side_grad = rest[20 : 19 + rows]
    rest = rest[19 + rows :]
    if gathered:
        block_out, tokens_grad, grad_here, group = rest[:4]
        rest = rest[4:]
    else:
        block_out, tokens_grad, grad_here, out_qkv, out_proj, out_router, *out_vecs = rest[:13]
        group, n1, n2, n3, n4 = rest[13:18]
        rest = rest[18:]
    branch, middle_grad, qkv_grad, sums, router, parts, y_here = rest[:7]
    s_y, q_y, s_g, q_g, local = rest[7:12]
    z, x, y, c = place_of(dims)
    me, n = z * across + x, y * cores + c
    count, model = tokens.shape
    stride = y_here.shape[1]
    pairs = model // PAIR
    per = 3 * PAIR
    n_proj = model // per
    small_at = n_proj + pairs
    lanes = lax.broadcasted_iota(jnp.int32, (count, PAIR), 1)

    def remote(src, dst, ssem, rsem, to):
        return pltpu.make_async_remote_copy(
            src_ref=src, dst_ref=dst, send_sem=ssem, recv_sem=rsem, device_id=to, device_id_type=MESH
        )

    peers = [((me + d) % wide, n) for d in range(1, wide)]
    peers += [device_at(dims, z, x, (y + d) % rows, c) for d in range(1, rows)]
    peers += [device_at(dims, z, x, y, 1 - c)]
    body = pl.ds(0, used)
    if used < stride:
        y_here[:, used:stride] = jnp.zeros((wide, stride - used, model), LOW)
    greet(peers)

    def y_copy(d, to):
        return remote(y_rows.at[to, body], y_here.at[me, body], s_y.at[d], q_y.at[d], (to, n))

    def give(k, carry):
        d = (k + wide // 2 - 1) % (wide - 1) + 1
        y_copy(d, ahead_of(dims, d)).start()
        return carry

    lax.fori_loop(0, wide - 1, give, 0)
    keep_y = pltpu.make_async_copy(y_rows.at[me, body], y_here.at[me, body], local.at[0])
    keep_y.start()
    piece = grad_here.shape[1] // PIECES

    def g_copies(i):
        copies = []
        for dy in range(1, rows):
            at = (dy - 1) * PIECES + i
            part = pl.ds(i * piece, piece)
            to = device_at(dims, z, x, (y + dy) % rows, c)
            copies.append(remote(side_grad[dy - 1].at[part], grad_here.at[dy - 1, part], s_g.at[at], q_g.at[at], to))
        return copies

    def give_grad(i):
        for copy in g_copies(i):
            copy.start()

    for i in range(PIECES):
        give_grad(i)

    if not gathered:
        s1, q1, s2, q2, s3, q3, s4, q4 = rest[12:20]
        height = group.shape[-2]

    def put(g, value):
        at = pl.ds(0, value.shape[1])
        value = value.astype(LOW)
        if gathered:
            group[g, :, at] = value
        else:
            group[g, :, :, :, :, :, at] = value.reshape(depth, across, rows, cores, height, at.size)

    def span(g):
        return pl.ds(0, PAIR) if isinstance(g, int) and g == small_at else pl.ds(0, per)

    def hop_core(g):
        return remote(
            group.at[g, :, :, :, 1 - c, :, span(g)], n1.at[g, :, :, :, :, span(g)], s1.at[g], q1.at[g],
            device_at(dims, z, x, y, 1 - c),
        )

    def hop_x(g, dx):
        at = g * (across - 1) + dx - 1
        return remote(
            n1.at[g, :, (x + dx) % across, :, :, span(g)], n2.at[at, :, :, :, span(g)],
            s2.at[at], q2.at[at], device_at(dims, z, (x + dx) % across, y, c),
        )

    def hop_y(g, dy):
        at = g * (rows - 1) + dy - 1
        return remote(
            n2.at[g * (across - 1), :, (y + dy) % rows, :, span(g)], n3.at[at, :, :, span(g)],
            s3.at[at], q3.at[at], device_at(dims, z, x, (y + dy) % rows, c),
        )

    def hop_z(g, dz):
        at = g * (depth - 1) + dz - 1
        return remote(
            n3.at[g * (rows - 1), (z + dz) % depth, :, span(g)], n4.at[at, :, span(g)],
            s4.at[at], q4.at[at], device_at(dims, (z + dz) % depth, x, y, c),
        )

    def start(g):
        if not gathered:
            hop_core(g).start()

    def begin(g):
        if gathered:
            return
        hop_core(g).wait_recv()
        w = span(g)
        n1[g, :, :, :, :, w] = (
            group[g, :, :, :, c, :, w].astype(F32) + n1[g, :, :, :, :, w].astype(F32)
        ).astype(LOW)
        for dx in range(1, across):
            hop_x(g, dx).start()

    def middle_of(g):
        if gathered:
            return
        w = span(g)
        at = g * (across - 1)
        acc = n1[g, :, x, :, :, w].astype(F32)
        for dx in range(1, across):
            hop_x(g, dx).wait_recv()
            acc = acc + n2[at + dx - 1, :, :, :, w].astype(F32)
        n2[at, :, :, :, w] = acc.astype(LOW)
        for dy in range(1, rows):
            hop_y(g, dy).start()

    def end(g):
        if gathered:
            return
        w = span(g)
        at = g * (rows - 1)
        for dy in range(1, rows):
            hop_y(g, dy).wait_recv()
        acc = n2[g * (across - 1), :, y, :, w].astype(F32)
        for dy in range(1, rows):
            acc = acc + n3[at + dy - 1, :, :, w].astype(F32)
        n3[at, :, :, w] = acc.astype(LOW)
        for dz in range(1, depth):
            hop_z(g, dz).start()

    def last(g):
        w = span(g)
        acc = n3[g * (rows - 1), z, :, w].astype(F32)
        for dz in range(1, depth):
            hop_z(g, dz).wait_recv()
            acc = acc + n4[g * (depth - 1) + dz - 1, :, w].astype(F32)
        return acc

    sums[...] = jnp.zeros_like(sums)
    slot_a, slot_b = slots[:, 0:1], slots[:, 1:2]
    slot_at = lax.broadcasted_iota(jnp.int32, (count, wide * stride), 1)
    third = PAIR // 4
    lane_at = lax.broadcasted_iota(jnp.int32, (stride, PAIR), 1)

    def split(w, carry):
        value = column_of(gate_slots[w])[0:stride]
        high = value.astype(LOW).astype(F32)
        mid = (value - high).astype(LOW).astype(F32)
        low = value - high - mid
        row = jnp.where(lane_at == w, high, 0.0) + jnp.where(lane_at == third + w, mid, 0.0)
        parts[w] = (row + jnp.where(lane_at == 2 * third + w, low, 0.0)).astype(LOW)
        return carry

    lax.fori_loop(0, wide, split, 0)
    picks = jnp.where((slot_at == slot_a) | (slot_at == slot_b), 1.0, 0.0).astype(LOW)
    picked = dot(picks, parts[...].reshape(wide * stride, PAIR))
    prob_grad = picked + pltpu.roll(picked, PAIR - third, 1) + pltpu.roll(picked, PAIR - 2 * third, 1)
    own = probs[...]
    prob_grad = jnp.where(lanes < experts, prob_grad, 0.0)
    logit_grad = (own * (prob_grad - jnp.sum(prob_grad * own, axis=1, keepdims=True))).astype(LOW)
    router[...] = dot(moe_low_t[...], logit_grad)
    moe_grad = dot(picks, token_rows[...].reshape(wide * stride, model)) + dot_nt(
        logit_grad, weights[:, 4 * model : 4 * model + PAIR]
    )
    xhat, scale = norm_parts(middle[...])
    sums[5:6] = jnp.sum(moe_grad * xhat, axis=0, keepdims=True)
    sums[6:7] = jnp.sum(moe_grad, axis=0, keepdims=True)
    mid = cotangent[...].astype(F32) + norm_back(moe_grad, vecs[5:6], xhat, scale)
    middle_grad[...] = mid
    branch[...] = mid.astype(LOW)
    sums[4:5] = jnp.sum(branch[...].astype(F32), axis=0, keepdims=True)
    for g in range(n_proj):
        put(g, dot(attended_t[...], branch[:, g * per : (g + 1) * per]))
        start(g)
    begin(0)

    sides = lax.broadcasted_iota(jnp.int32, (PAIR, count), 0)

    def attend(pair, carry):
        at = lambda which: pl.ds(pl.multiple_of(which * model + pair * PAIR, PAIR), PAIR)
        here = at(0)
        grad_mixed = dot_nt(branch[...], weights[here, 3 * model : 4 * model]).astype(LOW)
        q_pair, k_pair, v_pair = queries[:, here], keys[:, here], values[:, here]
        k_turned = jnp.transpose(k_pair)
        q_grad_t, k_grad, v_grad = None, None, None
        for part in range(2):
            side = (lanes < HEAD) if part == 0 else (lanes >= HEAD)
            side_t = (sides < HEAD) if part == 0 else (sides >= HEAD)
            own_keys = jnp.where(side, k_pair, LOW(0))
            own_values = jnp.where(side, v_pair, LOW(0))
            own_queries = jnp.where(side, q_pair, LOW(0))
            own_grads = jnp.where(side, grad_mixed, LOW(0))
            own_turned = jnp.where(side_t, k_turned, LOW(0))
            scores = dot_nt(own_keys, q_pair) + bias[...]
            attn = jnp.exp(scores - lse_rows[pl.ds(2 * pair + part, 1), :])
            attn_grad = dot_nt(own_values, grad_mixed)
            mean = jnp.sum(attn * attn_grad, axis=0, keepdims=True)
            score_grad = (attn * (attn_grad - mean)).astype(LOW)
            v_part = dot(attn.astype(LOW), own_grads)
            k_part = dot(score_grad, own_queries)
            q_part = dot(own_turned, score_grad)
            if part == 0:
                q_grad_t, k_grad, v_grad = q_part, k_part, v_part
            else:
                q_grad_t, k_grad, v_grad = q_grad_t + q_part, k_grad + k_part, v_grad + v_part
        q_grad = (jnp.transpose(q_grad_t) * HEAD**-0.5).astype(LOW)
        k_grad = k_grad.astype(LOW)
        v_grad = v_grad.astype(LOW)
        sums[2:3, here] = jnp.sum(q_grad.astype(F32), axis=0, keepdims=True)
        sums[3:4, here] = jnp.sum(v_grad.astype(F32), axis=0, keepdims=True)
        g = pair + n_proj
        for which, part in enumerate((q_grad, k_grad, v_grad)):
            qkv_grad[:, at(which)] = part
        put(g, dot(normed_t[...], jnp.concatenate([q_grad, k_grad, v_grad], axis=1)))
        start(g)
        if not gathered:
            begin(g - 1)

            @pl.when(g >= 5)
            def _():
                middle_of(g - 5)

            @pl.when(g >= 7)
            def _():
                end(g - 7)

        return carry

    lax.fori_loop(0, pairs, attend, 0)
    begin(small_at - 1)
    grad = dot_nt(qkv_grad[...], weights[:, : 3 * model])
    xhat, scale = norm_parts(tokens[...].astype(F32))
    sums[0:1] = jnp.sum(grad * xhat, axis=0, keepdims=True)
    sums[1:2] = jnp.sum(grad, axis=0, keepdims=True)
    stacked = jnp.concatenate([sums[...], jnp.zeros((PAIR - 8, model), F32)], axis=0)
    turned = pltpu.roll(jnp.transpose(stacked), experts, 1)
    wide_lanes = lax.broadcasted_iota(jnp.int32, (model, PAIR), 1)
    put(small_at, jnp.where(wide_lanes < experts, router[...], turned))
    start(small_at)
    for g in range(small_at - 5, small_at - 2):
        middle_of(g)
    for g in range(small_at - 7, small_at - 3):
        end(g)
    tokens_grad[...] = (middle_grad[...] + norm_back(grad, vecs[0:1], xhat, scale)).astype(LOW)
    begin(small_at)
    middle_of(small_at - 2)
    end(small_at - 3)
    middle_of(small_at - 1)
    middle_of(small_at)
    end(small_at - 2)
    end(small_at - 1)
    end(small_at)

    def taken(k, carry):
        d = k + 1
        y_copy(d, ahead_of(dims, d)).wait_send()
        y_copy(d, behind_of(dims, d)).wait_recv()
        return carry

    lax.fori_loop(0, wide - 1, taken, 0)
    keep_y.wait()
    returned = y_here[...].reshape(wide * stride, model)
    mixed = gates[:, 0:1] * dot(jnp.where(slot_at == slot_a, 1.0, 0.0).astype(LOW), returned)
    mixed += gates[:, 1:2] * dot(jnp.where(slot_at == slot_b, 1.0, 0.0).astype(LOW), returned)
    block_out[...] = (middle[...] + mixed).astype(LOW)
    if not gathered:
        for g in range(n_proj):
            out_proj[:, g * per : (g + 1) * per] = last(g)
        for pair in range(pairs):
            summed = last(n_proj + pair)
            for which in range(3):
                at = which * model + pair * PAIR
                out_qkv[:, at : at + PAIR] = summed[:, which * PAIR : (which + 1) * PAIR]
        summed = last(small_at)
        square = jnp.concatenate([summed, jnp.zeros((PAIR - height, PAIR), F32)], axis=0)
        turned = jnp.transpose(square)
        out_router[...] = turned[0:experts, 0:height]
        for i, ref in enumerate(out_vecs):
            ref[...] = turned[experts + i : experts + i + 1, 0:height]
        for g in range(small_at + 1):
            hop_core(g).wait_send()
            for dx in range(1, across):
                hop_x(g, dx).wait_send()
            for dy in range(1, rows):
                hop_y(g, dy).wait_send()
            for dz in range(1, depth):
                hop_z(g, dz).wait_send()
    for i in range(PIECES):
        for copy in g_copies(i):
            copy.wait()


def back_stage(
    dims, used, experts, gathered, tokens, saved, params, slots, token_rows, gate_slots, cotangent, y_rows, side_grads,
):
    depth, across, rows, cores = dims
    wide, narrow = depth * across, rows * cores
    count, model = tokens.shape
    stride = y_rows.shape[1]
    per = 3 * PAIR
    groups = model // per + model // PAIR + 1
    height = model // (wide * narrow)
    any_, vmem = pl.BlockSpec(memory_space=pl.ANY), pl.BlockSpec(memory_space=pltpu.VMEM)
    low = lambda *shape: jax.ShapeDtypeStruct(shape, LOW)
    f32 = lambda *shape: jax.ShapeDtypeStruct(shape, F32)
    sem = lambda size: [pltpu.SemaphoreType.DMA((size,))] * 2
    outs = [low(count, model), low(count, model), low(rows - 1, *side_grads[0].shape)]
    buffers, sems = [], []
    if gathered:
        outs.append(low(groups, model, per))
    else:
        outs += [f32(height, 3 * model), f32(height, model), f32(experts, height), *[f32(1, height)] * 7]
        buffers = [
            pltpu.VMEM((groups, depth, across, rows, cores, height, per), LOW),
            pltpu.VMEM((groups, depth, across, rows, height, per), LOW),
            pltpu.VMEM((groups * (across - 1), depth, rows, height, per), LOW),
            pltpu.VMEM((groups * (rows - 1), depth, height, per), LOW),
            pltpu.VMEM((groups * (depth - 1), height, per), LOW),
        ]
        sems = [
            *sem(groups), *sem(groups * (across - 1)), *sem(groups * (rows - 1)), *sem(groups * (depth - 1)),
        ]
    return pl.pallas_call(
        functools.partial(back_kernel, dims, used, experts, gathered),
        out_shape=tuple(outs),
        in_specs=[vmem] * 8 + [any_] + [vmem] * 10 + [any_] * rows,
        out_specs=[vmem] * 2 + [any_] + [vmem] * (len(outs) - 3),
        scratch_shapes=[
            *buffers,
            pltpu.VMEM((count, model), LOW),
            pltpu.VMEM((count, model), F32),
            pltpu.VMEM((count, 3 * model), LOW),
            pltpu.VMEM((8, model), F32),
            pltpu.VMEM((model, PAIR), F32),
            pltpu.VMEM((wide, stride, PAIR), LOW),
            pltpu.VMEM((wide, stride, model), LOW),
            *sem(wide), *sem((rows - 1) * PIECES),
            pltpu.SemaphoreType.DMA((1,)),
            *sems,
        ],
        compiler_params=pltpu.CompilerParams(
            collective_id=1, has_side_effects=True, vmem_limit_bytes=60 * 1024 * 1024
        ),
        cost_estimate=pl.CostEstimate(flops=16 * 10**9, bytes_accessed=40 * 10**6, transcendentals=4 * 10**6),
        name="back_stage",
    )(
        tokens, *saved, params, slots, token_rows, gate_slots, cotangent, y_rows, *side_grads
    )


def tail_kernel(count, *refs):
    inputs, own, other_out, refs = refs[:count], refs[count], refs[count + 1], refs[count + 2 :]
    rows = other_out.shape[0] + 1
    other_in, refs = refs[: rows - 1], refs[rows - 1 :]
    outputs, grad_in, grad_out = refs[:count], refs[count], refs[count + 1]
    terms, first, second, sems, loads, brings = refs[count + 2 : count + 8]
    held = refs[count + 8 :]
    arrivals = [pltpu.make_async_copy(own, terms.at[0], loads.at[0])]
    for i in range(1, rows):
        arrivals.append(pltpu.make_async_copy(other_in[i - 1], terms.at[i, 0], loads.at[2 * i - 1]))
        arrivals.append(pltpu.make_async_copy(other_out.at[i - 1], terms.at[i, 1], loads.at[2 * i]))
    bring = [pltpu.make_async_copy(src, dst, brings.at[i]) for i, (src, dst) in enumerate(zip(inputs, held))]
    copies = [pltpu.make_async_copy(src, dst, sems.at[i]) for i, (src, dst) in enumerate(zip(held, outputs))]
    for copy in bring + arrivals:
        copy.start()
    for into, out in zip(bring, copies):
        into.wait()
        out.start()
    for copy in arrivals:
        copy.wait()

    def total(which):
        acc = terms[0, which].astype(F32)
        for i in range(1, rows):
            acc = acc + terms[i, which].astype(F32)
        return acc

    first[0] = total(0)
    copies.append(pltpu.make_async_copy(first, grad_in, sems.at[count]))
    copies[-1].start()
    second[0] = jnp.transpose(total(1))
    copies.append(pltpu.make_async_copy(second, grad_out, sems.at[count + 1]))
    copies[-1].start()
    for copy in copies:
        copy.wait()


def tail_stage(arrays, own, other_out, other_in):
    any_ = pl.BlockSpec(memory_space=pl.ANY)
    _, model, ff = own.shape
    count = len(arrays)
    shapes = [jax.ShapeDtypeStruct(a.shape, a.dtype) for a in arrays]
    shapes += [jax.ShapeDtypeStruct((1, model, ff), F32), jax.ShapeDtypeStruct((1, ff, model), F32)]
    rows = other_out.shape[0] + 1
    return pl.pallas_call(
        functools.partial(tail_kernel, count),
        out_shape=tuple(shapes),
        in_specs=[any_] * (count + 1 + rows),
        out_specs=[any_] * (count + 2),
        scratch_shapes=[
            pltpu.VMEM((rows, 2, model, ff), LOW),
            pltpu.VMEM((1, model, ff), F32),
            pltpu.VMEM((1, ff, model), F32),
            pltpu.SemaphoreType.DMA((count + 2,)),
            pltpu.SemaphoreType.DMA((2 * rows - 1,)),
            pltpu.SemaphoreType.DMA((count,)),
            *[pltpu.VMEM(a.shape, a.dtype) for a in arrays],
        ],
        compiler_params=pltpu.CompilerParams(vmem_limit_bytes=58 * 1024 * 1024),
        name="results",
    )(*arrays, own, other_out, *other_in)


def gelu_and_slope(v):
    root = 0.7978845608028654
    cubic = 0.044715
    square = v * v
    half = 0.5 * jnp.tanh(v * (root + (root * cubic) * square)) + 0.5
    value = v * half
    slope = half + value * ((1.0 - half) * (2.0 * root + (6.0 * root * cubic) * square))
    return value, slope


def moe_kernel(
    dims, used, moe_low, slot_rows, slot_cols, gates, ups, b_in, b_out, w_in, w_out, *rest
):
    depth, across, rows, cores = dims
    wide = depth * across
    narrow = rows * cores
    side_out = rest[: rows - 1]
    rest = rest[rows - 1 :]
    token_rows, gate_slots, y_out, in_bias_grad, out_bias_grad = rest[:5]
    own_grad = rest[5]
    side_in, side_grad = rest[6 : 5 + rows], rest[5 + rows : 4 + 2 * rows]
    (
        full_in, full_out, x_send, x_here, g_send, g_here, dx_send, h_send, hidden, pre_grad, weighted,
        x_turned, w_turned, grad_send, grad_here, extra, extra_here, extra_y, blank, dx_part, back_part,
        local, blanks, s_wy, r_wy, s_y, r_y, s_ey, r_ey, s_in, r_in, s_out, r_out, s_x, r_x, s_g, r_g, s_dx, r_dx, s_h, r_h, s_w, r_w, s_e, r_e,
    ) = rest[4 + 2 * rows :]
    z, x, y, c = place_of(dims)
    me, n = z * across + x, y * cores + c
    count, model = moe_low.shape
    capacity = x_send.shape[1]
    gate_width = g_send.shape[2]
    ff = full_in.shape[2]
    other = device_at(dims, z, x, y, 1 - c)

    def remote(src, dst, ssem, rsem, to):
        return pltpu.make_async_remote_copy(
            src_ref=src, dst_ref=dst, send_sem=ssem, recv_sem=rsem, device_id=to, device_id_type=MESH
        )

    along_y = [device_at(dims, z, x, (y + i) % rows, c) for i in range(1, rows)]
    body = pl.ds(0, used)
    if used < capacity:
        x_here[:, used:capacity] = jnp.zeros((wide, capacity - used, model), LOW)
        blank[...] = jnp.zeros_like(blank)
    greet([((me + d) % wide, n) for d in range(1, wide)] + [other] + along_y)
    fills = []
    if used < capacity:
        for w in range(wide):
            fills.append(pltpu.make_async_copy(blank, token_rows.at[w, pl.ds(used, capacity - used)], blanks.at[w]))

    held = [((y - i) % rows) * cores + c for i in range(rows)]
    from_y, in_passes, out_loads, out_passes = [], [], [], []
    for i, h in enumerate(held):
        src_out = w_out.at[0] if i == 0 else side_out[i - 1].at[0]
        out_loads.append(pltpu.make_async_copy(src_out, full_out.at[h], local.at[i]))
        out_passes.append(remote(src_out, full_out.at[h], s_out.at[i], r_out.at[i], other))
        if i:
            from_y.append(remote(w_in.at[0], full_in.at[n], s_wy.at[i - 1], r_wy.at[i - 1], along_y[i - 1]))
        src_in = w_in.at[0] if i == 0 else full_in.at[h]
        in_passes.append(remote(src_in, full_in.at[h], s_in.at[i], r_in.at[i], other))
    in_load = pltpu.make_async_copy(w_in.at[0], full_in.at[n], local.at[rows])
    for copy in from_y + out_loads + out_passes:
        copy.start()

    slot_a, slot_b = slot_cols[:, 0:1], slot_cols[:, 1:2]
    gate_a, gate_b = gates[:, 0:1], gates[:, 1:2]
    row_at = lax.broadcasted_iota(jnp.int32, (capacity, count), 0)
    lane_at = lax.broadcasted_iota(jnp.int32, (count, gate_width), 1)
    source = moe_low[...]

    def rows_for(expert):
        first = expert * capacity
        hit = (slot_rows[0:1] - first == row_at) | (slot_rows[1:2] - first == row_at)
        picked = dot(jnp.where(hit, 1.0, 0.0).astype(LOW), source).astype(LOW)
        inside = lane_at < capacity
        hit_a = (slot_a - first == lane_at) & inside
        hit_b = (slot_b - first == lane_at) & inside
        gate = jnp.where(hit_a, gate_a, 0.0) + jnp.where(hit_b, gate_b, 0.0)
        return picked, jnp.sum(gate, axis=0, keepdims=True)

    def x_copy(d, to):
        return remote(x_send.at[to, body], x_here.at[me, body], s_x.at[d], r_x.at[d], (to, n))

    def g_copy(d, to):
        return remote(g_send.at[to], g_here.at[me], s_g.at[d], r_g.at[d], (to, n))

    def dx_copy(d, to):
        return remote(dx_send.at[to, body], token_rows.at[me, body], s_dx.at[d], r_dx.at[d], (to, n))

    def h_copy(d, to):
        return remote(h_send.at[to], gate_slots.at[me], s_h.at[d], r_h.at[d], (to, n))

    def dispatch(k, carry):
        d = (k + wide // 2 - 1) % (wide - 1) + 1
        to = ahead_of(dims, d)
        picked, gate = rows_for(to)
        x_send[to] = picked
        g_send[to] = gate
        x_copy(d, to).start()
        g_copy(d, to).start()
        return carry

    lax.fori_loop(0, wide - 1, dispatch, 0)
    in_load.start()
    in_passes[0].start()
    for copy in fills:
        copy.start()
    picked, gate = rows_for(me)
    x_here[me] = picked
    g_here[me] = gate
    extra[...] = jnp.zeros_like(extra)
    out_bias = b_out[...].astype(F32)
    for copy in out_loads:
        copy.wait()

    def backs_of(places):
        def backs(k, carry):
            two = pl.ds(2 * k, 2)
            up = ups[two].reshape(2 * capacity, model)
            for h in places:
                lanes = pl.ds(pl.multiple_of(h * ff, PAIR), ff)
                pre_grad[two, :, lanes] = dot_nt(up, full_out[h]).astype(LOW).reshape(2, capacity, ff)
            return carry

        return backs

    lax.fori_loop(0, wide // 2, backs_of([i * cores + c for i in range(rows)]), 0)
    for copy in out_passes:
        copy.wait_recv()
    lax.fori_loop(0, wide // 2, backs_of([i * cores + 1 - c for i in range(rows)]), 0)
    in_load.wait()
    in_passes[0].wait_recv()

    def expert(src, places, slot=None, first=True, final=True):
        own = x_here[src]
        up = ups[src]
        gate = jnp.transpose(jnp.broadcast_to(g_here[src], (PAIR, gate_width)))[:capacity, 0:1]
        if first:
            weighted[src] = (gate * up.astype(F32)).astype(LOW)
            back_total = jnp.sum(up.astype(F32) * out_bias, axis=1, keepdims=True)
            dx = None
        else:
            back_total = back_part[slot, :, 0:1]
            dx = dx_part[slot]
        for h in places:
            lanes = pl.ds(h * ff if isinstance(h, int) else pl.multiple_of(h * ff, PAIR), ff)
            pre = dot(own, full_in[h]) + b_in[h]
            back = pre_grad[src, :, lanes].astype(F32)
            value, slope = gelu_and_slope(pre)
            hidden[src, :, lanes] = value.astype(LOW)
            back_total += jnp.sum(value * back, axis=1, keepdims=True)
            wide_grad = slope * (gate * back)
            grad = wide_grad.astype(LOW)
            pre_grad[src, :, lanes] = grad
            extra[h, 0:1, :ff] += jnp.sum(wide_grad, axis=0, keepdims=True)
            part = dot_nt(grad, full_in[h])
            dx = part if dx is None else dx + part
        if final:
            dx_send[src] = dx.astype(LOW)
            spread = jnp.broadcast_to(back_total, (capacity, PAIR))
            spread = jnp.concatenate([spread, jnp.zeros((gate_width - capacity, PAIR), F32)], axis=0)
            h_send[src] = jnp.transpose(spread)[0:1]
        else:
            dx_part[slot] = dx
            back_part[slot] = jnp.broadcast_to(back_total, (capacity, PAIR))

    def source_of(k):
        d = (k + wide // 2 - 1) % (wide - 1) + 1
        return d, behind_of(dims, d)

    def land(k):
        d, src = source_of(k)
        x_copy(d, src).wait_recv()
        g_copy(d, src).wait_recv()
        return src

    def give_back(k):
        d, src = source_of(k)
        dx_copy(d, src).start()
        h_copy(d, src).start()

    near = [y * cores + i for i in range(cores)]
    far = [(y + i) % rows * cores + j for i in range(1, rows) for j in range(cores)]
    early = dx_part.shape[0] - 1
    expert(me, near, 0, final=False)

    def begin(k, carry):
        expert(land(k), near, k + 1, final=False)
        return carry

    lax.fori_loop(0, early, begin, 0)
    for i in range(1, rows):
        from_y[i - 1].wait_recv()
        in_passes[i].start()
    for copy in in_passes[1:]:
        copy.wait_recv()

    def complete(k, carry):
        expert(source_of(k)[1], far, k + 1, first=False)
        return carry

    def serve(k, carry):
        expert(land(k), range(narrow))
        give_back(k - early)
        return carry

    lax.fori_loop(0, early, complete, 0)
    expert(me, far, 0, first=False)
    keep_rows = pltpu.make_async_copy(dx_send.at[me, body], token_rows.at[me, body], local.at[2 * rows])
    keep_gate = pltpu.make_async_copy(h_send.at[me], gate_slots.at[me], local.at[2 * rows + 1])
    keep_rows.start()
    keep_gate.start()
    lax.fori_loop(early, wide - 1, serve, 0)

    def give_rest(k, carry):
        give_back(k)
        return carry

    lax.fori_loop(wide - 1 - early, wide - 1, give_rest, 0)

    all_rows = wide * capacity
    x_turned[...] = jnp.transpose(x_here[...].reshape(all_rows, model))
    w_turned[...] = jnp.transpose(weighted[...].reshape(all_rows, model))
    bias_grad = jnp.sum(weighted[...].reshape(all_rows, model).astype(F32), axis=0, keepdims=True)
    for h in range(narrow):
        extra[h, 1:2] = bias_grad

    def grad_of(which, h):
        lanes = pl.ds(pl.multiple_of(h * ff, PAIR), ff)
        if which == 0:
            return dot(x_turned[...], pre_grad[:, :, lanes].reshape(all_rows, ff))
        return dot(w_turned[...], hidden[:, :, lanes].reshape(all_rows, ff))

    order = [*range(1, rows), 0]
    swaps, by_y, keep_grads = [], [], []
    for i in order:
        at = (y + i) % rows
        kept, given = at * cores + c, at * cores + 1 - c
        for which in range(2):
            k = 2 * i + which
            grad_send[i, which] = grad_of(which, given).astype(LOW)
            swap = remote(grad_send.at[i, which], grad_here.at[i, which], s_w.at[k], r_w.at[k], other)
            swap.start()
            swaps.append(swap)
            if which == 0:
                swap_extra = remote(extra.at[given], extra_here.at[i], s_e.at[i], r_e.at[i], other)
                swap_extra.start()
                swaps.append(swap_extra)
            grad = grad_of(which, kept)
            swap.wait_recv()
            grad_here[i, which] = (grad + grad_here[i, which].astype(F32)).astype(LOW)
            if which == 0:
                swap_extra.wait_recv()
                extra_here[i] = extra_here[i] + extra[kept]
            if i and which == 0:
                by_y.append(
                    remote(grad_here.at[i, 0], side_in[i - 1], s_y.at[i - 1], r_y.at[i - 1], along_y[i - 1])
                )
                by_y[-1].start()
                by_y.append(
                    remote(extra_here.at[i], extra_y.at[i - 1], s_ey.at[i - 1], r_ey.at[i - 1], along_y[i - 1])
                )
                by_y[-1].start()
        source, target = (grad_here.at[i, 1], side_grad[i - 1]) if i else (grad_here.at[0], own_grad)
        keep_grads.append(pltpu.make_async_copy(source, target, local.at[2 * rows + 3 + i]))
        keep_grads[-1].start()

    some = 4

    def outputs(k, carry):
        total = None
        at = pl.ds(k * some, some)
        for h in range(narrow):
            part = dot(hidden[at, :, h * ff : (h + 1) * ff].reshape(some * capacity, ff), full_out[h])
            total = part if total is None else total + part
        x_send[at] = (total + out_bias).astype(LOW).reshape(some, capacity, model)
        return carry

    def sent(k, carry):
        to = ahead_of(dims, k + 1)
        x_copy(k + 1, to).wait_send()
        g_copy(k + 1, to).wait_send()
        return carry

    lax.fori_loop(0, wide - 1, sent, 0)
    lax.fori_loop(0, wide // some, outputs, 0)
    keep_y = pltpu.make_async_copy(x_send, y_out, local.at[2 * rows + 2])
    keep_y.start()
    bias_rows = extra_here[0]
    for copy in by_y:
        copy.wait_recv()
    for i in range(1, rows):
        bias_rows = bias_rows + extra_y[i - 1]
    in_bias_grad[...] = bias_rows[0:1, :ff]
    out_bias_grad[...] = bias_rows[1:2]

    def finish(k, carry):
        d = k + 1
        back = behind_of(dims, d)
        dx_copy(d, back).wait_recv()
        h_copy(d, back).wait_recv()
        dx_copy(d, back).wait_send()
        h_copy(d, back).wait_send()
        return carry

    lax.fori_loop(0, wide - 1, finish, 0)
    for copy in from_y + in_passes + out_passes + swaps + by_y:
        copy.wait_send()
    for copy in fills:
        copy.wait()
    for copy in [keep_rows, keep_gate, keep_y] + keep_grads:
        copy.wait()


def moe_stage(dims, used, capacity, moe_low, slot_rows, slots, gates, ups, b_in, b_out, w_in, w_out, side_out):
    depth, across, rows, cores = dims
    wide, narrow = depth * across, rows * cores
    count, model = moe_low.shape
    ff = w_in.shape[2]
    gate_width = -(-capacity // PAIR) * PAIR
    any_, vmem = pl.BlockSpec(memory_space=pl.ANY), pl.BlockSpec(memory_space=pltpu.VMEM)
    low = lambda *shape: jax.ShapeDtypeStruct(shape, LOW)
    f32 = lambda *shape: jax.ShapeDtypeStruct(shape, F32)
    sem = lambda size: [pltpu.SemaphoreType.DMA((size,))] * 2
    outs = pl.pallas_call(
        functools.partial(moe_kernel, dims, used),
        out_shape=(
            low(wide, capacity, model), f32(wide, 1, gate_width), low(wide, capacity, model),
            f32(1, ff), f32(1, model), low(2, model, ff), *[low(model, ff)] * (2 * rows - 2),
        ),
        in_specs=[vmem] * 7 + [any_] * (1 + rows),
        out_specs=[any_] * 3 + [vmem] * 2 + [any_] * (2 * rows - 1),
        scratch_shapes=[
            pltpu.VMEM((narrow, model, ff), LOW),
            pltpu.VMEM((narrow, ff, model), LOW),
            pltpu.VMEM((wide, capacity, model), LOW),
            pltpu.VMEM((wide, capacity, model), LOW),
            pltpu.VMEM((wide, 1, gate_width), F32),
            pltpu.VMEM((wide, 1, gate_width), F32),
            pltpu.VMEM((wide, capacity, model), LOW),
            pltpu.VMEM((wide, 1, gate_width), F32),
            pltpu.VMEM((wide, capacity, narrow * ff), LOW),
            pltpu.VMEM((wide, capacity, narrow * ff), LOW),
            pltpu.VMEM((wide, capacity, model), LOW),
            pltpu.VMEM((model, wide * capacity), LOW),
            pltpu.VMEM((model, wide * capacity), LOW),
            pltpu.VMEM((rows, 2, model, ff), LOW),
            pltpu.VMEM((rows, 2, model, ff), LOW),
            pltpu.VMEM((narrow, 8, model), F32),
            pltpu.VMEM((rows, 8, model), F32),
            pltpu.VMEM((rows - 1, 8, model), F32),
            pltpu.VMEM((max(capacity - used, 8), model), LOW),
            pltpu.VMEM((1 + min(EARLY, wide - 1), capacity, model), F32),
            pltpu.VMEM((1 + min(EARLY, wide - 1), capacity, PAIR), F32),
            pltpu.SemaphoreType.DMA((3 * rows + 3,)),
            pltpu.SemaphoreType.DMA((wide,)),
            *sem(rows), *sem(rows), *sem(rows), *sem(rows), *sem(rows), *sem(wide), *sem(wide), *sem(wide), *sem(wide), *sem(2 * rows), *sem(rows),
        ],
        compiler_params=pltpu.CompilerParams(
            collective_id=2, has_side_effects=True, vmem_limit_bytes=60 * 1024 * 1024
        ),
        cost_estimate=pl.CostEstimate(flops=36 * 10**9, bytes_accessed=25 * 10**6, transcendentals=4 * 10**6),
        name="moe_stage",
    )(moe_low, slot_rows, slots, gates, ups, b_in, b_out, w_in, w_out, *side_out)
    return outs[:3], outs[3:5], outs[5], outs[6 : 5 + rows], outs[5 + rows :]


def per_device(
    dims,
    tokens, segment_ids, patch_valid, routes, priority, gain_attn, shift_attn, w_qkv, query_bias, value_bias,
    w_proj, proj_bias, gain_moe, shift_moe, w_router, w_in, in_bias, w_out, out_bias, cotangent,
):
    count, model = tokens.shape
    experts = w_router.shape[1]
    capacity = (210 * count + 100 * experts - 1) // (100 * experts)
    shard_rows = gain_attn.shape[0]
    vectors = jnp.stack([gain_attn, shift_attn, query_bias, value_bias, proj_bias, gain_moe, shift_moe])
    stride = -(-capacity // 16) * 16
    gathered = shard_rows % 8 != 0
    every = ("wide", "narrow")
    if gathered:
        empty = jnp.zeros((shard_rows, PAIR - 7 - experts), LOW)
        pack = jnp.concatenate([w_qkv, w_proj, w_router, jnp.transpose(vectors), empty], axis=1)
        pack = [lax.all_gather(pack, every, axis=0, tiled=True)]
    else:
        pack = [w_qkv, w_proj, jnp.transpose(w_router), vectors]
    params, saved, (slots, slot_rows, full_b_in, ups), side_out = front_stage(
        dims, experts, capacity, stride, gathered, pack, tokens, segment_ids, patch_valid, routes, priority,
        cotangent, w_out, in_bias,
    )
    moe_low, gates = saved[7], saved[10]
    used = -(-capacity // 8) * 8
    (token_rows, gate_slots, y_rows), bias_grads, own_grad, other_in, side_grads = moe_stage(
        dims, used, stride, moe_low, slot_rows, slots, gates, ups, full_b_in, out_bias, w_in, w_out, side_out
    )
    outs = back_stage(
        dims, used, experts, gathered, tokens, saved, params, slots, token_rows, gate_slots, cotangent, y_rows, side_grads,
    )
    settled = tail_stage([*outs[:2], *outs[3:], *bias_grads], own_grad, outs[2], other_in)
    outs, (grad_in_bias, grad_out_bias, grad_w_in, grad_w_out) = settled[:-4], settled[-4:]
    block_out, tokens_grad = outs[:2]
    if gathered:
        groups = lax.psum_scatter(outs[2].astype(F32), every, scatter_dimension=1, tiled=True)
        n_proj = model // (3 * PAIR)
        grad_proj = jnp.concatenate(list(groups[:n_proj]), axis=1)
        by_head = groups[n_proj:-1].reshape(-1, shard_rows, 3, PAIR)
        grad_qkv = by_head.transpose(1, 2, 0, 3).reshape(shard_rows, -1)
        grad_router = groups[-1, :, :experts]
        vector = [groups[-1, :, experts + i] for i in range(7)]
    else:
        grad_qkv, grad_proj, grad_router = outs[2:5]
        grad_router = jnp.transpose(grad_router)
        vector = [row.reshape(-1) for row in outs[5:]]
    return (
        block_out,
        tokens_grad,
        vector[0],
        vector[1],
        grad_qkv,
        vector[2],
        vector[3],
        grad_proj,
        vector[4],
        vector[5],
        vector[6],
        grad_router,
        grad_w_in,
        grad_in_bias,
        grad_w_out,
        grad_out_bias,
    )


def solution(mesh):
    dims = grid_of(mesh.shape["wide"], mesh.shape["narrow"])
    every = ("wide", "narrow")
    rows, vector = P(every, None), P(every)
    return jax.shard_map(
        functools.partial(per_device, dims),
        mesh=mesh,
        in_specs=(
            rows, rows, rows, rows, rows, vector, vector, rows, vector, vector, rows, vector, vector, vector,
            rows, P("wide", None, "narrow"), P("wide", "narrow"), P("wide", "narrow", None), P("wide", None), rows,
        ),
        out_specs=(
            rows, rows, vector, vector, rows, vector, vector, rows, vector, vector, vector, rows,
            P("wide", None, "narrow"), P("wide", "narrow"), P("wide", "narrow", None), P("wide", None),
        ),
        check_vma=False,
    )
```

```python
import functools

import jax
import jax.numpy as jnp
from jax import lax
from jax.experimental import pallas as pl
from jax.experimental.pallas import tpu as pltpu
from jax.sharding import PartitionSpec as P

HEAD = 64
PAIR = 2 * HEAD
EPSILON = 1e-06
MASKED = -1000000000.0
MESH = pl.DeviceIdType.MESH
LOW = jnp.bfloat16
F32 = jnp.float32
PIECES = 8
EARLY = 1
LAG = 2
VMEM_LIMIT = 58 * 1024 * 1024


def dot(a, b):
    return jnp.dot(a, b, preferred_element_type=F32)


def dot_nt(a, b):
    return lax.dot_general(a, b, (((1,), (1,)), ((), ())), preferred_element_type=F32)


def dot_tn(a, b):
    return lax.dot_general(a, b, (((0,), (0,)), ((), ())), preferred_element_type=F32)


def grid_of(wide, narrow):
    along_x = 1 << ((wide.bit_length() - 1) // 2)
    return wide // along_x, along_x, narrow // 2, 2


def place_of(dims):
    depth, across, rows, cores = dims
    wide, narrow = lax.axis_index("wide"), lax.axis_index("narrow")
    return wide // across, wide % across, narrow // cores, narrow % cores


def device_at(dims, z, x, y, c):
    depth, across, rows, cores = dims
    return (z * across + x, y * cores + c)


def ahead_of(dims, d):
    depth, across, rows, cores = dims
    z, x, y, c = place_of(dims)
    return (z + d // across) % depth * across + (x + d % across) % across


def behind_of(dims, d):
    depth, across, rows, cores = dims
    z, x, y, c = place_of(dims)
    return (z + depth - d // across) % depth * across + (x + across - d % across) % across


def greet(peers):
    barrier = pltpu.get_barrier_semaphore()
    for peer in peers:
        pl.semaphore_signal(barrier, inc=1, device_id=peer, device_id_type=MESH)
    pl.semaphore_wait(barrier, len(peers))


def neighbours(dims):
    depth, across, rows, cores = dims
    z, x, y, c = place_of(dims)
    peers = [device_at(dims, (z + d) % depth, x, y, c) for d in range(1, depth)]
    peers += [device_at(dims, z, (x + d) % across, y, c) for d in range(1, across)]
    peers += [device_at(dims, z, x, (y + d) % rows, c) for d in range(1, rows)]
    peers += [device_at(dims, z, x, y, 1 - c)]
    return peers


def norm_parts(values):
    center = jnp.mean(values, axis=-1, keepdims=True)
    offset = values - center
    spread = jnp.mean(offset * offset, axis=-1, keepdims=True)
    scale = lax.rsqrt(spread + EPSILON)
    return offset * scale, scale


def column_of(row):
    return jnp.transpose(jnp.broadcast_to(row, (PAIR, row.shape[1])))[:, 0:1]


def front_kernel(
    dims, experts, capacity, gathered, heads, *rest
):
    depth, across, rows, cores = dims
    wide, narrow = depth * across, rows * cores
    pack_refs, rest = rest[:heads], rest[heads:]
    tokens, seg_row, valid_row, routes, priority, cotangent, w_out, b_in = rest[:8]
    rest = rest[8:]
    (
        params, normed_t, q_out, k_out, v_out, attended_t, lse_rows, middle, moe_low, moe_low_t, probs_out, gates_out, vecs,
        bias_t, slots_out, slot_rows, full_b_in, ups,
    ) = rest[:18]
    side_out = rest[18 : 17 + rows]
    (
        normed, attended, total, bias, lse, up_send, b_send, shard, turn, blank,
        s1, r1, sx, rx, sy, ry, sa, ra, sb, rb, sc, rc, s_up, r_up, s_w, r_w, s_b, r_b, local, blanks,
    ) = rest[17 + rows :]
    z, x, y, c = place_of(dims)
    me, n = z * across + x, y * cores + c
    count, model = tokens.shape
    stride = ups.shape[1]
    lanes = lax.broadcasted_iota(jnp.int32, (count, PAIR), 1)

    def remote(src, dst, ssem, rsem, to):
        return pltpu.make_async_remote_copy(
            src_ref=src, dst_ref=dst, send_sem=ssem, recv_sem=rsem, device_id=to, device_id_type=MESH
        )

    def send(src, dst, ssem, rsem, to):
        copy = remote(src, dst, ssem, rsem, to)
        copy.start()
        return copy

    if not gathered:
        w_qkv, w_proj, router_t, vectors = pack_refs
        packs = [
            pltpu.make_async_copy(w_qkv, shard.at[:, pl.ds(0, 3 * model)], local.at[3]),
            pltpu.make_async_copy(w_proj, shard.at[:, pl.ds(3 * model, model)], local.at[4]),
        ]
        for copy in packs:
            copy.start()
        height = shard.shape[0]
        turn[...] = jnp.zeros_like(turn)
        turn[0:experts, 0:height] = router_t[...].astype(F32)
        turn[experts : experts + 7, 0:height] = vectors[...].astype(F32)
        shard[:, 4 * model : 4 * model + PAIR] = jnp.transpose(turn[...])[0:height].astype(LOW)
    b_send[...] = b_in[...].astype(F32)
    peers = [((me + d) % wide, n) for d in range(1, wide)]
    peers += [(me, (n + d) % narrow) for d in range(1, narrow)]
    greet(peers)
    if not gathered:
        for copy in packs:
            copy.wait()

    first, by_x, by_y, half_a, half_b, by_core = {}, {}, {}, {}, {}, {}
    keeps = []
    if not gathered:
        width = shard.shape[1]
        cut = (width // 256) * 128

        def block(dz, dx, dy, core):
            at = ((z - dz) % depth) * across + (x - dx) % across
            return params.at[(at * rows + (y - dy) % rows) * cores + core]

        own = block(0, 0, 0, c)
        keeps.append(pltpu.make_async_copy(shard, own, local.at[0]))
        keeps[-1].start()
        for dz in range(1, depth):
            first[dz] = send(
                shard, own, s1.at[dz - 1], r1.at[dz - 1], device_at(dims, (z + dz) % depth, x, y, c)
            )

    def to_core(dz, dx, dy):
        at = (dz * across + dx) * rows + dy
        src = shard if (dz, dx, dy) == (0, 0, 0) else block(dz, dx, dy, c)
        by_core[at] = send(
            src, block(dz, dx, dy, c), sc.at[at], rc.at[at], device_at(dims, z, x, y, 1 - c)
        )

    def spread(dz):
        if dz:
            first[dz].wait_recv()
        src = block(dz, 0, 0, c) if dz else shard
        for dx in range(1, across):
            at = dz * (across - 1) + dx - 1
            by_x[dz, dx] = send(
                src, block(dz, 0, 0, c), sx.at[at], rx.at[at],
                device_at(dims, z, (x + dx) % across, y, c),
            )
        for dy in range(1, rows):
            at = dz * (rows - 1) + dy - 1
            by_y[dz, dy] = send(
                src, block(dz, 0, 0, c), sy.at[at], ry.at[at],
                device_at(dims, z, x, (y + dy) % rows, c),
            )
        to_core(dz, 0, 0)

    def corner(dz):
        for dx in range(1, across):
            by_x[dz, dx].wait_recv()
            part = block(dz, dx, 0, c).at[:, pl.ds(0, cut)]
            for dy in range(1, rows):
                at = (dz * (across - 1) + dx - 1) * (rows - 1) + dy - 1
                half_a[dz, dx, dy] = send(
                    part, part, sa.at[at], ra.at[at], device_at(dims, z, x, (y + dy) % rows, c)
                )
            to_core(dz, dx, 0)
        for dy in range(1, rows):
            by_y[dz, dy].wait_recv()
            part = block(dz, 0, dy, c).at[:, pl.ds(cut, width - cut)]
            for dx in range(1, across):
                at = (dz * (across - 1) + dx - 1) * (rows - 1) + dy - 1
                half_b[dz, dx, dy] = send(
                    part, part, sb.at[at], rb.at[at], device_at(dims, z, (x + dx) % across, y, c)
                )
            to_core(dz, 0, dy)

    def finish(dz):
        for dx in range(1, across):
            for dy in range(1, rows):
                half_a[dz, dx, dy].wait_recv()
                half_b[dz, dx, dy].wait_recv()
                to_core(dz, dx, dy)

    if not gathered:
        spread(0)
    b_copies = []
    for d in range(1, narrow):
        b_copies.append(send(b_send, full_b_in.at[n], s_b.at[d], r_b.at[d], (me, (n + d) % narrow)))
    keeps.append(pltpu.make_async_copy(b_send, full_b_in.at[n], local.at[1]))
    keeps[-1].start()
    w_copies = []

    piece = w_out.shape[1] // PIECES

    def weight_piece(i):
        for dy in range(1, rows):
            at = (dy - 1) * PIECES + i
            part = pl.ds(i * piece, piece)
            to = device_at(dims, z, x, (y + dy) % rows, c)
            w_copies.append(send(w_out.at[:, part], side_out[dy - 1].at[:, part], s_w.at[at], r_w.at[at], to))

    used = -(-capacity // 8) * 8
    fills = []
    if used < stride:
        blank[...] = jnp.zeros_like(blank)
        for w in range(wide):
            fills.append(pltpu.make_async_copy(blank, ups.at[w, pl.ds(used, stride - used)], blanks.at[w]))
            fills[-1].start()

    half = PAIR // 2
    valid = valid_row[...].astype(F32)
    valid_col = column_of(valid)
    rank_row = priority[...].astype(F32)
    ahead = jnp.where(rank_row < column_of(rank_row), 1.0, 0.0).astype(LOW)
    first_at = column_of(routes[0:1].astype(F32)).astype(jnp.int32)
    second_at = column_of(routes[1:2].astype(F32)).astype(jnp.int32)
    hit_first, hit_second = lanes == first_at, lanes == second_at + half
    hot = jnp.where(hit_first | hit_second, valid_col, 0.0)
    earlier = dot(ahead, hot.astype(LOW))
    filled = pltpu.roll(jnp.sum(hot, axis=0, keepdims=True), half, 1)
    filled = jnp.broadcast_to(jnp.where(lanes[0:1] >= half, filled, 0.0), (8, PAIR))[0:1]
    earlier = earlier + filled
    place_a = jnp.sum(jnp.where(hit_first, earlier, 0.0), axis=1, keepdims=True).astype(jnp.int32)
    place_b = jnp.sum(jnp.where(hit_second, earlier, 0.0), axis=1, keepdims=True).astype(jnp.int32)
    kept_a = (place_a < capacity) & (valid_col > 0.5)
    kept_b = (place_b < capacity) & (valid_col > 0.5)
    slot_a = jnp.where(kept_a, first_at * stride + place_a, -1)
    slot_b = jnp.where(kept_b, second_at * stride + place_b, -1)
    slots = jnp.where(lanes == 0, slot_a, slot_b)
    slots_out[...] = jnp.where(lanes < 2, slots, jnp.where(lanes == 2, first_at, second_at))
    slot_rows[...] = jnp.transpose(slots.astype(F32))[0:8].astype(jnp.int32)


    row_at = lax.broadcasted_iota(jnp.int32, (stride, count), 0)

    def up_copy(d, to):
        body = pl.ds(0, used)
        return remote(up_send.at[to, body], ups.at[me, body], s_up.at[d], r_up.at[d], (to, n))

    def rows_for(expert):
        start = expert * stride
        hit = (slot_rows[0:1] - start == row_at) | (slot_rows[1:2] - start == row_at)
        return dot(jnp.where(hit, 1.0, 0.0).astype(LOW), cotangent[...]).astype(LOW)

    def give(d):
        to = ahead_of(dims, d)
        up_send[to] = rows_for(to)
        up_copy(d, to).start()

    def dispatch(k, carry):
        give(k + 1)
        return carry

    if not gathered:
        same_x = [(j + depth // 2 - 1) % (depth - 1) + 1 for j in range(depth - 1)]
        for step in range(1, depth):
            spread(step)
            corner(step - 1)
            if step >= 2:
                finish(step - 2)
        for j in same_x:
            give(across * j)
        corner(depth - 1)
        for i in range(PIECES):
            weight_piece(i)
        finish(depth - 2)
        finish(depth - 1)
        for j in [*same_x, 0]:
            for dx in range(1, across):
                give(across * j + dx)
    else:
        lax.fori_loop(0, wide - 1, dispatch, 0)
        keeps.append(pltpu.make_async_copy(pack_refs[0], params, local.at[0]))
        keeps[-1].start()
        for i in range(PIECES):
            weight_piece(i)
    segments = seg_row[...].astype(F32)
    keys_at = lax.broadcasted_iota(jnp.int32, (count, count), 1)
    rows_at = lax.broadcasted_iota(jnp.int32, (count, count), 0)
    allowed = (column_of(segments) == segments) & ((valid > 0.5) | (keys_at == rows_at))
    bias[...] = jnp.where(allowed, 0.0, MASKED)
    xhat, _ = norm_parts(tokens[...].astype(F32))
    total[...] = xhat
    lse[...] = jnp.zeros_like(lse)
    bias_t[...] = jnp.where(
        (column_of(segments) == segments) & ((valid_col > 0.5) | (keys_at == rows_at)), 0.0, MASKED
    )
    up_send[me] = rows_for(me)
    body = pl.ds(0, used)
    keep_up = pltpu.make_async_copy(up_send.at[me, body], ups.at[me, body], local.at[2])
    keep_up.start()
    for copy in by_core.values():
        copy.wait_recv()
    for copy in keeps:
        copy.wait()


    def columns(at):
        return params[:, at] if gathered else params[:, :, at].reshape(model, at.size)

    small = columns(pl.ds(4 * model, PAIR))
    vecs[...] = jnp.transpose(small.astype(F32))[experts : experts + 8]
    normed[...] = (total[...] * vecs[0:1] + vecs[1:2]).astype(LOW)

    def attend(pair, carry):
        at = lambda which: pl.ds(pl.multiple_of(which * model + pair * PAIR, PAIR), PAIR)
        here = at(0)
        source = normed[...]
        three = dot(source, jnp.concatenate([columns(at(0)), columns(at(1)), columns(at(2))], axis=1))
        queries = (three[:, :PAIR] + vecs[2:3, here]).astype(LOW) * LOW(HEAD**-0.5)
        keys = three[:, PAIR : 2 * PAIR].astype(LOW)
        values = (three[:, 2 * PAIR :] + vecs[3:4, here]).astype(LOW)
        q_out[:, here] = queries
        k_out[:, here] = keys
        v_out[:, here] = values
        mixed = None
        for part in range(2):
            side = (lanes < HEAD) if part == 0 else (lanes >= HEAD)
            own_keys = jnp.where(side, keys, LOW(0))
            own_values = jnp.where(side, values, LOW(0))
            scores = dot_nt(queries, own_keys) + bias[...]
            peak = jnp.max(scores, axis=1, keepdims=True)
            raised = jnp.exp(scores - peak)
            row_total = jnp.sum(raised, axis=1, keepdims=True)
            attn = (raised * (1.0 / row_total)).astype(LOW)
            piece = dot(attn, own_values)
            mixed = piece if mixed is None else mixed + piece
            lse[...] = jnp.where(lanes == 2 * pair + part, peak + jnp.log(row_total), lse[...])
        mixed = mixed.astype(LOW)
        attended[:, here] = mixed
        return carry

    lax.fori_loop(0, model // PAIR, attend, 0)

    def project(k, carry):
        here = pl.ds(pl.multiple_of(k * 2 * PAIR, PAIR), 2 * PAIR)
        there = pl.ds(pl.multiple_of(3 * model + k * 2 * PAIR, PAIR), 2 * PAIR)
        total[:, here] = dot(attended[...], columns(there))
        return carry

    lax.fori_loop(0, model // (2 * PAIR), project, 0)
    lse_rows[...] = jnp.transpose(lse[...])
    normed_t[...] = jnp.transpose(normed[...])
    attended_t[...] = jnp.transpose(attended[...])
    mid = tokens[...].astype(F32) + (total[...] + vecs[4:5])
    middle[...] = mid
    xhat, _ = norm_parts(mid)
    low = (xhat * vecs[5:6] + vecs[6:7]).astype(LOW)
    moe_low[...] = low
    moe_low_t[...] = jnp.transpose(low)
    logits = jnp.where(lanes < experts, dot(low, columns(pl.ds(4 * model, PAIR))), -jnp.inf)
    raised = jnp.exp(logits - jnp.max(logits, axis=1, keepdims=True))
    probs = raised / jnp.sum(raised, axis=1, keepdims=True)
    probs_out[...] = probs
    gate_a = jnp.sum(jnp.where(lanes == first_at, probs, 0.0), axis=1, keepdims=True)
    gate_b = jnp.sum(jnp.where(lanes == second_at, probs, 0.0), axis=1, keepdims=True)
    gates_out[...] = jnp.where(lanes == 0, gate_a, gate_b)

    def settle(k, carry):
        d = k + 1
        up_copy(d, ahead_of(dims, d)).wait_send()
        up_copy(d, behind_of(dims, d)).wait_recv()
        return carry

    lax.fori_loop(0, wide - 1, settle, 0)
    keep_up.wait()
    for copy in w_copies + b_copies + fills:
        copy.wait()
    for group in (first, by_x, by_y, half_a, half_b, by_core):
        for copy in group.values():
            copy.wait_send()


def front_stage(
    dims, experts, capacity, stride, gathered, pack, tokens, segment_ids, patch_valid, routes, priority,
    cotangent, w_out, in_bias,
):
    depth, across, rows, cores = dims
    wide, narrow = depth * across, rows * cores
    count, model = tokens.shape
    used = -(-capacity // 8) * 8
    any_, vmem = pl.BlockSpec(memory_space=pl.ANY), pl.BlockSpec(memory_space=pltpu.VMEM)
    low = lambda *shape: jax.ShapeDtypeStruct(shape, LOW)
    f32 = lambda *shape: jax.ShapeDtypeStruct(shape, F32)
    i32 = lambda *shape: jax.ShapeDtypeStruct(shape, jnp.int32)
    width = 4 * model + PAIR
    height = model if gathered else pack[0].shape[0]
    full = (height, width) if gathered else (wide * narrow, height, width)
    packed = 1 if gathered else height
    corners = depth * (across - 1) * (rows - 1)
    sems = []
    for size in (
        depth - 1, depth * (across - 1), depth * (rows - 1), corners, corners, depth * across * rows,
        wide, (rows - 1) * PIECES, narrow,
    ):
        sems += [pltpu.SemaphoreType.DMA((size,))] * 2
    outs = pl.pallas_call(
        functools.partial(front_kernel, dims, experts, capacity, gathered, len(pack)),
        out_shape=(
            low(*full), low(model, count), low(count, model), low(count, model), low(count, model),
            low(model, count), f32(PAIR, count), f32(count, model), low(count, model), low(model, count),
            f32(count, PAIR), f32(count, PAIR), f32(8, model), f32(count, count), i32(count, PAIR), i32(8, count),
            f32(narrow, 1, in_bias.shape[1]), low(wide, stride, model), *[low(*w_out.shape)] * (rows - 1),
        ),
        in_specs=([any_] if gathered else [any_, any_, vmem, vmem]) + [vmem] * 6 + [any_, vmem],
        out_specs=[vmem] * 17 + [any_] * rows,
        scratch_shapes=[
            pltpu.VMEM((count, model), LOW),
            pltpu.VMEM((count, model), LOW),
            pltpu.VMEM((count, model), F32),
            pltpu.VMEM((count, count), F32),
            pltpu.VMEM((count, PAIR), F32),
            pltpu.VMEM((wide, stride, model), LOW),
            pltpu.VMEM((1, in_bias.shape[1]), F32),
            pltpu.VMEM((packed, width), LOW),
            pltpu.VMEM((PAIR, PAIR), F32),
            pltpu.VMEM((max(stride - used, 8), model), LOW),
            *sems,
            pltpu.SemaphoreType.DMA((5,)),
            pltpu.SemaphoreType.DMA((wide,)),
        ],
        compiler_params=pltpu.CompilerParams(
            collective_id=0, has_side_effects=True, vmem_limit_bytes=VMEM_LIMIT
        ),
        cost_estimate=pl.CostEstimate(flops=7 * 10**9, bytes_accessed=20 * 10**6, transcendentals=4 * 10**6),
        name="front_stage",
    )(*pack, tokens, segment_ids, patch_valid, jnp.transpose(routes), priority, cotangent, w_out, in_bias)
    params = outs[0] if gathered else outs[0].reshape(wide * narrow * height, width)
    return params, outs[1:14], outs[14:18], outs[18:]


def norm_back(grad, gain, xhat, scale):
    scaled = grad * gain
    mean_a = jnp.mean(scaled, axis=-1, keepdims=True)
    mean_b = jnp.mean(scaled * xhat, axis=-1, keepdims=True)
    return scale * (scaled - mean_a - xhat * mean_b)


def back_kernel(dims, used, experts, gathered, *rest):
    depth, across, rows, cores = dims
    wide, narrow = depth * across, rows * cores
    (
        tokens, normed_t, queries, keys, values, attended_t, lse_rows, middle, _, moe_low_t, probs, gates, vecs, bias,
        weights, slots, token_rows, gate_slots, cotangent, y_rows,
    ) = rest[:20]
    side_grad = rest[20 : 19 + rows]
    rest = rest[19 + rows :]
    if gathered:
        block_out, tokens_grad, grad_here, group = rest[:4]
        rest = rest[4:]
    else:
        block_out, tokens_grad, grad_here, out_qkv, out_proj, out_router, *out_vecs = rest[:13]
        group, n1, n2, n3, n4 = rest[13:18]
        rest = rest[18:]
    branch, middle_grad, qkv_grad, sums, router, parts, y_here = rest[:7]
    s_y, q_y, s_g, q_g, local = rest[7:12]
    z, x, y, c = place_of(dims)
    me, n = z * across + x, y * cores + c
    count, model = tokens.shape
    stride = y_here.shape[1]
    pairs = model // PAIR
    per = 3 * PAIR
    n_proj = model // per
    small_at = n_proj + pairs
    lanes = lax.broadcasted_iota(jnp.int32, (count, PAIR), 1)

    def remote(src, dst, ssem, rsem, to):
        return pltpu.make_async_remote_copy(
            src_ref=src, dst_ref=dst, send_sem=ssem, recv_sem=rsem, device_id=to, device_id_type=MESH
        )

    peers = [((me + d) % wide, n) for d in range(1, wide)]
    peers += [device_at(dims, z, x, (y + d) % rows, c) for d in range(1, rows)]
    peers += [device_at(dims, z, x, y, 1 - c)]
    body = pl.ds(0, used)
    if used < stride:
        y_here[:, used:stride] = jnp.zeros((wide, stride - used, model), LOW)
    greet(peers)

    def y_copy(d, to):
        return remote(y_rows.at[to, body], y_here.at[me, body], s_y.at[d], q_y.at[d], (to, n))

    def give(k, carry):
        d = (k + wide // 2 - 1) % (wide - 1) + 1
        y_copy(d, ahead_of(dims, d)).start()
        return carry

    lax.fori_loop(0, wide - 1, give, 0)
    keep_y = pltpu.make_async_copy(y_rows.at[me, body], y_here.at[me, body], local.at[0])
    keep_y.start()
    piece = grad_here.shape[1] // PIECES

    def g_copies(i):
        copies = []
        for dy in range(1, rows):
            at = (dy - 1) * PIECES + i
            part = pl.ds(i * piece, piece)
            to = device_at(dims, z, x, (y + dy) % rows, c)
            copies.append(remote(side_grad[dy - 1].at[part], grad_here.at[dy - 1, part], s_g.at[at], q_g.at[at], to))
        return copies

    def give_grad(i):
        for copy in g_copies(i):
            copy.start()

    for i in range(PIECES):
        give_grad(i)

    if not gathered:
        s1, q1, s2, q2, s3, q3, s4, q4 = rest[12:20]
        height = group.shape[-2]

    def put(g, value):
        at = pl.ds(0, value.shape[1])
        value = value.astype(LOW)
        if gathered:
            group[g, :, at] = value
        else:
            group[g, :, :, :, :, :, at] = value.reshape(depth, across, rows, cores, height, at.size)

    def span(g):
        return pl.ds(0, PAIR) if isinstance(g, int) and g == small_at else pl.ds(0, per)

    def hop_core(g):
        return remote(
            group.at[g, :, :, :, 1 - c, :, span(g)], n1.at[g, :, :, :, :, span(g)], s1.at[g], q1.at[g],
            device_at(dims, z, x, y, 1 - c),
        )

    def hop_x(g, dx):
        at = g * (across - 1) + dx - 1
        return remote(
            n1.at[g, :, (x + dx) % across, :, :, span(g)], n2.at[at, :, :, :, span(g)],
            s2.at[at], q2.at[at], device_at(dims, z, (x + dx) % across, y, c),
        )

    def hop_y(g, dy):
        at = g * (rows - 1) + dy - 1
        return remote(
            n2.at[g * (across - 1), :, (y + dy) % rows, :, span(g)], n3.at[at, :, :, span(g)],
            s3.at[at], q3.at[at], device_at(dims, z, x, (y + dy) % rows, c),
        )

    def hop_z(g, dz):
        at = g * (depth - 1) + dz - 1
        return remote(
            n3.at[g * (rows - 1), (z + dz) % depth, :, span(g)], n4.at[at, :, span(g)],
            s4.at[at], q4.at[at], device_at(dims, (z + dz) % depth, x, y, c),
        )

    def start(g):
        if not gathered:
            hop_core(g).start()

    def begin(g):
        if gathered:
            return
        hop_core(g).wait_recv()
        w = span(g)
        n1[g, :, :, :, :, w] = (
            group[g, :, :, :, c, :, w].astype(F32) + n1[g, :, :, :, :, w].astype(F32)
        ).astype(LOW)
        for dx in range(1, across):
            hop_x(g, dx).start()

    def middle_of(g):
        if gathered:
            return
        w = span(g)
        at = g * (across - 1)
        acc = n1[g, :, x, :, :, w].astype(F32)
        for dx in range(1, across):
            hop_x(g, dx).wait_recv()
            acc = acc + n2[at + dx - 1, :, :, :, w].astype(F32)
        n2[at, :, :, :, w] = acc.astype(LOW)
        for dy in range(1, rows):
            hop_y(g, dy).start()

    def end(g):
        if gathered:
            return
        w = span(g)
        at = g * (rows - 1)
        for dy in range(1, rows):
            hop_y(g, dy).wait_recv()
        acc = n2[g * (across - 1), :, y, :, w].astype(F32)
        for dy in range(1, rows):
            acc = acc + n3[at + dy - 1, :, :, w].astype(F32)
        n3[at, :, :, w] = acc.astype(LOW)
        for dz in range(1, depth):
            hop_z(g, dz).start()

    def last(g):
        w = span(g)
        acc = n3[g * (rows - 1), z, :, w].astype(F32)
        for dz in range(1, depth):
            hop_z(g, dz).wait_recv()
            acc = acc + n4[g * (depth - 1) + dz - 1, :, w].astype(F32)
        return acc

    sums[...] = jnp.zeros_like(sums)
    slot_a, slot_b = slots[:, 0:1], slots[:, 1:2]
    slot_at = lax.broadcasted_iota(jnp.int32, (count, wide * stride), 1)
    third = PAIR // 4
    lane_at = lax.broadcasted_iota(jnp.int32, (stride, PAIR), 1)

    def split(w, carry):
        value = column_of(gate_slots[w])[0:stride]
        high = value.astype(LOW).astype(F32)
        mid = (value - high).astype(LOW).astype(F32)
        low = value - high - mid
        row = jnp.where(lane_at == w, high, 0.0) + jnp.where(lane_at == third + w, mid, 0.0)
        parts[w] = (row + jnp.where(lane_at == 2 * third + w, low, 0.0)).astype(LOW)
        return carry

    lax.fori_loop(0, wide, split, 0)
    picks = jnp.where((slot_at == slot_a) | (slot_at == slot_b), 1.0, 0.0).astype(LOW)
    picked = dot(picks, parts[...].reshape(wide * stride, PAIR))
    prob_grad = picked + pltpu.roll(picked, PAIR - third, 1) + pltpu.roll(picked, PAIR - 2 * third, 1)
    own = probs[...]
    prob_grad = jnp.where(lanes < experts, prob_grad, 0.0)
    logit_grad = (own * (prob_grad - jnp.sum(prob_grad * own, axis=1, keepdims=True))).astype(LOW)
    router[...] = dot(moe_low_t[...], logit_grad)
    moe_grad = dot(picks, token_rows[...].reshape(wide * stride, model)) + dot_nt(
        logit_grad, weights[:, 4 * model : 4 * model + PAIR]
    )
    xhat, scale = norm_parts(middle[...])
    sums[5:6] = jnp.sum(moe_grad * xhat, axis=0, keepdims=True)
    sums[6:7] = jnp.sum(moe_grad, axis=0, keepdims=True)
    mid = cotangent[...].astype(F32) + norm_back(moe_grad, vecs[5:6], xhat, scale)
    middle_grad[...] = mid
    branch[...] = mid.astype(LOW)
    sums[4:5] = jnp.sum(branch[...].astype(F32), axis=0, keepdims=True)
    for g in range(n_proj):
        put(g, dot(attended_t[...], branch[:, g * per : (g + 1) * per]))
        start(g)
    begin(0)

    sides = lax.broadcasted_iota(jnp.int32, (PAIR, count), 0)

    def attend(pair, carry):
        at = lambda which: pl.ds(pl.multiple_of(which * model + pair * PAIR, PAIR), PAIR)
        here = at(0)
        grad_mixed = dot_nt(branch[...], weights[here, 3 * model : 4 * model]).astype(LOW)
        q_pair, k_pair, v_pair = queries[:, here], keys[:, here], values[:, here]
        k_turned = jnp.transpose(k_pair)
        q_grad_t, k_grad, v_grad = None, None, None
        for part in range(2):
            side = (lanes < HEAD) if part == 0 else (lanes >= HEAD)
            side_t = (sides < HEAD) if part == 0 else (sides >= HEAD)
            own_keys = jnp.where(side, k_pair, LOW(0))
            own_values = jnp.where(side, v_pair, LOW(0))
            own_queries = jnp.where(side, q_pair, LOW(0))
            own_grads = jnp.where(side, grad_mixed, LOW(0))
            own_turned = jnp.where(side_t, k_turned, LOW(0))
            scores = dot_nt(own_keys, q_pair) + bias[...]
            attn = jnp.exp(scores - lse_rows[pl.ds(2 * pair + part, 1), :])
            attn_grad = dot_nt(own_values, grad_mixed)
            mean = jnp.sum(attn * attn_grad, axis=0, keepdims=True)
            score_grad = (attn * (attn_grad - mean)).astype(LOW)
            v_part = dot(attn.astype(LOW), own_grads)
            k_part = dot(score_grad, own_queries)
            q_part = dot(own_turned, score_grad)
            if part == 0:
                q_grad_t, k_grad, v_grad = q_part, k_part, v_part
            else:
                q_grad_t, k_grad, v_grad = q_grad_t + q_part, k_grad + k_part, v_grad + v_part
        q_grad = (jnp.transpose(q_grad_t) * HEAD**-0.5).astype(LOW)
        k_grad = k_grad.astype(LOW)
        v_grad = v_grad.astype(LOW)
        sums[2:3, here] = jnp.sum(q_grad.astype(F32), axis=0, keepdims=True)
        sums[3:4, here] = jnp.sum(v_grad.astype(F32), axis=0, keepdims=True)
        g = pair + n_proj
        for which, part in enumerate((q_grad, k_grad, v_grad)):
            qkv_grad[:, at(which)] = part
        put(g, dot(normed_t[...], jnp.concatenate([q_grad, k_grad, v_grad], axis=1)))
        start(g)
        if not gathered:
            begin(g - 1)

            @pl.when(g >= 5)
            def _():
                middle_of(g - 5)

            @pl.when(g >= 7)
            def _():
                end(g - 7)

        return carry

    lax.fori_loop(0, pairs, attend, 0)
    begin(small_at - 1)
    grad = dot_nt(qkv_grad[...], weights[:, : 3 * model])
    xhat, scale = norm_parts(tokens[...].astype(F32))
    sums[0:1] = jnp.sum(grad * xhat, axis=0, keepdims=True)
    sums[1:2] = jnp.sum(grad, axis=0, keepdims=True)
    stacked = jnp.concatenate([sums[...], jnp.zeros((PAIR - 8, model), F32)], axis=0)
    turned = pltpu.roll(jnp.transpose(stacked), experts, 1)
    wide_lanes = lax.broadcasted_iota(jnp.int32, (model, PAIR), 1)
    put(small_at, jnp.where(wide_lanes < experts, router[...], turned))
    start(small_at)
    for g in range(small_at - 5, small_at - 2):
        middle_of(g)
    for g in range(small_at - 7, small_at - 3):
        end(g)
    tokens_grad[...] = (middle_grad[...] + norm_back(grad, vecs[0:1], xhat, scale)).astype(LOW)
    begin(small_at)
    middle_of(small_at - 2)
    end(small_at - 3)
    middle_of(small_at - 1)
    middle_of(small_at)
    end(small_at - 2)
    end(small_at - 1)
    end(small_at)

    def taken(k, carry):
        d = k + 1
        y_copy(d, ahead_of(dims, d)).wait_send()
        y_copy(d, behind_of(dims, d)).wait_recv()
        return carry

    lax.fori_loop(0, wide - 1, taken, 0)
    keep_y.wait()
    returned = y_here[...].reshape(wide * stride, model)
    mixed = gates[:, 0:1] * dot(jnp.where(slot_at == slot_a, 1.0, 0.0).astype(LOW), returned)
    mixed += gates[:, 1:2] * dot(jnp.where(slot_at == slot_b, 1.0, 0.0).astype(LOW), returned)
    block_out[...] = (middle[...] + mixed).astype(LOW)
    if not gathered:
        for g in range(n_proj):
            out_proj[:, g * per : (g + 1) * per] = last(g)
        for pair in range(pairs):
            summed = last(n_proj + pair)
            for which in range(3):
                at = which * model + pair * PAIR
                out_qkv[:, at : at + PAIR] = summed[:, which * PAIR : (which + 1) * PAIR]
        summed = last(small_at)
        square = jnp.concatenate([summed, jnp.zeros((PAIR - height, PAIR), F32)], axis=0)
        turned = jnp.transpose(square)
        out_router[...] = turned[0:experts, 0:height]
        for i, ref in enumerate(out_vecs):
            ref[...] = turned[experts + i : experts + i + 1, 0:height]
        for g in range(small_at + 1):
            hop_core(g).wait_send()
            for dx in range(1, across):
                hop_x(g, dx).wait_send()
            for dy in range(1, rows):
                hop_y(g, dy).wait_send()
            for dz in range(1, depth):
                hop_z(g, dz).wait_send()
    for i in range(PIECES):
        for copy in g_copies(i):
            copy.wait()


def back_stage(
    dims, used, experts, gathered, tokens, saved, params, slots, token_rows, gate_slots, cotangent, y_rows, side_grads,
):
    depth, across, rows, cores = dims
    wide, narrow = depth * across, rows * cores
    count, model = tokens.shape
    stride = y_rows.shape[1]
    per = 3 * PAIR
    groups = model // per + model // PAIR + 1
    height = model // (wide * narrow)
    any_, vmem = pl.BlockSpec(memory_space=pl.ANY), pl.BlockSpec(memory_space=pltpu.VMEM)
    low = lambda *shape: jax.ShapeDtypeStruct(shape, LOW)
    f32 = lambda *shape: jax.ShapeDtypeStruct(shape, F32)
    sem = lambda size: [pltpu.SemaphoreType.DMA((size,))] * 2
    outs = [low(count, model), low(count, model), low(rows - 1, *side_grads[0].shape)]
    buffers, sems = [], []
    if gathered:
        outs.append(low(groups, model, per))
    else:
        outs += [f32(height, 3 * model), f32(height, model), f32(experts, height), *[f32(1, height)] * 7]
        buffers = [
            pltpu.VMEM((groups, depth, across, rows, cores, height, per), LOW),
            pltpu.VMEM((groups, depth, across, rows, height, per), LOW),
            pltpu.VMEM((groups * (across - 1), depth, rows, height, per), LOW),
            pltpu.VMEM((groups * (rows - 1), depth, height, per), LOW),
            pltpu.VMEM((groups * (depth - 1), height, per), LOW),
        ]
        sems = [
            *sem(groups), *sem(groups * (across - 1)), *sem(groups * (rows - 1)), *sem(groups * (depth - 1)),
        ]
    return pl.pallas_call(
        functools.partial(back_kernel, dims, used, experts, gathered),
        out_shape=tuple(outs),
        in_specs=[vmem] * 8 + [any_] + [vmem] * 10 + [any_] * rows,
        out_specs=[vmem] * 2 + [any_] + [vmem] * (len(outs) - 3),
        scratch_shapes=[
            *buffers,
            pltpu.VMEM((count, model), LOW),
            pltpu.VMEM((count, model), F32),
            pltpu.VMEM((count, 3 * model), LOW),
            pltpu.VMEM((8, model), F32),
            pltpu.VMEM((model, PAIR), F32),
            pltpu.VMEM((wide, stride, PAIR), LOW),
            pltpu.VMEM((wide, stride, model), LOW),
            *sem(wide), *sem((rows - 1) * PIECES),
            pltpu.SemaphoreType.DMA((1,)),
            *sems,
        ],
        compiler_params=pltpu.CompilerParams(
            collective_id=1, has_side_effects=True, vmem_limit_bytes=60 * 1024 * 1024
        ),
        cost_estimate=pl.CostEstimate(flops=16 * 10**9, bytes_accessed=40 * 10**6, transcendentals=4 * 10**6),
        name="back_stage",
    )(
        tokens, *saved, params, slots, token_rows, gate_slots, cotangent, y_rows, *side_grads
    )


def tail_kernel(count, *refs):
    inputs, own, other_out, refs = refs[:count], refs[count], refs[count + 1], refs[count + 2 :]
    rows = other_out.shape[0] + 1
    other_in, refs = refs[: rows - 1], refs[rows - 1 :]
    outputs, grad_in, grad_out = refs[:count], refs[count], refs[count + 1]
    terms, first, second, sems, loads, brings = refs[count + 2 : count + 8]
    held = refs[count + 8 :]
    arrivals = [pltpu.make_async_copy(own, terms.at[0], loads.at[0])]
    for i in range(1, rows):
        arrivals.append(pltpu.make_async_copy(other_in[i - 1], terms.at[i, 0], loads.at[2 * i - 1]))
        arrivals.append(pltpu.make_async_copy(other_out.at[i - 1], terms.at[i, 1], loads.at[2 * i]))
    bring = [pltpu.make_async_copy(src, dst, brings.at[i]) for i, (src, dst) in enumerate(zip(inputs, held))]
    copies = [pltpu.make_async_copy(src, dst, sems.at[i]) for i, (src, dst) in enumerate(zip(held, outputs))]
    for copy in arrivals + bring:
        copy.start()
    for copy in arrivals:
        copy.wait()

    def total(which):
        acc = terms[0, which].astype(F32)
        for i in range(1, rows):
            acc = acc + terms[i, which].astype(F32)
        return acc

    first[0] = total(0)
    copies.append(pltpu.make_async_copy(first, grad_in, sems.at[count]))
    copies[-1].start()
    for into, out in zip(bring, copies):
        into.wait()
        out.start()
    second[0] = jnp.transpose(total(1))
    copies.append(pltpu.make_async_copy(second, grad_out, sems.at[count + 1]))
    copies[-1].start()
    for copy in copies:
        copy.wait()


def tail_stage(arrays, own, other_out, other_in):
    any_ = pl.BlockSpec(memory_space=pl.ANY)
    _, model, ff = own.shape
    count = len(arrays)
    shapes = [jax.ShapeDtypeStruct(a.shape, a.dtype) for a in arrays]
    shapes += [jax.ShapeDtypeStruct((1, model, ff), F32), jax.ShapeDtypeStruct((1, ff, model), F32)]
    rows = other_out.shape[0] + 1
    return pl.pallas_call(
        functools.partial(tail_kernel, count),
        out_shape=tuple(shapes),
        in_specs=[any_] * (count + 1 + rows),
        out_specs=[any_] * (count + 2),
        scratch_shapes=[
            pltpu.VMEM((rows, 2, model, ff), LOW),
            pltpu.VMEM((1, model, ff), F32),
            pltpu.VMEM((1, ff, model), F32),
            pltpu.SemaphoreType.DMA((count + 2,)),
            pltpu.SemaphoreType.DMA((2 * rows - 1,)),
            pltpu.SemaphoreType.DMA((count,)),
            *[pltpu.VMEM(a.shape, a.dtype) for a in arrays],
        ],
        compiler_params=pltpu.CompilerParams(vmem_limit_bytes=58 * 1024 * 1024),
        name="results",
    )(*arrays, own, other_out, *other_in)


def gelu_and_slope(v):
    root = 0.7978845608028654
    cubic = 0.044715
    square = v * v
    half = 0.5 * jnp.tanh(v * (root + (root * cubic) * square)) + 0.5
    value = v * half
    slope = half + value * ((1.0 - half) * (2.0 * root + (6.0 * root * cubic) * square))
    return value, slope


def moe_kernel(
    dims, used, moe_low, slot_rows, slot_cols, gates, ups, b_in, b_out, w_in, w_out, *rest
):
    depth, across, rows, cores = dims
    wide = depth * across
    narrow = rows * cores
    side_out = rest[: rows - 1]
    rest = rest[rows - 1 :]
    token_rows, gate_slots, y_out, in_bias_grad, out_bias_grad = rest[:5]
    own_grad = rest[5]
    side_in, side_grad = rest[6 : 5 + rows], rest[5 + rows : 4 + 2 * rows]
    (
        full_in, full_out, x_send, x_here, g_send, g_here, dx_send, h_send, hidden, pre_grad, weighted,
        x_turned, w_turned, grad_send, grad_here, extra, extra_here, extra_y, blank, dx_part, back_part,
        local, blanks, s_wy, r_wy, s_y, r_y, s_ey, r_ey, s_in, r_in, s_out, r_out, s_x, r_x, s_g, r_g, s_dx, r_dx, s_h, r_h, s_w, r_w, s_e, r_e,
    ) = rest[4 + 2 * rows :]
    z, x, y, c = place_of(dims)
    me, n = z * across + x, y * cores + c
    count, model = moe_low.shape
    capacity = x_send.shape[1]
    gate_width = g_send.shape[2]
    ff = full_in.shape[2]
    other = device_at(dims, z, x, y, 1 - c)

    def remote(src, dst, ssem, rsem, to):
        return pltpu.make_async_remote_copy(
            src_ref=src, dst_ref=dst, send_sem=ssem, recv_sem=rsem, device_id=to, device_id_type=MESH
        )

    along_y = [device_at(dims, z, x, (y + i) % rows, c) for i in range(1, rows)]
    body = pl.ds(0, used)
    if used < capacity:
        x_here[:, used:capacity] = jnp.zeros((wide, capacity - used, model), LOW)
        blank[...] = jnp.zeros_like(blank)
    greet([((me + d) % wide, n) for d in range(1, wide)] + [other] + along_y)
    fills = []
    if used < capacity:
        for w in range(wide):
            fills.append(pltpu.make_async_copy(blank, token_rows.at[w, pl.ds(used, capacity - used)], blanks.at[w]))

    held = [((y - i) % rows) * cores + c for i in range(rows)]
    from_y, in_passes, out_loads, out_passes = [], [], [], []
    for i, h in enumerate(held):
        src_out = w_out.at[0] if i == 0 else side_out[i - 1].at[0]
        out_loads.append(pltpu.make_async_copy(src_out, full_out.at[h], local.at[i]))
        out_passes.append(remote(src_out, full_out.at[h], s_out.at[i], r_out.at[i], other))
        if i:
            from_y.append(remote(w_in.at[0], full_in.at[n], s_wy.at[i - 1], r_wy.at[i - 1], along_y[i - 1]))
        src_in = w_in.at[0] if i == 0 else full_in.at[h]
        in_passes.append(remote(src_in, full_in.at[h], s_in.at[i], r_in.at[i], other))
    in_load = pltpu.make_async_copy(w_in.at[0], full_in.at[n], local.at[rows])
    for copy in from_y + out_loads + out_passes:
        copy.start()

    slot_a, slot_b = slot_cols[:, 0:1], slot_cols[:, 1:2]
    gate_a, gate_b = gates[:, 0:1], gates[:, 1:2]
    row_at = lax.broadcasted_iota(jnp.int32, (capacity, count), 0)
    lane_at = lax.broadcasted_iota(jnp.int32, (count, gate_width), 1)
    source = moe_low[...]

    def rows_for(expert):
        first = expert * capacity
        hit = (slot_rows[0:1] - first == row_at) | (slot_rows[1:2] - first == row_at)
        picked = dot(jnp.where(hit, 1.0, 0.0).astype(LOW), source).astype(LOW)
        inside = lane_at < capacity
        hit_a = (slot_a - first == lane_at) & inside
        hit_b = (slot_b - first == lane_at) & inside
        gate = jnp.where(hit_a, gate_a, 0.0) + jnp.where(hit_b, gate_b, 0.0)
        return picked, jnp.sum(gate, axis=0, keepdims=True)

    def x_copy(d, to):
        return remote(x_send.at[to, body], x_here.at[me, body], s_x.at[d], r_x.at[d], (to, n))

    def g_copy(d, to):
        return remote(g_send.at[to], g_here.at[me], s_g.at[d], r_g.at[d], (to, n))

    def dx_copy(d, to):
        return remote(dx_send.at[to, body], token_rows.at[me, body], s_dx.at[d], r_dx.at[d], (to, n))

    def h_copy(d, to):
        return remote(h_send.at[to], gate_slots.at[me], s_h.at[d], r_h.at[d], (to, n))

    def dispatch(k, carry):
        d = (k + wide // 2 - 1) % (wide - 1) + 1
        to = ahead_of(dims, d)
        picked, gate = rows_for(to)
        x_send[to] = picked
        g_send[to] = gate
        x_copy(d, to).start()
        g_copy(d, to).start()
        return carry

    lax.fori_loop(0, wide - 1, dispatch, 0)
    in_load.start()
    in_passes[0].start()
    for copy in fills:
        copy.start()
    picked, gate = rows_for(me)
    x_here[me] = picked
    g_here[me] = gate
    extra[...] = jnp.zeros_like(extra)
    out_bias = b_out[...].astype(F32)
    for copy in out_loads:
        copy.wait()

    def backs_of(places):
        def backs(k, carry):
            two = pl.ds(2 * k, 2)
            up = ups[two].reshape(2 * capacity, model)
            for h in places:
                lanes = pl.ds(pl.multiple_of(h * ff, PAIR), ff)
                pre_grad[two, :, lanes] = dot_nt(up, full_out[h]).astype(LOW).reshape(2, capacity, ff)
            return carry

        return backs

    lax.fori_loop(0, wide // 2, backs_of([i * cores + c for i in range(rows)]), 0)
    for copy in out_passes:
        copy.wait_recv()
    lax.fori_loop(0, wide // 2, backs_of([i * cores + 1 - c for i in range(rows)]), 0)
    in_load.wait()
    in_passes[0].wait_recv()

    def expert(src, places, slot=None, first=True, final=True):
        own = x_here[src]
        up = ups[src]
        gate = jnp.transpose(jnp.broadcast_to(g_here[src], (PAIR, gate_width)))[:capacity, 0:1]
        if first:
            weighted[src] = (gate * up.astype(F32)).astype(LOW)
            back_total = jnp.sum(up.astype(F32) * out_bias, axis=1, keepdims=True)
            dx = None
        else:
            back_total = back_part[slot, :, 0:1]
            dx = dx_part[slot]
        for h in places:
            lanes = pl.ds(h * ff if isinstance(h, int) else pl.multiple_of(h * ff, PAIR), ff)
            pre = dot(own, full_in[h]) + b_in[h]
            back = pre_grad[src, :, lanes].astype(F32)
            value, slope = gelu_and_slope(pre)
            hidden[src, :, lanes] = value.astype(LOW)
            back_total += jnp.sum(value * back, axis=1, keepdims=True)
            wide_grad = slope * (gate * back)
            grad = wide_grad.astype(LOW)
            pre_grad[src, :, lanes] = grad
            extra[h, 0:1, :ff] += jnp.sum(wide_grad, axis=0, keepdims=True)
            part = dot_nt(grad, full_in[h])
            dx = part if dx is None else dx + part
        if final:
            dx_send[src] = dx.astype(LOW)
            spread = jnp.broadcast_to(back_total, (capacity, PAIR))
            spread = jnp.concatenate([spread, jnp.zeros((gate_width - capacity, PAIR), F32)], axis=0)
            h_send[src] = jnp.transpose(spread)[0:1]
        else:
            dx_part[slot] = dx
            back_part[slot] = jnp.broadcast_to(back_total, (capacity, PAIR))

    def source_of(k):
        d = (k + wide // 2 - 1) % (wide - 1) + 1
        return d, behind_of(dims, d)

    def land(k):
        d, src = source_of(k)
        x_copy(d, src).wait_recv()
        g_copy(d, src).wait_recv()
        return src

    def give_back(k):
        d, src = source_of(k)
        dx_copy(d, src).start()
        h_copy(d, src).start()

    near = [y * cores + i for i in range(cores)]
    far = [(y + i) % rows * cores + j for i in range(1, rows) for j in range(cores)]
    early = dx_part.shape[0] - 1
    expert(me, near, 0, final=False)

    def begin(k, carry):
        expert(land(k), near, k + 1, final=False)
        return carry

    lax.fori_loop(0, early, begin, 0)
    for i in range(1, rows):
        from_y[i - 1].wait_recv()
        in_passes[i].start()
    for copy in in_passes[1:]:
        copy.wait_recv()

    def complete(k, carry):
        expert(source_of(k)[1], far, k + 1, first=False)
        return carry

    def serve(k, carry):
        expert(land(k), range(narrow))

        @pl.when(k >= LAG)
        def _():
            give_back(k - LAG)

        return carry

    lax.fori_loop(0, early, complete, 0)
    expert(me, far, 0, first=False)
    keep_rows = pltpu.make_async_copy(dx_send.at[me, body], token_rows.at[me, body], local.at[2 * rows])
    keep_gate = pltpu.make_async_copy(h_send.at[me], gate_slots.at[me], local.at[2 * rows + 1])
    keep_rows.start()
    keep_gate.start()
    lax.fori_loop(early, wide - 1, serve, 0)

    def give_rest(k, carry):
        give_back(k)
        return carry

    lax.fori_loop(wide - 1 - LAG, wide - 1, give_rest, 0)

    all_rows = wide * capacity
    x_turned[...] = jnp.transpose(x_here[...].reshape(all_rows, model))
    w_turned[...] = jnp.transpose(weighted[...].reshape(all_rows, model))
    bias_grad = jnp.sum(weighted[...].reshape(all_rows, model).astype(F32), axis=0, keepdims=True)
    for h in range(narrow):
        extra[h, 1:2] = bias_grad

    def grad_of(which, h):
        lanes = pl.ds(pl.multiple_of(h * ff, PAIR), ff)
        if which == 0:
            return dot(x_turned[...], pre_grad[:, :, lanes].reshape(all_rows, ff))
        return dot(w_turned[...], hidden[:, :, lanes].reshape(all_rows, ff))

    order = [*range(1, rows), 0]
    swaps, by_y, keep_grads = [], [], []
    for i in order:
        at = (y + i) % rows
        kept, given = at * cores + c, at * cores + 1 - c
        for which in range(2):
            k = 2 * i + which
            grad_send[i, which] = grad_of(which, given).astype(LOW)
            swap = remote(grad_send.at[i, which], grad_here.at[i, which], s_w.at[k], r_w.at[k], other)
            swap.start()
            swaps.append(swap)
            if which == 0:
                swap_extra = remote(extra.at[given], extra_here.at[i], s_e.at[i], r_e.at[i], other)
                swap_extra.start()
                swaps.append(swap_extra)
            grad = grad_of(which, kept)
            swap.wait_recv()
            grad_here[i, which] = (grad + grad_here[i, which].astype(F32)).astype(LOW)
            if which == 0:
                swap_extra.wait_recv()
                extra_here[i] = extra_here[i] + extra[kept]
            if i and which == 0:
                by_y.append(
                    remote(grad_here.at[i, 0], side_in[i - 1], s_y.at[i - 1], r_y.at[i - 1], along_y[i - 1])
                )
                by_y[-1].start()
                by_y.append(
                    remote(extra_here.at[i], extra_y.at[i - 1], s_ey.at[i - 1], r_ey.at[i - 1], along_y[i - 1])
                )
                by_y[-1].start()
        source, target = (grad_here.at[i, 1], side_grad[i - 1]) if i else (grad_here.at[0], own_grad)
        keep_grads.append(pltpu.make_async_copy(source, target, local.at[2 * rows + 3 + i]))
        keep_grads[-1].start()

    some = 4

    def outputs(k, carry):
        total = None
        at = pl.ds(k * some, some)
        for h in range(narrow):
            part = dot(hidden[at, :, h * ff : (h + 1) * ff].reshape(some * capacity, ff), full_out[h])
            total = part if total is None else total + part
        x_send[at] = (total + out_bias).astype(LOW).reshape(some, capacity, model)
        return carry

    def sent(k, carry):
        to = ahead_of(dims, k + 1)
        x_copy(k + 1, to).wait_send()
        g_copy(k + 1, to).wait_send()
        return carry

    lax.fori_loop(0, wide - 1, sent, 0)
    lax.fori_loop(0, wide // some, outputs, 0)
    keep_y = pltpu.make_async_copy(x_send, y_out, local.at[2 * rows + 2])
    keep_y.start()
    bias_rows = extra_here[0]
    for copy in by_y:
        copy.wait_recv()
    for i in range(1, rows):
        bias_rows = bias_rows + extra_y[i - 1]
    in_bias_grad[...] = bias_rows[0:1, :ff]
    out_bias_grad[...] = bias_rows[1:2]

    def finish(k, carry):
        d = k + 1
        back = behind_of(dims, d)
        dx_copy(d, back).wait_recv()
        h_copy(d, back).wait_recv()
        dx_copy(d, back).wait_send()
        h_copy(d, back).wait_send()
        return carry

    lax.fori_loop(0, wide - 1, finish, 0)
    for copy in from_y + in_passes + out_passes + swaps + by_y:
        copy.wait_send()
    for copy in fills:
        copy.wait()
    for copy in [keep_rows, keep_gate, keep_y] + keep_grads:
        copy.wait()


def moe_stage(dims, used, capacity, moe_low, slot_rows, slots, gates, ups, b_in, b_out, w_in, w_out, side_out):
    depth, across, rows, cores = dims
    wide, narrow = depth * across, rows * cores
    count, model = moe_low.shape
    ff = w_in.shape[2]
    gate_width = -(-capacity // PAIR) * PAIR
    any_, vmem = pl.BlockSpec(memory_space=pl.ANY), pl.BlockSpec(memory_space=pltpu.VMEM)
    low = lambda *shape: jax.ShapeDtypeStruct(shape, LOW)
    f32 = lambda *shape: jax.ShapeDtypeStruct(shape, F32)
    sem = lambda size: [pltpu.SemaphoreType.DMA((size,))] * 2
    outs = pl.pallas_call(
        functools.partial(moe_kernel, dims, used),
        out_shape=(
            low(wide, capacity, model), f32(wide, 1, gate_width), low(wide, capacity, model),
            f32(1, ff), f32(1, model), low(2, model, ff), *[low(model, ff)] * (2 * rows - 2),
        ),
        in_specs=[vmem] * 7 + [any_] * (1 + rows),
        out_specs=[any_] * 3 + [vmem] * 2 + [any_] * (2 * rows - 1),
        scratch_shapes=[
            pltpu.VMEM((narrow, model, ff), LOW),
            pltpu.VMEM((narrow, ff, model), LOW),
            pltpu.VMEM((wide, capacity, model), LOW),
            pltpu.VMEM((wide, capacity, model), LOW),
            pltpu.VMEM((wide, 1, gate_width), F32),
            pltpu.VMEM((wide, 1, gate_width), F32),
            pltpu.VMEM((wide, capacity, model), LOW),
            pltpu.VMEM((wide, 1, gate_width), F32),
            pltpu.VMEM((wide, capacity, narrow * ff), LOW),
            pltpu.VMEM((wide, capacity, narrow * ff), LOW),
            pltpu.VMEM((wide, capacity, model), LOW),
            pltpu.VMEM((model, wide * capacity), LOW),
            pltpu.VMEM((model, wide * capacity), LOW),
            pltpu.VMEM((rows, 2, model, ff), LOW),
            pltpu.VMEM((rows, 2, model, ff), LOW),
            pltpu.VMEM((narrow, 8, model), F32),
            pltpu.VMEM((rows, 8, model), F32),
            pltpu.VMEM((rows - 1, 8, model), F32),
            pltpu.VMEM((max(capacity - used, 8), model), LOW),
            pltpu.VMEM((1 + min(EARLY, wide - 1), capacity, model), F32),
            pltpu.VMEM((1 + min(EARLY, wide - 1), capacity, PAIR), F32),
            pltpu.SemaphoreType.DMA((3 * rows + 3,)),
            pltpu.SemaphoreType.DMA((wide,)),
            *sem(rows), *sem(rows), *sem(rows), *sem(rows), *sem(rows), *sem(wide), *sem(wide), *sem(wide), *sem(wide), *sem(2 * rows), *sem(rows),
        ],
        compiler_params=pltpu.CompilerParams(
            collective_id=2, has_side_effects=True, vmem_limit_bytes=60 * 1024 * 1024
        ),
        cost_estimate=pl.CostEstimate(flops=36 * 10**9, bytes_accessed=25 * 10**6, transcendentals=4 * 10**6),
        name="moe_stage",
    )(moe_low, slot_rows, slots, gates, ups, b_in, b_out, w_in, w_out, *side_out)
    return outs[:3], outs[3:5], outs[5], outs[6 : 5 + rows], outs[5 + rows :]


def per_device(
    dims,
    tokens, segment_ids, patch_valid, routes, priority, gain_attn, shift_attn, w_qkv, query_bias, value_bias,
    w_proj, proj_bias, gain_moe, shift_moe, w_router, w_in, in_bias, w_out, out_bias, cotangent,
):
    count, model = tokens.shape
    experts = w_router.shape[1]
    capacity = (210 * count + 100 * experts - 1) // (100 * experts)
    shard_rows = gain_attn.shape[0]
    vectors = jnp.stack([gain_attn, shift_attn, query_bias, value_bias, proj_bias, gain_moe, shift_moe])
    stride = -(-capacity // 16) * 16
    gathered = shard_rows % 8 != 0
    every = ("wide", "narrow")
    if gathered:
        empty = jnp.zeros((shard_rows, PAIR - 7 - experts), LOW)
        pack = jnp.concatenate([w_qkv, w_proj, w_router, jnp.transpose(vectors), empty], axis=1)
        pack = [lax.all_gather(pack, every, axis=0, tiled=True)]
    else:
        pack = [w_qkv, w_proj, jnp.transpose(w_router), vectors]
    params, saved, (slots, slot_rows, full_b_in, ups), side_out = front_stage(
        dims, experts, capacity, stride, gathered, pack, tokens, segment_ids, patch_valid, routes, priority,
        cotangent, w_out, in_bias,
    )
    moe_low, gates = saved[7], saved[10]
    used = -(-capacity // 8) * 8
    (token_rows, gate_slots, y_rows), bias_grads, own_grad, other_in, side_grads = moe_stage(
        dims, used, stride, moe_low, slot_rows, slots, gates, ups, full_b_in, out_bias, w_in, w_out, side_out
    )
    outs = back_stage(
        dims, used, experts, gathered, tokens, saved, params, slots, token_rows, gate_slots, cotangent, y_rows, side_grads,
    )
    settled = tail_stage([*outs[:2], *outs[3:], *bias_grads], own_grad, outs[2], other_in)
    outs, (grad_in_bias, grad_out_bias, grad_w_in, grad_w_out) = settled[:-4], settled[-4:]
    block_out, tokens_grad = outs[:2]
    if gathered:
        groups = lax.psum_scatter(outs[2].astype(F32), every, scatter_dimension=1, tiled=True)
        n_proj = model // (3 * PAIR)
        grad_proj = jnp.concatenate(list(groups[:n_proj]), axis=1)
        by_head = groups[n_proj:-1].reshape(-1, shard_rows, 3, PAIR)
        grad_qkv = by_head.transpose(1, 2, 0, 3).reshape(shard_rows, -1)
        grad_router = groups[-1, :, :experts]
        vector = [groups[-1, :, experts + i] for i in range(7)]
    else:
        grad_qkv, grad_proj, grad_router = outs[2:5]
        grad_router = jnp.transpose(grad_router)
        vector = [row.reshape(-1) for row in outs[5:]]
    return (
        block_out,
        tokens_grad,
        vector[0],
        vector[1],
        grad_qkv,
        vector[2],
        vector[3],
        grad_proj,
        vector[4],
        vector[5],
        vector[6],
        grad_router,
        grad_w_in,
        grad_in_bias,
        grad_w_out,
        grad_out_bias,
    )


def solution(mesh):
    dims = grid_of(mesh.shape["wide"], mesh.shape["narrow"])
    every = ("wide", "narrow")
    rows, vector = P(every, None), P(every)
    return jax.shard_map(
        functools.partial(per_device, dims),
        mesh=mesh,
        in_specs=(
            rows, rows, rows, rows, rows, vector, vector, rows, vector, vector, rows, vector, vector, vector,
            rows, P("wide", None, "narrow"), P("wide", "narrow"), P("wide", "narrow", None), P("wide", None), rows,
        ),
        out_specs=(
            rows, rows, vector, vector, rows, vector, vector, rows, vector, vector, vector, rows,
            P("wide", None, "narrow"), P("wide", "narrow"), P("wide", "narrow", None), P("wide", None),
        ),
        check_vma=False,
    )
```
